32 devices in a mesh: brick: 8 (over z, x), sub: 4 (over y, core).
Axes of the slice: x: 2, y: 2, z: 4, core: 2. Of those that a mesh axis runs over, the one named last changes fastest.
Arguments:
- psi: bfloat16 [128, 48, 2304], P(('brick', 'sub')), may hold values from -6 to 6
- potential: bfloat16 [128, 48, 2304], P(('brick', 'sub')), may hold values from -5 to 5
- offsets: int32 [128], P(('brick', 'sub')), may hold values from 0 to 255, as said below
- kernel: bfloat16 [128, 100], P(('brick', 'sub')), may hold values from -0.8984375 to 0.8984375
- multipliers: bfloat16 [128, 100], P(('brick', 'sub')), may hold values from -0.8984375 to 0.8984375
- pattern: int32 [128, 25], P(('brick', 'sub')), may hold values 0 or 1
Outputs:
- gradient: bfloat16 [128, 48, 2304], P(('brick', 'sub'))
- margin_band: float32 [128, 100], P(('brick', 'sub'))
- hamiltonian_band: float32 [128, 100], P(('brick', 'sub'))
The draws below stay inside these ranges and needn't reach their ends.
Inputs may be any that keep to these rules, and one draw needn't show every extreme that they name: offsets[a] = (8 * (a // 4) + 8 / 2 - 48 / 2 + u) mod 256 with an integer u from -24 to 24; both ends are taken by some function.
All inputs are finite; a program needn't handle non-finite values. No bound on the sum of `pattern` on one device may be relied on, other than what follows from the above.
Results may differ from the reference program's by a relative error of at most 0.0059.
Values may be sent and summed in bfloat16 or wider, within the bound.
No kernel may reach another device: no remote copies, remote signals or barrier semaphores. Data moves between devices by JAX's collectives and lax.ppermute only.
A program may use at most 128 MiB of HBM per device.

```python
import math
import jax
import jax.numpy as jnp
from jax import lax

L = 48
Q = 8
FN_DEV = 4
JIT = 24
K = 6
F = 128
NX = 256
BAND = 100
DEVICES = 32


def draw_offsets(key, part):
    shift_key = jax.random.fold_in(key, 11)
    displace = jax.random.randint(shift_key, (F,), -JIT, JIT + 1)
    displace = displace.at[0].set(-JIT).at[1].set(JIT)
    owner_rank = jnp.arange(F, dtype=jnp.int32) // FN_DEV
    return jnp.mod(owner_rank * Q + Q // 2 - L // 2 + displace, NX).astype(jnp.int32)


def plant(drawn, own_key, least, largest):
    shape = drawn.shape
    place = [jax.random.randint(jax.random.fold_in(own_key, axis), (), 0, shape[axis]) for axis in range(len(shape))]
    drawn = drawn.at[tuple(place)].set(least)
    longest = shape.index(max(shape))
    place[longest] = (place[longest] + 1) % shape[longest]
    return drawn.at[tuple(place)].set(largest)


def block_levels(rng, shape, cuts, least, top_value):
    def one(axis_at, parts):
        heights = jax.random.uniform(jax.random.fold_in(jax.random.fold_in(rng, 6), axis_at), (parts,), jnp.float32, least / len(cuts), top_value / len(cuts))
        return jnp.repeat(jnp.exp(heights), shape[axis_at] // parts).reshape((-1,) + (1,) * (len(shape) - axis_at - 1))

    level = one(*cuts[0])
    for cut in cuts[1:]:
        level = level * one(*cut)
    return level


def scatter_about(own_key, extent, width, limit, shards=(), kind=jnp.bfloat16):
    drawn = jax.random.normal(own_key, extent, jnp.float32) * width
    if len(shards) > 0:
        drawn = block_levels(own_key, extent, shards, -0.22, 0.18) * drawn
    return jnp.clip(drawn, min=-limit, max=limit).astype(kind)


def setup_inputs(seed: int = 0) -> dict:
    arg_keys = jax.random.split(jax.random.key(seed), 7)
    return {
        "psi": scatter_about(arg_keys[0], (F, L, L * L), 1.0, 6.0, ((0, 32),)),
        "potential": scatter_about(arg_keys[1], (F, L, L * L), 1.0, 5.0, ((0, 32),)),
        "offsets": draw_offsets(jax.random.fold_in(arg_keys[6], 71), 0),
        "kernel": scatter_about(arg_keys[3], (F, BAND), 0.15, 0.8984375, ((0, 32),)),
        "multipliers": scatter_about(arg_keys[4], (F, BAND), 0.15, 0.8984375, ((0, 32),)),
        "pattern": plant((jax.random.randint(arg_keys[5], (F, 4 * K + 1), 0, 4) < 3).astype(jnp.int32), jax.random.fold_in(arg_keys[5], 1), 0, 1),
    }


filter_reach = 14


def kinetic_matrix(edge_len):
    positions = jnp.arange(edge_len, dtype=jnp.int32)
    offset_gap = positions[:, None] - positions[None, :]
    distance = jnp.abs(offset_gap).astype(jnp.float32)
    parity_sign = 1.0 - 2.0 * (jnp.abs(offset_gap) % 2).astype(jnp.float32)
    off_diag = parity_sign / jnp.maximum(distance, 1.0) ** 2
    entries = jnp.where(offset_gap == 0, math.pi ** 2 / 6.0, off_diag)
    entries = jnp.where(jnp.abs(offset_gap) <= filter_reach, entries, 0.0)
    return entries.astype(jnp.bfloat16)


def reference(psi, potential, offsets, kernel, multipliers, pattern):
    kinetic = kinetic_matrix(L).astype(jnp.float32)

    def h_block(inputs):
        functions, local_pot = inputs
        coeffs = functions.astype(jnp.float32).reshape(FN_DEV, L, L, L)
        summed = jnp.einsum("wx,fxyz->fwyz", kinetic, coeffs)
        summed = summed + jnp.einsum("wy,fxyz->fxwz", kinetic, coeffs)
        summed = summed + jnp.einsum("wz,fxyz->fxyw", kinetic, coeffs)
        result = summed.reshape(FN_DEV, L, L * L) + local_pot.astype(jnp.float32) * functions.astype(jnp.float32)
        return result.astype(jnp.bfloat16)

    hpsi = lax.map(h_block, (psi.reshape(DEVICES, FN_DEV, L, L * L), potential.reshape(DEVICES, FN_DEV, L, L * L)))
    hpsi = hpsi.reshape(F, L, L * L)
    spread = jnp.repeat(pattern, FN_DEV, axis=1).astype(jnp.bfloat16)
    kernel_eff = (kernel * spread).astype(jnp.float32)
    multi_eff = (multipliers * spread).astype(jnp.float32)
    band_reach = 2 * K
    columns = jnp.arange(BAND, dtype=jnp.int32)
    shift_owner = columns // FN_DEV - band_reach
    member_idx = columns % FN_DEV
    piece_count = L // Q + 1
    volume_scale = 1.0 / float(L ** 3)

    def align(function, shift_by):
        padded = jnp.pad(function, ((L, L), (0, 0)))
        return lax.dynamic_slice_in_dim(padded, (L - shift_by).astype(jnp.int32), L, 0)

    def one(func_index):
        owner_rank = func_index // FN_DEV
        partners = (jnp.mod(owner_rank + shift_owner, DEVICES) * FN_DEV + member_idx).astype(jnp.int32)
        start_at = offsets[func_index]
        plane_gap = jnp.mod(offsets[partners] - start_at + NX // 2, NX) - NX // 2
        plane_gap = jnp.clip(plane_gap, -L, L).astype(jnp.int32)
        aligned = jax.vmap(align)(psi[partners], plane_gap).astype(jnp.float32)
        aligned_h = jax.vmap(align)(hpsi[partners], plane_gap).astype(jnp.float32)
        own_coeffs = psi[func_index].astype(jnp.float32)
        local_plane = jnp.arange(L, dtype=jnp.int32)
        device_of = jnp.mod(start_at + local_plane, NX) // Q
        device_rel = jnp.mod(device_of - device_of[0], DEVICES)
        onehot = (device_rel[:, None] == jnp.arange(piece_count, dtype=jnp.int32)[None, :]).astype(jnp.float32)
        plane_sums = jnp.einsum("pq,bpq->bp", own_coeffs, aligned)
        energy_sums = jnp.einsum("pq,bpq->bp", own_coeffs, aligned_h)
        margin_part = (jnp.dot(plane_sums, onehot) * volume_scale).astype(jnp.bfloat16)
        energy_part = (jnp.dot(energy_sums, onehot) * volume_scale).astype(jnp.bfloat16)
        margin_row = jnp.sum(margin_part.astype(jnp.float32), axis=1)
        energy_row = jnp.sum(energy_part.astype(jnp.float32), axis=1)
        grad = jnp.einsum("b,bpq->pq", kernel_eff[func_index], aligned_h)
        grad = grad - jnp.einsum("b,bpq->pq", multi_eff[func_index], aligned)
        return grad.astype(jnp.bfloat16), margin_row, energy_row

    gradient, margin_band, hamiltonian_band = lax.map(one, jnp.arange(F, dtype=jnp.int32))
    return gradient, margin_band, hamiltonian_band
```

```python
import functools
import math

import jax
import jax.numpy as jnp
import numpy as np
from jax import lax
from jax.experimental import pallas as pl
from jax.experimental.pallas import tpu as pltpu
from jax.sharding import PartitionSpec as P

Q = 8
K = 6


filter_reach = 14


def shifted(block, axis, distance):
    devices = range(lax.axis_size(axis))
    route = [((i - distance) % len(devices), i) for i in devices]
    return lax.ppermute(block, axis, route)


def kinetic_matrix(edge_len):
    positions = jnp.arange(edge_len, dtype=jnp.int32)
    offset_gap = positions[:, None] - positions[None, :]
    distance = jnp.abs(offset_gap).astype(jnp.float32)
    parity_sign = 1.0 - 2.0 * (jnp.abs(offset_gap) % 2).astype(jnp.float32)
    off_diag = parity_sign / jnp.maximum(distance, 1.0) ** 2
    entries = jnp.where(offset_gap == 0, math.pi**2 / 6.0, off_diag)
    entries = jnp.where(jnp.abs(offset_gap) <= filter_reach, entries, 0.0)
    return entries.astype(jnp.bfloat16)


def cross_matrix(kinetic, edge_len):
    kin_float = kinetic.astype(jnp.float32)
    identity = jnp.eye(edge_len, dtype=jnp.float32)
    return (jnp.kron(kin_float, identity) + jnp.kron(identity, kin_float)).astype(jnp.bfloat16)


def apply_hamiltonian(psi, potential):
    fn_count, edge_len, plane_len = psi.shape
    kinetic = kinetic_matrix(edge_len)
    first_pass = jnp.einsum("wx,fxq->fwq", kinetic, psi, preferred_element_type=jnp.float32)
    cross = cross_matrix(kinetic, edge_len)
    second_pass = jnp.dot(
        psi.reshape(fn_count * edge_len, plane_len), cross, preferred_element_type=jnp.float32
    )
    summed = first_pass + second_pass.reshape(fn_count, edge_len, plane_len)
    result = summed + potential.astype(jnp.float32) * psi.astype(jnp.float32)
    return result.astype(jnp.bfloat16)


def embed(functions, region_start, window_len):

    def place(function, start_at):
        zeros_block = jnp.zeros((window_len, function.shape[1]), function.dtype)
        return lax.dynamic_update_slice_in_dim(zeros_block, function, start_at, 0)

    return jax.vmap(place)(functions, region_start)


def extract(window, region_start, edge_len):

    def take(planes, start_at):
        return lax.dynamic_slice_in_dim(planes, start_at, edge_len, 0)

    return jax.vmap(take)(window, region_start)


def dense_kernel(band_rows, group_count, band_reach, fn_count):
    dense_rows = []
    for slot_group in range(group_count):
        padded = jnp.pad(
            band_rows[slot_group], ((0, 0), (group_count * fn_count, group_count * fn_count))
        )
        first_col = (group_count + band_reach - slot_group) * fn_count
        dense_rows.append(padded[:, first_col : first_col + group_count * fn_count])
    return jnp.concatenate(dense_rows, axis=0)


def band_from_dense(dense, group_count, band_reach, fn_count):
    padded = jnp.pad(dense, ((0, 0), (band_reach * fn_count, band_reach * fn_count)))
    band_width = (2 * band_reach + 1) * fn_count
    pieces = []
    for slot_group in range(group_count):
        first_col = slot_group * fn_count
        pieces.append(padded[first_col : first_col + fn_count, first_col : first_col + band_width])
    return jnp.stack(pieces)


def grid_work(phi, hphi, kernel_rows, multi_rows, group_count, band_reach, fn_count, edge_len):
    volume_scale = 1.0 / float(edge_len**3)
    contract = (((1,), (1,)), ((), ()))
    margin = lax.dot_general(phi, phi, contract, preferred_element_type=jnp.float32) * volume_scale
    energy = lax.dot_general(phi, hphi, contract, preferred_element_type=jnp.float32) * volume_scale
    mixed = jnp.concatenate(
        [
            dense_kernel(kernel_rows, group_count, band_reach, fn_count),
            -dense_kernel(multi_rows, group_count, band_reach, fn_count),
        ],
        axis=1,
    )
    stacked = jnp.concatenate([hphi, phi], axis=0)
    grad = jnp.dot(mixed, stacked, preferred_element_type=jnp.float32).astype(jnp.bfloat16)
    margin_rows = band_from_dense(margin, group_count, band_reach, fn_count).astype(jnp.bfloat16)
    energy_rows = band_from_dense(energy, group_count, band_reach, fn_count).astype(jnp.bfloat16)
    return (grad, margin_rows, energy_rows)


def shards(psi, potential, offsets, kernel, multipliers, pattern):
    fn_count, edge_len, plane_len = psi.shape
    sub_count = lax.axis_size("sub")
    brick_count = lax.axis_size("brick")
    total_planes = Q * sub_count * brick_count
    band_reach = 2 * K
    band_width = kernel.shape[1]
    hpsi = apply_hamiltonian(psi, potential)
    spread = jnp.repeat(pattern, fn_count, axis=1).astype(jnp.bfloat16)
    kernel_eff = kernel * spread
    multi_eff = multipliers * spread
    margin_sum = jnp.zeros((fn_count, band_width), jnp.float32)
    energy_sum = jnp.zeros((fn_count, band_width), jnp.float32)
    my_rank = lax.axis_index("brick") * sub_count + lax.axis_index("sub")
    group_count = 2 * K + 1
    window_len = group_count * Q
    region_start = jnp.mod(offsets - (my_rank - K) * Q, total_planes)
    window_psi = embed(psi, region_start, window_len)
    window_hpsi = embed(hpsi, region_start, window_len)
    arrived = [None] * group_count
    for offset in range(-K, K + 1):
        first_plane = (offset + K) * Q
        payload = (
            window_psi[:, first_plane : first_plane + Q],
            window_hpsi[:, first_plane : first_plane + Q],
            kernel_eff,
            multi_eff,
        )
        if offset != 0:
            payload = shifted(
                (payload[0], payload[1], payload[2], payload[3]), ("brick", "sub"), offset
            )
        arrived[K - offset] = payload
    phi = jnp.concatenate([arrival[0] for arrival in arrived], axis=0).reshape(
        group_count * fn_count, Q * plane_len
    )
    hphi = jnp.concatenate([arrival[1] for arrival in arrived], axis=0).reshape(
        group_count * fn_count, Q * plane_len
    )
    kernel_rows = jnp.stack([arrival[2] for arrival in arrived])
    multi_rows = jnp.stack([arrival[3] for arrival in arrived])
    grad, margin_rows, energy_rows = grid_work(
        phi, hphi, kernel_rows, multi_rows, group_count, band_reach, fn_count, edge_len
    )
    grad = grad.reshape(group_count, fn_count, Q, plane_len)
    window = [None] * group_count
    for offset in range(-K, K + 1):
        slot_group = K - offset
        payload = (grad[slot_group], margin_rows[slot_group], energy_rows[slot_group])
        if offset != 0:
            payload = shifted((payload[0], payload[1], payload[2]), ("brick", "sub"), -offset)
        window[offset + K] = payload[0]
        margin_sum = margin_sum + payload[1].astype(jnp.float32)
        energy_sum = energy_sum + payload[2].astype(jnp.float32)
    gradient = extract(jnp.concatenate(window, axis=1), region_start, edge_len)
    return (gradient, margin_sum, energy_sum)


SUBLANES = 8
LANES = 128


def iota(shape, dim):
    return lax.broadcasted_iota(jnp.int32, shape, dim)


def plan_of(devices, fn_count, edge_len, plane_len, band_width):
    tiles = plane_len // LANES
    for shares in range(1, tiles + 1):
        if devices % shares or tiles % shares:
            continue
        classes = devices // shares
        per_class = edge_len // classes
        fits = (
            plane_len % LANES == 0
            and edge_len % classes == 0
            and (devices * Q) % classes == 0
            and classes & (classes - 1) == 0
            and fn_count * 2 == SUBLANES
            and per_class == 3
            and edge_len % SUBLANES == 0
            and band_width + 2 <= LANES
            and devices * SUBLANES == 2 * LANES
            and band_width == (4 * K + 1) * fn_count
        )
        if fits:
            return classes, shares
    return None


def kinetic_numpy(edge_len):
    positions = np.arange(edge_len)
    gap = np.abs(positions[:, None] - positions[None, :])
    sign = 1.0 - 2.0 * (gap % 2)
    entries = sign / np.maximum(gap, 1).astype(np.float32) ** 2
    entries = np.where(gap == 0, np.float32(math.pi**2 / 6.0), entries)
    entries = np.where(gap <= filter_reach, entries, 0.0)
    return entries.astype(np.float32)


def cross_stack(edge_len, rows, reach):
    kin = kinetic_numpy(edge_len).astype(jnp.bfloat16).astype(np.float32)
    line = kin[0]
    blocks = []
    for step in range(-reach, reach + 1):
        gap = np.abs(np.arange(rows)[:, None] + step * rows - np.arange(rows)[None, :])
        along_y = np.where(gap <= filter_reach, line[np.minimum(gap, edge_len - 1)], 0.0)
        block = np.kron(along_y, np.eye(edge_len, dtype=np.float32))
        if step == 0:
            block = block + np.kron(np.eye(rows, dtype=np.float32), kin)
        blocks.append(block)
    return np.concatenate(blocks, axis=0).astype(jnp.bfloat16)


def dot(a, b):
    return lax.dot_general(a, b, (((1,), (0,)), ((), ())), preferred_element_type=jnp.float32)


def dot_nt(a, b):
    return lax.dot_general(a, b, (((1,), (1,)), ((), ())), preferred_element_type=jnp.float32)


def pick(index, values):
    out = jnp.full(index.shape, values[0], jnp.int32)
    for k in range(1, len(values)):
        out = jnp.where(index == k, values[k], out)
    return out


def send_kernel(
    dims, offs_ref, psi_ref, pot_ref, kin_ref, cross_ref, kern_ref, mult_ref, patt_ref, out_ref
):
    fn_count, edge, plane_len, classes, shares, chunk, reach = dims
    rows = fn_count * edge
    tiles = plane_len // LANES // shares
    width = kern_ref.shape[1]
    psi = psi_ref[...].reshape(rows, plane_len)
    pot = pot_ref[...].reshape(rows, plane_len)
    chunks = plane_len // chunk
    offs = [offs_ref[k] for k in range(fn_count)]

    group = out_ref.shape[2] // tiles * SUBLANES
    shape = (classes, group, LANES)
    cls, item = iota(shape, 0), iota(shape, 1)
    kind = (item >= group // 2).astype(jnp.int32)
    item = item - kind * (group // 2)
    depth, member = item // fn_count, item % fn_count
    source = kind * rows + member * edge + depth * classes
    source = source + jnp.bitwise_and(cls - pick(member, offs), classes - 1)
    lane = iota(shape, 2)
    select = jnp.concatenate(
        [
            jnp.where(source == lane + k * LANES, 1.0, 0.0).astype(jnp.bfloat16)
            for k in range(2 * rows // LANES)
        ],
        axis=2,
    ).reshape(classes * group, 2 * rows)

    for j in range(chunks):
        lo, hi = max(0, j - reach), min(chunks, j + reach + 1)
        here = slice(j * chunk, (j + 1) * chunk)
        acc = dot(
            psi[:, lo * chunk : hi * chunk],
            cross_ref[(lo - j + reach) * chunk : (hi - j + reach) * chunk, :],
        )
        mine = psi[:, here]
        acc = acc + dot(kin_ref[...], mine)
        acc = acc + pot[:, here].astype(jnp.float32) * mine.astype(jnp.float32)
        both = jnp.concatenate([mine, acc.astype(jnp.bfloat16)], axis=0)
        ordered = dot(select, both)
        for t in range(chunk // LANES):
            tile = j * (chunk // LANES) + t
            share, local = tile // tiles, tile % tiles
            piece = ordered[:, t * LANES : (t + 1) * LANES].astype(jnp.bfloat16)
            piece = piece.reshape(classes, group // SUBLANES, SUBLANES, LANES)
            for part in range(group // SUBLANES):
                out_ref[:, share, part * tiles + local] = piece[:, part]

    blocks = patt_ref.shape[1]
    spread = jnp.where(
        iota((blocks, width), 1) // fn_count == iota((blocks, width), 0), 1.0, 0.0
    ).astype(jnp.bfloat16)
    flags = dot(patt_ref[...].astype(jnp.float32).astype(jnp.bfloat16), spread)
    small = jnp.concatenate(
        [
            kern_ref[...].astype(jnp.float32) * flags,
            mult_ref[...].astype(jnp.float32) * flags,
        ],
        axis=0,
    )
    small = jnp.concatenate(
        [small, jnp.zeros((SUBLANES, LANES - width), jnp.float32)], axis=1
    )
    at, lane = iota((SUBLANES, LANES), 0), iota((SUBLANES, LANES), 1)
    off = pick(at % fn_count, offs)
    small = jnp.where(lane == width, (off // 256).astype(jnp.float32), small)
    small = jnp.where(lane == width + 1, (off % 256).astype(jnp.float32), small)
    small = small.astype(jnp.bfloat16)
    for share in range(shares):
        out_ref[:, share, group // SUBLANES * tiles] = jnp.broadcast_to(
            small[None], (classes, SUBLANES, LANES)
        )


def grid_kernel(dims, in_ref, out_ref):
    fn_count, edge, classes, shares, width, band_reach, sub_count = dims
    devices, units = in_ref.shape[0], in_ref.shape[1]
    tiles = (units - 1) // 3
    full = devices * SUBLANES
    my_class = (lax.axis_index("brick") * sub_count + lax.axis_index("sub")) // shares
    classes_bits = classes.bit_length() - 1

    small = in_ref[:, units - 1]
    flat = small.reshape(full, LANES)
    where_hi, where_lo = width, width + 1
    lane_a, lane_b = iota((LANES, full), 0), iota((full, LANES), 1)
    weigh_a = jnp.where(lane_a == where_hi, 256.0, jnp.where(lane_a == where_lo, 1.0, 0.0))
    weigh_b = jnp.where(lane_b == where_hi, 256.0, jnp.where(lane_b == where_lo, 1.0, 0.0))
    off_row = dot(flat, weigh_a.astype(jnp.bfloat16)).astype(jnp.int32)
    off_col = dot_nt(weigh_b.astype(jnp.bfloat16), flat).astype(jnp.int32)

    planes = devices * Q // classes

    def first_plane(off):
        inner = jnp.bitwise_and(my_class - off, classes - 1)
        return jnp.right_shift(off + inner - my_class, classes_bits)

    gap = first_plane(off_row) - first_plane(off_col)
    half_row = jnp.bitwise_and(iota((full, full), 0) // fn_count, 1)
    half_col = jnp.bitwise_and(iota((full, full), 1) // fn_count, 1)

    def mask(row_depth, col_depth):
        return jnp.bitwise_and(gap + row_depth - col_depth, planes - 1) == 0

    col_depth = (half_col, jnp.where(half_col == 0, 2, 0), half_col + 1)
    low = [mask(half_row, d) for d in col_depth]
    top = [mask(2, d) for d in col_depth]

    halves = small.astype(jnp.float32)
    turned = pltpu.roll(halves, fn_count, axis=1)
    upper = iota(halves.shape, 1) < fn_count
    expand = jnp.where(
        (iota((LANES, full), 0) == iota((LANES, full), 1) // SUBLANES * fn_count + iota((LANES, full), 1) % fn_count)
        & (iota((LANES, full), 0) < width),
        1.0,
        0.0,
    ).astype(jnp.bfloat16)

    def dense(rows):
        wide = dot(rows.reshape(full, LANES).astype(jnp.bfloat16), expand)
        turned_rows = []
        for owner in range(devices):
            shift = (owner - band_reach) * SUBLANES % full
            block = wide[owner * SUBLANES : (owner + 1) * SUBLANES]
            turned_rows.append(pltpu.roll(block, shift, axis=1) if shift else block)
        return jnp.concatenate(turned_rows, axis=0)

    plus = dense(jnp.where(upper, halves, turned))
    minus = -dense(jnp.where(upper, turned, halves))
    coef = (minus, jnp.where(half_col == 0, minus, plus), plus)
    mixed = jnp.concatenate(
        [
            jnp.concatenate([jnp.where(k, c, 0.0).astype(jnp.bfloat16) for k, c in zip(ks, coef)], axis=1)
            for ks in (low, top)
        ],
        axis=0,
    )

    stacked = [
        jnp.concatenate([in_ref[:, part * tiles + t].reshape(full, LANES) for t in range(tiles)], axis=1)
        for part in range(3)
    ]
    grad = dot(mixed, jnp.concatenate(stacked, axis=0))
    upper = iota((devices, SUBLANES, LANES), 1) < fn_count
    for t in range(tiles):
        out_ref[:, t] = (
            grad[:full, t * LANES : (t + 1) * LANES].reshape(devices, SUBLANES, LANES).astype(jnp.bfloat16)
        )
    second = grad[full:].reshape(devices, SUBLANES, tiles * LANES)
    for v in range((tiles + 1) // 2):
        even = second[:, :, 2 * v * LANES : (2 * v + 1) * LANES]
        if 2 * v + 1 < tiles:
            even = jnp.where(upper, even, second[:, :, (2 * v + 1) * LANES : (2 * v + 2) * LANES])
        out_ref[:, tiles + v] = even.astype(jnp.bfloat16)

    sums = []
    for part in range(3):
        low_gram = jnp.where(low[part], dot_nt(stacked[0], stacked[part]), 0.0)
        top_gram = dot_nt(stacked[1], stacked[part])
        top_gram = jnp.where(top[part] & (half_row == 0), top_gram, 0.0)
        total = (low_gram + top_gram).reshape(devices, SUBLANES, full)
        sums.append(total + pltpu.roll(total, fn_count, axis=1))
    first = sums[0] + pltpu.roll(sums[0], full - fn_count, axis=2)
    third = sums[2] + pltpu.roll(sums[2], fn_count, axis=2)
    lanes_half = jnp.bitwise_and(iota((devices, SUBLANES, full), 2) // fn_count, 1)
    bands = sums[1] + jnp.where(lanes_half == 0, first, third)
    bands = jnp.where(upper, bands[:, :, :LANES], bands[:, :, LANES:])
    bands = bands * (1.0 / float(edge**3))
    out_ref[:, tiles + (tiles + 1) // 2] = bands.astype(jnp.bfloat16)


def receive_kernel(dims, offs_ref, in_ref, grad_ref, margin_ref, energy_ref):
    fn_count, edge, plane_len, classes, shares, band_reach, sub_count = dims
    tiles = plane_len // LANES // shares
    rows = fn_count * edge
    devices = classes * shares
    width = margin_ref.shape[1]
    rank = lax.axis_index("brick") * sub_count + lax.axis_index("sub")
    offs = [offs_ref[k] for k in range(fn_count)]
    inner = classes * SUBLANES

    shape = (fn_count, edge, inner)
    member, plane = iota(shape, 0), iota(shape, 1)
    slot = iota(shape, 2)
    cls, sub = slot // SUBLANES, slot % SUBLANES
    half, owner_fn = sub // fn_count, sub % fn_count
    at = jnp.bitwise_and(cls - pick(owner_fn, offs), classes - 1)
    same = owner_fn == member
    low = jnp.where(same & (plane == at + half * classes), 1.0, 0.0)
    top = same & (plane == at + 2 * classes)
    for parity in range(2):
        tops = jnp.where(top & (half == parity), 1.0, 0.0)
        place = jnp.concatenate([low.astype(jnp.bfloat16), tops.astype(jnp.bfloat16)], axis=2)
        place = place.reshape(rows, 2 * inner)
        columns, spots = [], []
        for share in range(shares):
            for t in range(parity, tiles, 2):
                columns.append(
                    jnp.concatenate(
                        [
                            in_ref[:, share, t].reshape(inner, LANES),
                            in_ref[:, share, tiles + t // 2].reshape(inner, LANES),
                        ],
                        axis=0,
                    )
                )
                spots.append((share * tiles + t) * LANES)
        placed = dot(place, jnp.concatenate(columns, axis=1)).astype(jnp.bfloat16)
        for n, spot in enumerate(spots):
            grad_ref[:, :, spot : spot + LANES] = placed[:, n * LANES : (n + 1) * LANES].reshape(
                fn_count, edge, LANES
            )

    total = jnp.sum(
        in_ref[:, :, tiles + (tiles + 1) // 2].reshape(devices, SUBLANES, LANES).astype(jnp.float32), axis=0
    )
    lane, col = iota((LANES, LANES), 0), iota((LANES, LANES), 1)
    partner = lax.rem(rank + col // fn_count - band_reach + devices, devices)
    for kind, ref in ((0, margin_ref), (1, energy_ref)):
        wanted = partner * SUBLANES + kind * fn_count + col % fn_count
        picked = [
            lax.dot_general(
                total,
                jnp.where(wanted == lane + part * LANES, 1.0, 0.0),
                (((1,), (0,)), ((), ())),
                preferred_element_type=jnp.float32,
                precision=lax.Precision.HIGHEST,
            )
            for part in range(2)
        ]
        ref[...] = (picked[0][:fn_count] + picked[1][fn_count:])[:, :width]


def transposed_shards(classes, shares, psi, potential, offsets, kernel, multipliers, pattern):
    fn_count, edge, plane_len = psi.shape
    sub_count = lax.axis_size("sub")
    devices = sub_count * lax.axis_size("brick")
    width = kernel.shape[1]
    tiles = plane_len // LANES // shares
    band_reach = 2 * K
    chunk = edge * SUBLANES
    reach = -(-filter_reach // SUBLANES)
    params = pltpu.CompilerParams(vmem_limit_bytes=56 * 2**20)
    smem = pl.BlockSpec(memory_space=pltpu.SMEM)
    vmem = pl.BlockSpec(memory_space=pltpu.VMEM)

    kinetic = np.kron(np.eye(fn_count, dtype=np.float32), kinetic_numpy(edge)).astype(jnp.bfloat16)
    cross = cross_stack(edge, SUBLANES, reach)
    units = 3 * tiles + 1
    sent = pl.pallas_call(
        functools.partial(send_kernel, (fn_count, edge, plane_len, classes, shares, chunk, reach)),
        out_shape=jax.ShapeDtypeStruct((classes, shares, units, SUBLANES, LANES), jnp.bfloat16),
        in_specs=[smem] + [vmem] * 7,
        out_specs=vmem,
        compiler_params=params,
        name="send",
    )(offsets, psi, potential, jnp.asarray(kinetic), jnp.asarray(cross), kernel, multipliers, pattern)
    sent = sent.reshape(devices, units, SUBLANES, LANES)
    axes = ("brick", "sub")
    held = lax.all_to_all(sent, axes, 0, 0, tiled=True)

    back_units = tiles + (tiles + 1) // 2 + 1
    made = pl.pallas_call(
        functools.partial(grid_kernel, (fn_count, edge, classes, shares, width, band_reach, sub_count)),
        out_shape=jax.ShapeDtypeStruct((devices, back_units, SUBLANES, LANES), jnp.bfloat16),
        in_specs=[vmem],
        out_specs=vmem,
        compiler_params=params,
        name="grid",
    )(held)
    back = lax.all_to_all(made, axes, 0, 0, tiled=True)
    back = back.reshape(classes, shares, back_units, SUBLANES, LANES)
    return pl.pallas_call(
        functools.partial(receive_kernel, (fn_count, edge, plane_len, classes, shares, band_reach, sub_count)),
        out_shape=(
            jax.ShapeDtypeStruct(psi.shape, jnp.bfloat16),
            jax.ShapeDtypeStruct((fn_count, width), jnp.float32),
            jax.ShapeDtypeStruct((fn_count, width), jnp.float32),
        ),
        in_specs=[smem, vmem],
        out_specs=(vmem, vmem, vmem),
        compiler_params=params,
        name="receive",
    )(offsets, back)


def any_shards(psi, potential, offsets, kernel, multipliers, pattern):
    devices = lax.axis_size("brick") * lax.axis_size("sub")
    plan = plan_of(devices, *psi.shape, kernel.shape[1])
    if plan is None:
        return shards(psi, potential, offsets, kernel, multipliers, pattern)
    return transposed_shards(*plan, psi, potential, offsets, kernel, multipliers, pattern)


def solution(mesh):
    in_specs = (
        P(("brick", "sub"), None, None),
        P(("brick", "sub"), None, None),
        P(("brick", "sub")),
        P(("brick", "sub"), None),
        P(("brick", "sub"), None),
        P(("brick", "sub"), None),
    )
    out_specs = (
        P(("brick", "sub"), None, None),
        P(("brick", "sub"), None),
        P(("brick", "sub"), None),
    )
    return jax.shard_map(any_shards, mesh=mesh, in_specs=in_specs, out_specs=out_specs, check_vma=False)
```

```python
import functools
import math

import jax
import jax.numpy as jnp
import numpy as np
from jax import lax
from jax.experimental import pallas as pl
from jax.experimental.pallas import tpu as pltpu
from jax.sharding import PartitionSpec as P

Q = 8
K = 6


filter_reach = 14


def shifted(block, axis, distance):
    devices = range(lax.axis_size(axis))
    route = [((i - distance) % len(devices), i) for i in devices]
    return lax.ppermute(block, axis, route)


def kinetic_matrix(edge_len):
    positions = jnp.arange(edge_len, dtype=jnp.int32)
    offset_gap = positions[:, None] - positions[None, :]
    distance = jnp.abs(offset_gap).astype(jnp.float32)
    parity_sign = 1.0 - 2.0 * (jnp.abs(offset_gap) % 2).astype(jnp.float32)
    off_diag = parity_sign / jnp.maximum(distance, 1.0) ** 2
    entries = jnp.where(offset_gap == 0, math.pi**2 / 6.0, off_diag)
    entries = jnp.where(jnp.abs(offset_gap) <= filter_reach, entries, 0.0)
    return entries.astype(jnp.bfloat16)


def cross_matrix(kinetic, edge_len):
    kin_float = kinetic.astype(jnp.float32)
    identity = jnp.eye(edge_len, dtype=jnp.float32)
    return (jnp.kron(kin_float, identity) + jnp.kron(identity, kin_float)).astype(jnp.bfloat16)


def apply_hamiltonian(psi, potential):
    fn_count, edge_len, plane_len = psi.shape
    kinetic = kinetic_matrix(edge_len)
    first_pass = jnp.einsum("wx,fxq->fwq", kinetic, psi, preferred_element_type=jnp.float32)
    cross = cross_matrix(kinetic, edge_len)
    second_pass = jnp.dot(
        psi.reshape(fn_count * edge_len, plane_len), cross, preferred_element_type=jnp.float32
    )
    summed = first_pass + second_pass.reshape(fn_count, edge_len, plane_len)
    result = summed + potential.astype(jnp.float32) * psi.astype(jnp.float32)
    return result.astype(jnp.bfloat16)


def embed(functions, region_start, window_len):

    def place(function, start_at):
        zeros_block = jnp.zeros((window_len, function.shape[1]), function.dtype)
        return lax.dynamic_update_slice_in_dim(zeros_block, function, start_at, 0)

    return jax.vmap(place)(functions, region_start)


def extract(window, region_start, edge_len):

    def take(planes, start_at):
        return lax.dynamic_slice_in_dim(planes, start_at, edge_len, 0)

    return jax.vmap(take)(window, region_start)


def dense_kernel(band_rows, group_count, band_reach, fn_count):
    dense_rows = []
    for slot_group in range(group_count):
        padded = jnp.pad(
            band_rows[slot_group], ((0, 0), (group_count * fn_count, group_count * fn_count))
        )
        first_col = (group_count + band_reach - slot_group) * fn_count
        dense_rows.append(padded[:, first_col : first_col + group_count * fn_count])
    return jnp.concatenate(dense_rows, axis=0)


def band_from_dense(dense, group_count, band_reach, fn_count):
    padded = jnp.pad(dense, ((0, 0), (band_reach * fn_count, band_reach * fn_count)))
    band_width = (2 * band_reach + 1) * fn_count
    pieces = []
    for slot_group in range(group_count):
        first_col = slot_group * fn_count
        pieces.append(padded[first_col : first_col + fn_count, first_col : first_col + band_width])
    return jnp.stack(pieces)


def grid_work(phi, hphi, kernel_rows, multi_rows, group_count, band_reach, fn_count, edge_len):
    volume_scale = 1.0 / float(edge_len**3)
    contract = (((1,), (1,)), ((), ()))
    margin = lax.dot_general(phi, phi, contract, preferred_element_type=jnp.float32) * volume_scale
    energy = lax.dot_general(phi, hphi, contract, preferred_element_type=jnp.float32) * volume_scale
    mixed = jnp.concatenate(
        [
            dense_kernel(kernel_rows, group_count, band_reach, fn_count),
            -dense_kernel(multi_rows, group_count, band_reach, fn_count),
        ],
        axis=1,
    )
    stacked = jnp.concatenate([hphi, phi], axis=0)
    grad = jnp.dot(mixed, stacked, preferred_element_type=jnp.float32).astype(jnp.bfloat16)
    margin_rows = band_from_dense(margin, group_count, band_reach, fn_count).astype(jnp.bfloat16)
    energy_rows = band_from_dense(energy, group_count, band_reach, fn_count).astype(jnp.bfloat16)
    return (grad, margin_rows, energy_rows)


def shards(psi, potential, offsets, kernel, multipliers, pattern):
    fn_count, edge_len, plane_len = psi.shape
    sub_count = lax.axis_size("sub")
    brick_count = lax.axis_size("brick")
    total_planes = Q * sub_count * brick_count
    band_reach = 2 * K
    band_width = kernel.shape[1]
    hpsi = apply_hamiltonian(psi, potential)
    spread = jnp.repeat(pattern, fn_count, axis=1).astype(jnp.bfloat16)
    kernel_eff = kernel * spread
    multi_eff = multipliers * spread
    margin_sum = jnp.zeros((fn_count, band_width), jnp.float32)
    energy_sum = jnp.zeros((fn_count, band_width), jnp.float32)
    my_rank = lax.axis_index("brick") * sub_count + lax.axis_index("sub")
    group_count = 2 * K + 1
    window_len = group_count * Q
    region_start = jnp.mod(offsets - (my_rank - K) * Q, total_planes)
    window_psi = embed(psi, region_start, window_len)
    window_hpsi = embed(hpsi, region_start, window_len)
    arrived = [None] * group_count
    for offset in range(-K, K + 1):
        first_plane = (offset + K) * Q
        payload = (
            window_psi[:, first_plane : first_plane + Q],
            window_hpsi[:, first_plane : first_plane + Q],
            kernel_eff,
            multi_eff,
        )
        if offset != 0:
            payload = shifted(
                (payload[0], payload[1], payload[2], payload[3]), ("brick", "sub"), offset
            )
        arrived[K - offset] = payload
    phi = jnp.concatenate([arrival[0] for arrival in arrived], axis=0).reshape(
        group_count * fn_count, Q * plane_len
    )
    hphi = jnp.concatenate([arrival[1] for arrival in arrived], axis=0).reshape(
        group_count * fn_count, Q * plane_len
    )
    kernel_rows = jnp.stack([arrival[2] for arrival in arrived])
    multi_rows = jnp.stack([arrival[3] for arrival in arrived])
    grad, margin_rows, energy_rows = grid_work(
        phi, hphi, kernel_rows, multi_rows, group_count, band_reach, fn_count, edge_len
    )
    grad = grad.reshape(group_count, fn_count, Q, plane_len)
    window = [None] * group_count
    for offset in range(-K, K + 1):
        slot_group = K - offset
        payload = (grad[slot_group], margin_rows[slot_group], energy_rows[slot_group])
        if offset != 0:
            payload = shifted((payload[0], payload[1], payload[2]), ("brick", "sub"), -offset)
        window[offset + K] = payload[0]
        margin_sum = margin_sum + payload[1].astype(jnp.float32)
        energy_sum = energy_sum + payload[2].astype(jnp.float32)
    gradient = extract(jnp.concatenate(window, axis=1), region_start, edge_len)
    return (gradient, margin_sum, energy_sum)


SUBLANES = 8
LANES = 128


def iota(shape, dim):
    return lax.broadcasted_iota(jnp.int32, shape, dim)


def plan_of(devices, fn_count, edge_len, plane_len, band_width):
    tiles = plane_len // LANES
    for shares in range(1, tiles + 1):
        if devices % shares or tiles % shares:
            continue
        classes = devices // shares
        per_class = edge_len // classes
        fits = (
            plane_len % LANES == 0
            and edge_len % classes == 0
            and (devices * Q) % classes == 0
            and classes & (classes - 1) == 0
            and fn_count * 2 == SUBLANES
            and per_class == 3
            and edge_len % SUBLANES == 0
            and band_width + 2 <= LANES
            and devices * SUBLANES == 2 * LANES
            and band_width == (4 * K + 1) * fn_count
        )
        if fits:
            return classes, shares
    return None


def kinetic_numpy(edge_len):
    positions = np.arange(edge_len)
    gap = np.abs(positions[:, None] - positions[None, :])
    sign = 1.0 - 2.0 * (gap % 2)
    entries = sign / np.maximum(gap, 1).astype(np.float32) ** 2
    entries = np.where(gap == 0, np.float32(math.pi**2 / 6.0), entries)
    entries = np.where(gap <= filter_reach, entries, 0.0)
    return entries.astype(np.float32)


def cross_stack(edge_len, rows, reach):
    kin = kinetic_numpy(edge_len).astype(jnp.bfloat16).astype(np.float32)
    line = kin[0]
    blocks = []
    for step in range(-reach, reach + 1):
        gap = np.abs(np.arange(rows)[:, None] + step * rows - np.arange(rows)[None, :])
        along_y = np.where(gap <= filter_reach, line[np.minimum(gap, edge_len - 1)], 0.0)
        block = np.kron(along_y, np.eye(edge_len, dtype=np.float32))
        if step == 0:
            block = block + np.kron(np.eye(rows, dtype=np.float32), kin)
        blocks.append(block)
    return np.concatenate(blocks, axis=0).astype(jnp.bfloat16)


def dot(a, b):
    return lax.dot_general(a, b, (((1,), (0,)), ((), ())), preferred_element_type=jnp.float32)


def dot_nt(a, b):
    return lax.dot_general(a, b, (((1,), (1,)), ((), ())), preferred_element_type=jnp.float32)


def in_hbm(array):
    return pltpu.with_memory_space_constraint(array, pltpu.HBM)


def pick(index, values):
    out = jnp.full(index.shape, values[0], jnp.int32)
    for k in range(1, len(values)):
        out = jnp.where(index == k, values[k], out)
    return out


def send_kernel(
    dims, offs_hbm, psi_hbm, pot_hbm, kin_hbm, cross_hbm, kern_hbm, mult_hbm, patt_hbm, out_ref,
    offs_ref, psi_ref, pot_ref, kin_ref, cross_ref, kern_ref, mult_ref, patt_ref, sems
):
    fn_count, edge, plane_len, classes, shares, chunk, reach = dims
    rows = fn_count * edge
    tiles = plane_len // LANES // shares
    parts = 3
    copies = [
        pltpu.make_async_copy(source, target, sems.at[n])
        for n, (source, target) in enumerate(
            (
                (offs_hbm, offs_ref),
                (psi_hbm, psi_ref),
                (kin_hbm, kin_ref),
                (cross_hbm, cross_ref),
                (pot_hbm, pot_ref),
                (kern_hbm, kern_ref),
                (mult_hbm, mult_ref),
                (patt_hbm, patt_ref),
            )
        )
    ]
    for copy in copies:
        copy.start()
    width = kern_ref.shape[1]
    chunks = plane_len // chunk
    copies[0].wait()
    offs = [offs_ref[k] for k in range(fn_count)]

    shape = (classes, 2 * SUBLANES, LANES)
    cls, item, lane = iota(shape, 0), iota(shape, 1), iota(shape, 2)
    inner = jnp.bitwise_and(cls - pick(item % fn_count, offs), classes - 1)
    base = item % fn_count * edge + inner

    def select(first):
        depth = item // fn_count - first
        source = jnp.where((depth >= 0) & (depth < parts), base + depth * classes, -1)
        wide = [
            jnp.where(source == lane + k * LANES, 1.0, 0.0).astype(jnp.bfloat16)
            for k in range(-(-rows // LANES))
        ]
        return jnp.concatenate(wide, axis=2).reshape(classes * 2 * SUBLANES, -1)[:, :rows]

    own, applied = select(0), select(1)
    for copy in copies[1:4]:
        copy.wait()
    psi = psi_ref[...].reshape(rows, plane_len)
    lead = jnp.concatenate([kin_ref[...], own], axis=0)
    copies[4].wait()
    pot = pot_ref[...].reshape(rows, plane_len)

    for j in range(chunks):
        lo, hi = max(0, j - reach), min(chunks, j + reach + 1)
        here = slice(j * chunk, (j + 1) * chunk)
        acc = dot(
            psi[:, lo * chunk : hi * chunk],
            cross_ref[(lo - j + reach) * chunk : (hi - j + reach) * chunk, :],
        )
        mine = psi[:, here]
        led = dot(lead, mine)
        acc = acc + led[:rows]
        acc = acc + pot[:, here].astype(jnp.float32) * mine.astype(jnp.float32)
        sorted_h = dot(applied, acc.astype(jnp.bfloat16))
        for t in range(chunk // LANES):
            tile = j * (chunk // LANES) + t
            share, local = tile // tiles, tile % tiles
            at = slice(t * LANES, (t + 1) * LANES)
            first = led[rows:, at].reshape(classes, 2, SUBLANES, LANES)
            second = sorted_h[:, at].reshape(classes, 2, SUBLANES, LANES)
            out_ref[:, share, local] = first[:, 0].astype(jnp.bfloat16)
            out_ref[:, share, tiles + local] = (first[:, 1] + second[:, 0]).astype(jnp.bfloat16)
            out_ref[:, share, 2 * tiles + local] = second[:, 1].astype(jnp.bfloat16)

    for copy in copies[5:]:
        copy.wait()
    blocks = patt_ref.shape[1]
    spread = jnp.where(
        iota((blocks, width), 1) // fn_count == iota((blocks, width), 0), 1.0, 0.0
    ).astype(jnp.bfloat16)
    flags = dot(patt_ref[...].astype(jnp.float32).astype(jnp.bfloat16), spread)
    small = jnp.concatenate(
        [
            kern_ref[...].astype(jnp.float32) * flags,
            mult_ref[...].astype(jnp.float32) * flags,
        ],
        axis=0,
    )
    small = jnp.concatenate(
        [small, jnp.zeros((SUBLANES, LANES - width), jnp.float32)], axis=1
    )
    at, lane = iota((SUBLANES, LANES), 0), iota((SUBLANES, LANES), 1)
    off = pick(at % fn_count, offs)
    small = jnp.where(lane == width, (off // 256).astype(jnp.float32), small)
    small = jnp.where(lane == width + 1, (off % 256).astype(jnp.float32), small)
    small = small.astype(jnp.bfloat16)
    for share in range(shares):
        out_ref[:, share, parts * tiles] = jnp.broadcast_to(small[None], (classes, SUBLANES, LANES))


def grid_kernel(dims, in_ref, out_ref):
    fn_count, edge, classes, shares, width, band_reach, sub_count = dims
    devices, units = in_ref.shape[0], in_ref.shape[1]
    tiles = (units - 1) // 3
    full = devices * SUBLANES
    my_class = (lax.axis_index("brick") * sub_count + lax.axis_index("sub")) // shares
    classes_bits = classes.bit_length() - 1

    small = in_ref[:, units - 1]
    flat = small.reshape(full, LANES)
    where_hi, where_lo = width, width + 1
    lane_a, lane_b = iota((LANES, full), 0), iota((full, LANES), 1)
    weigh_a = jnp.where(lane_a == where_hi, 256.0, jnp.where(lane_a == where_lo, 1.0, 0.0))
    weigh_b = jnp.where(lane_b == where_hi, 256.0, jnp.where(lane_b == where_lo, 1.0, 0.0))
    off_row = dot(flat, weigh_a.astype(jnp.bfloat16)).astype(jnp.int32)
    off_col = dot_nt(weigh_b.astype(jnp.bfloat16), flat).astype(jnp.int32)

    planes = devices * Q // classes

    def first_plane(off):
        inner = jnp.bitwise_and(my_class - off, classes - 1)
        return jnp.right_shift(off + inner - my_class, classes_bits)

    gap = first_plane(off_row) - first_plane(off_col)
    half_row = jnp.bitwise_and(iota((full, full), 0) // fn_count, 1)
    half_col = jnp.bitwise_and(iota((full, full), 1) // fn_count, 1)

    def mask(row_depth, col_depth):
        return jnp.bitwise_and(gap + row_depth - col_depth, planes - 1) == 0

    col_depth = (half_col, jnp.where(half_col == 0, 2, 0), half_col + 1)
    low = [mask(half_row, d) for d in col_depth]
    top = [mask(2, d) for d in col_depth]

    halves = small.astype(jnp.float32)
    turned = pltpu.roll(halves, fn_count, axis=1)
    upper = iota(halves.shape, 1) < fn_count
    expand = jnp.where(
        (iota((LANES, full), 0) == iota((LANES, full), 1) // SUBLANES * fn_count + iota((LANES, full), 1) % fn_count)
        & (iota((LANES, full), 0) < width),
        1.0,
        0.0,
    ).astype(jnp.bfloat16)

    def dense(rows):
        wide = dot(rows.reshape(full, LANES).astype(jnp.bfloat16), expand)
        turned_rows = []
        for owner in range(devices):
            shift = (owner - band_reach) * SUBLANES % full
            block = wide[owner * SUBLANES : (owner + 1) * SUBLANES]
            turned_rows.append(pltpu.roll(block, shift, axis=1) if shift else block)
        return jnp.concatenate(turned_rows, axis=0)

    plus = dense(jnp.where(upper, halves, turned))
    minus = -dense(jnp.where(upper, turned, halves))
    coef = (minus, jnp.where(half_col == 0, minus, plus), plus)
    mixed = jnp.concatenate(
        [
            jnp.concatenate([jnp.where(k, c, 0.0).astype(jnp.bfloat16) for k, c in zip(ks, coef)], axis=1)
            for ks in (low, top)
        ],
        axis=0,
    )

    stacked = [
        jnp.concatenate([in_ref[:, part * tiles + t].reshape(full, LANES) for t in range(tiles)], axis=1)
        for part in range(3)
    ]
    grad = dot(mixed, jnp.concatenate(stacked, axis=0))
    upper = iota((devices, SUBLANES, LANES), 1) < fn_count
    for t in range(tiles):
        out_ref[:, t] = (
            grad[:full, t * LANES : (t + 1) * LANES].reshape(devices, SUBLANES, LANES).astype(jnp.bfloat16)
        )
    second = grad[full:].reshape(devices, SUBLANES, tiles * LANES)
    for v in range((tiles + 1) // 2):
        even = second[:, :, 2 * v * LANES : (2 * v + 1) * LANES]
        if 2 * v + 1 < tiles:
            even = jnp.where(upper, even, second[:, :, (2 * v + 1) * LANES : (2 * v + 2) * LANES])
        out_ref[:, tiles + v] = even.astype(jnp.bfloat16)

    sums = []
    for part in range(3):
        low_gram = jnp.where(low[part], dot_nt(stacked[0], stacked[part]), 0.0)
        top_gram = dot_nt(stacked[1], stacked[part])
        top_gram = jnp.where(top[part] & (half_row == 0), top_gram, 0.0)
        total = (low_gram + top_gram).reshape(devices, SUBLANES, full)
        sums.append(total + pltpu.roll(total, fn_count, axis=1))
    first = sums[0] + pltpu.roll(sums[0], full - fn_count, axis=2)
    third = sums[2] + pltpu.roll(sums[2], fn_count, axis=2)
    lanes_half = jnp.bitwise_and(iota((devices, SUBLANES, full), 2) // fn_count, 1)
    bands = sums[1] + jnp.where(lanes_half == 0, first, third)
    bands = jnp.where(upper, bands[:, :, :LANES], bands[:, :, LANES:])
    bands = bands * (1.0 / float(edge**3))
    out_ref[:, tiles + (tiles + 1) // 2] = bands.astype(jnp.bfloat16)


def receive_kernel(dims, offs_hbm, in_ref, grad_ref, margin_ref, energy_ref, offs_ref, sem):
    fn_count, edge, plane_len, classes, shares, band_reach, sub_count = dims
    tiles = plane_len // LANES // shares
    rows = fn_count * edge
    devices = classes * shares
    width = margin_ref.shape[1]
    copy = pltpu.make_async_copy(offs_hbm, offs_ref, sem)
    copy.start()
    copy.wait()
    rank = lax.axis_index("brick") * sub_count + lax.axis_index("sub")
    offs = [offs_ref[k] for k in range(fn_count)]
    inner = classes * SUBLANES

    shape = (fn_count, edge, inner)
    member, plane = iota(shape, 0), iota(shape, 1)
    slot = iota(shape, 2)
    cls, sub = slot // SUBLANES, slot % SUBLANES
    half, owner_fn = sub // fn_count, sub % fn_count
    at = jnp.bitwise_and(cls - pick(owner_fn, offs), classes - 1)
    same = owner_fn == member
    low = jnp.where(same & (plane == at + half * classes), 1.0, 0.0)
    top = same & (plane == at + 2 * classes)
    for parity in range(2):
        tops = jnp.where(top & (half == parity), 1.0, 0.0)
        place = jnp.concatenate([low.astype(jnp.bfloat16), tops.astype(jnp.bfloat16)], axis=2)
        place = place.reshape(rows, 2 * inner)
        columns, spots = [], []
        for share in range(shares):
            for t in range(parity, tiles, 2):
                columns.append(
                    jnp.concatenate(
                        [
                            in_ref[:, share, t].reshape(inner, LANES),
                            in_ref[:, share, tiles + t // 2].reshape(inner, LANES),
                        ],
                        axis=0,
                    )
                )
                spots.append((share * tiles + t) * LANES)
        placed = dot(place, jnp.concatenate(columns, axis=1)).astype(jnp.bfloat16)
        for n, spot in enumerate(spots):
            grad_ref[:, :, spot : spot + LANES] = placed[:, n * LANES : (n + 1) * LANES].reshape(
                fn_count, edge, LANES
            )

    total = jnp.sum(
        in_ref[:, :, tiles + (tiles + 1) // 2].reshape(devices, SUBLANES, LANES).astype(jnp.float32), axis=0
    )
    lane, col = iota((LANES, LANES), 0), iota((LANES, LANES), 1)
    partner = lax.rem(rank + col // fn_count - band_reach + devices, devices)
    for kind, ref in ((0, margin_ref), (1, energy_ref)):
        wanted = partner * SUBLANES + kind * fn_count + col % fn_count
        picked = [
            lax.dot_general(
                total,
                jnp.where(wanted == lane + part * LANES, 1.0, 0.0),
                (((1,), (0,)), ((), ())),
                preferred_element_type=jnp.float32,
                precision=lax.Precision.HIGHEST,
            )
            for part in range(2)
        ]
        ref[...] = (picked[0][:fn_count] + picked[1][fn_count:])[:, :width]


def transposed_shards(classes, shares, psi, potential, offsets, kernel, multipliers, pattern):
    fn_count, edge, plane_len = psi.shape
    sub_count = lax.axis_size("sub")
    devices = sub_count * lax.axis_size("brick")
    width = kernel.shape[1]
    tiles = plane_len // LANES // shares
    band_reach = 2 * K
    chunk = edge * SUBLANES
    reach = -(-filter_reach // SUBLANES)
    params = pltpu.CompilerParams(vmem_limit_bytes=20 * 2**20)
    vmem = pl.BlockSpec(memory_space=pltpu.VMEM)

    kinetic = np.kron(np.eye(fn_count, dtype=np.float32), kinetic_numpy(edge)).astype(jnp.bfloat16)
    cross = cross_stack(edge, SUBLANES, reach)
    units = 3 * tiles + 1
    offsets = in_hbm(offsets)
    sent = pl.pallas_call(
        functools.partial(send_kernel, (fn_count, edge, plane_len, classes, shares, chunk, reach)),
        out_shape=jax.ShapeDtypeStruct((classes, shares, units, SUBLANES, LANES), jnp.bfloat16),
        in_specs=[pl.BlockSpec(memory_space=pltpu.HBM)] * 8,
        out_specs=vmem,
        scratch_shapes=[
            pltpu.SMEM(offsets.shape, offsets.dtype),
            pltpu.VMEM(psi.shape, psi.dtype),
            pltpu.VMEM(potential.shape, potential.dtype),
            pltpu.VMEM(kinetic.shape, jnp.bfloat16),
            pltpu.VMEM(cross.shape, jnp.bfloat16),
            pltpu.VMEM(kernel.shape, kernel.dtype),
            pltpu.VMEM(multipliers.shape, multipliers.dtype),
            pltpu.VMEM(pattern.shape, pattern.dtype),
            pltpu.SemaphoreType.DMA((8,)),
        ],
        compiler_params=params,
        name="send",
    )(
        offsets,
        *(in_hbm(x) for x in (psi, potential, jnp.asarray(kinetic), jnp.asarray(cross))),
        *(in_hbm(x) for x in (kernel, multipliers, pattern)),
    )
    sent = sent.reshape(devices, units, SUBLANES, LANES)
    axes = ("brick", "sub")
    held = lax.all_to_all(sent, axes, 0, 0, tiled=True)

    back_units = tiles + (tiles + 1) // 2 + 1
    made = pl.pallas_call(
        functools.partial(grid_kernel, (fn_count, edge, classes, shares, width, band_reach, sub_count)),
        out_shape=jax.ShapeDtypeStruct((devices, back_units, SUBLANES, LANES), jnp.bfloat16),
        in_specs=[vmem],
        out_specs=vmem,
        compiler_params=params,
        name="grid",
    )(held)
    back = lax.all_to_all(made, axes, 0, 0, tiled=True)
    back = back.reshape(classes, shares, back_units, SUBLANES, LANES)
    return pl.pallas_call(
        functools.partial(receive_kernel, (fn_count, edge, plane_len, classes, shares, band_reach, sub_count)),
        out_shape=(
            jax.ShapeDtypeStruct(psi.shape, jnp.bfloat16),
            jax.ShapeDtypeStruct((fn_count, width), jnp.float32),
            jax.ShapeDtypeStruct((fn_count, width), jnp.float32),
        ),
        in_specs=[pl.BlockSpec(memory_space=pltpu.HBM), vmem],
        out_specs=(vmem, vmem, vmem),
        scratch_shapes=[pltpu.SMEM(offsets.shape, offsets.dtype), pltpu.SemaphoreType.DMA],
        compiler_params=params,
        name="receive",
    )(offsets, back)


def any_shards(psi, potential, offsets, kernel, multipliers, pattern):
    devices = lax.axis_size("brick") * lax.axis_size("sub")
    plan = plan_of(devices, *psi.shape, kernel.shape[1])
    if plan is None:
        return shards(psi, potential, offsets, kernel, multipliers, pattern)
    return transposed_shards(*plan, psi, potential, offsets, kernel, multipliers, pattern)


def solution(mesh):
    in_specs = (
        P(("brick", "sub"), None, None),
        P(("brick", "sub"), None, None),
        P(("brick", "sub")),
        P(("brick", "sub"), None),
        P(("brick", "sub"), None),
        P(("brick", "sub"), None),
    )
    out_specs = (
        P(("brick", "sub"), None, None),
        P(("brick", "sub"), None),
        P(("brick", "sub"), None),
    )
    return jax.shard_map(any_shards, mesh=mesh, in_specs=in_specs, out_specs=out_specs, check_vma=False)
```

```python
import functools
import math

import jax
import jax.numpy as jnp
import numpy as np
from jax import lax
from jax.experimental import pallas as pl
from jax.experimental.pallas import tpu as pltpu
from jax.sharding import PartitionSpec as P

Q = 8
K = 6


filter_reach = 14


def shifted(block, axis, distance):
    devices = range(lax.axis_size(axis))
    route = [((i - distance) % len(devices), i) for i in devices]
    return lax.ppermute(block, axis, route)


def kinetic_matrix(edge_len):
    positions = jnp.arange(edge_len, dtype=jnp.int32)
    offset_gap = positions[:, None] - positions[None, :]
    distance = jnp.abs(offset_gap).astype(jnp.float32)
    parity_sign = 1.0 - 2.0 * (jnp.abs(offset_gap) % 2).astype(jnp.float32)
    off_diag = parity_sign / jnp.maximum(distance, 1.0) ** 2
    entries = jnp.where(offset_gap == 0, math.pi**2 / 6.0, off_diag)
    entries = jnp.where(jnp.abs(offset_gap) <= filter_reach, entries, 0.0)
    return entries.astype(jnp.bfloat16)


def cross_matrix(kinetic, edge_len):
    kin_float = kinetic.astype(jnp.float32)
    identity = jnp.eye(edge_len, dtype=jnp.float32)
    return (jnp.kron(kin_float, identity) + jnp.kron(identity, kin_float)).astype(jnp.bfloat16)


def apply_hamiltonian(psi, potential):
    fn_count, edge_len, plane_len = psi.shape
    kinetic = kinetic_matrix(edge_len)
    first_pass = jnp.einsum("wx,fxq->fwq", kinetic, psi, preferred_element_type=jnp.float32)
    cross = cross_matrix(kinetic, edge_len)
    second_pass = jnp.dot(
        psi.reshape(fn_count * edge_len, plane_len), cross, preferred_element_type=jnp.float32
    )
    summed = first_pass + second_pass.reshape(fn_count, edge_len, plane_len)
    result = summed + potential.astype(jnp.float32) * psi.astype(jnp.float32)
    return result.astype(jnp.bfloat16)


def embed(functions, region_start, window_len):

    def place(function, start_at):
        zeros_block = jnp.zeros((window_len, function.shape[1]), function.dtype)
        return lax.dynamic_update_slice_in_dim(zeros_block, function, start_at, 0)

    return jax.vmap(place)(functions, region_start)


def extract(window, region_start, edge_len):

    def take(planes, start_at):
        return lax.dynamic_slice_in_dim(planes, start_at, edge_len, 0)

    return jax.vmap(take)(window, region_start)


def dense_kernel(band_rows, group_count, band_reach, fn_count):
    dense_rows = []
    for slot_group in range(group_count):
        padded = jnp.pad(
            band_rows[slot_group], ((0, 0), (group_count * fn_count, group_count * fn_count))
        )
        first_col = (group_count + band_reach - slot_group) * fn_count
        dense_rows.append(padded[:, first_col : first_col + group_count * fn_count])
    return jnp.concatenate(dense_rows, axis=0)


def band_from_dense(dense, group_count, band_reach, fn_count):
    padded = jnp.pad(dense, ((0, 0), (band_reach * fn_count, band_reach * fn_count)))
    band_width = (2 * band_reach + 1) * fn_count
    pieces = []
    for slot_group in range(group_count):
        first_col = slot_group * fn_count
        pieces.append(padded[first_col : first_col + fn_count, first_col : first_col + band_width])
    return jnp.stack(pieces)


def grid_work(phi, hphi, kernel_rows, multi_rows, group_count, band_reach, fn_count, edge_len):
    volume_scale = 1.0 / float(edge_len**3)
    contract = (((1,), (1,)), ((), ()))
    margin = lax.dot_general(phi, phi, contract, preferred_element_type=jnp.float32) * volume_scale
    energy = lax.dot_general(phi, hphi, contract, preferred_element_type=jnp.float32) * volume_scale
    mixed = jnp.concatenate(
        [
            dense_kernel(kernel_rows, group_count, band_reach, fn_count),
            -dense_kernel(multi_rows, group_count, band_reach, fn_count),
        ],
        axis=1,
    )
    stacked = jnp.concatenate([hphi, phi], axis=0)
    grad = jnp.dot(mixed, stacked, preferred_element_type=jnp.float32).astype(jnp.bfloat16)
    margin_rows = band_from_dense(margin, group_count, band_reach, fn_count).astype(jnp.bfloat16)
    energy_rows = band_from_dense(energy, group_count, band_reach, fn_count).astype(jnp.bfloat16)
    return (grad, margin_rows, energy_rows)


def shards(psi, potential, offsets, kernel, multipliers, pattern):
    fn_count, edge_len, plane_len = psi.shape
    sub_count = lax.axis_size("sub")
    brick_count = lax.axis_size("brick")
    total_planes = Q * sub_count * brick_count
    band_reach = 2 * K
    band_width = kernel.shape[1]
    hpsi = apply_hamiltonian(psi, potential)
    spread = jnp.repeat(pattern, fn_count, axis=1).astype(jnp.bfloat16)
    kernel_eff = kernel * spread
    multi_eff = multipliers * spread
    margin_sum = jnp.zeros((fn_count, band_width), jnp.float32)
    energy_sum = jnp.zeros((fn_count, band_width), jnp.float32)
    my_rank = lax.axis_index("brick") * sub_count + lax.axis_index("sub")
    group_count = 2 * K + 1
    window_len = group_count * Q
    region_start = jnp.mod(offsets - (my_rank - K) * Q, total_planes)
    window_psi = embed(psi, region_start, window_len)
    window_hpsi = embed(hpsi, region_start, window_len)
    arrived = [None] * group_count
    for offset in range(-K, K + 1):
        first_plane = (offset + K) * Q
        payload = (
            window_psi[:, first_plane : first_plane + Q],
            window_hpsi[:, first_plane : first_plane + Q],
            kernel_eff,
            multi_eff,
        )
        if offset != 0:
            payload = shifted(
                (payload[0], payload[1], payload[2], payload[3]), ("brick", "sub"), offset
            )
        arrived[K - offset] = payload
    phi = jnp.concatenate([arrival[0] for arrival in arrived], axis=0).reshape(
        group_count * fn_count, Q * plane_len
    )
    hphi = jnp.concatenate([arrival[1] for arrival in arrived], axis=0).reshape(
        group_count * fn_count, Q * plane_len
    )
    kernel_rows = jnp.stack([arrival[2] for arrival in arrived])
    multi_rows = jnp.stack([arrival[3] for arrival in arrived])
    grad, margin_rows, energy_rows = grid_work(
        phi, hphi, kernel_rows, multi_rows, group_count, band_reach, fn_count, edge_len
    )
    grad = grad.reshape(group_count, fn_count, Q, plane_len)
    window = [None] * group_count
    for offset in range(-K, K + 1):
        slot_group = K - offset
        payload = (grad[slot_group], margin_rows[slot_group], energy_rows[slot_group])
        if offset != 0:
            payload = shifted((payload[0], payload[1], payload[2]), ("brick", "sub"), -offset)
        window[offset + K] = payload[0]
        margin_sum = margin_sum + payload[1].astype(jnp.float32)
        energy_sum = energy_sum + payload[2].astype(jnp.float32)
    gradient = extract(jnp.concatenate(window, axis=1), region_start, edge_len)
    return (gradient, margin_sum, energy_sum)


SUBLANES = 8
LANES = 128


def iota(shape, dim):
    return lax.broadcasted_iota(jnp.int32, shape, dim)


def plan_of(devices, fn_count, edge_len, plane_len, band_width):
    tiles = plane_len // LANES
    for shares in range(1, tiles + 1):
        if devices % shares or tiles % shares:
            continue
        classes = devices // shares
        per_class = edge_len // classes
        fits = (
            plane_len % LANES == 0
            and edge_len % classes == 0
            and (devices * Q) % classes == 0
            and classes & (classes - 1) == 0
            and fn_count * 2 == SUBLANES
            and per_class == 3
            and edge_len % SUBLANES == 0
            and band_width + 2 <= LANES
            and devices * SUBLANES == 2 * LANES
            and band_width == (4 * K + 1) * fn_count
        )
        if fits:
            return classes, shares
    return None


def kinetic_numpy(edge_len):
    positions = np.arange(edge_len)
    gap = np.abs(positions[:, None] - positions[None, :])
    sign = 1.0 - 2.0 * (gap % 2)
    entries = sign / np.maximum(gap, 1).astype(np.float32) ** 2
    entries = np.where(gap == 0, np.float32(math.pi**2 / 6.0), entries)
    entries = np.where(gap <= filter_reach, entries, 0.0)
    return entries.astype(np.float32)


def cross_stack(edge_len, rows, reach):
    kin = kinetic_numpy(edge_len).astype(jnp.bfloat16).astype(np.float32)
    line = kin[0]
    blocks = []
    for step in range(-reach, reach + 1):
        gap = np.abs(np.arange(rows)[:, None] + step * rows - np.arange(rows)[None, :])
        along_y = np.where(gap <= filter_reach, line[np.minimum(gap, edge_len - 1)], 0.0)
        block = np.kron(along_y, np.eye(edge_len, dtype=np.float32))
        if step == 0:
            block = block + np.kron(np.eye(rows, dtype=np.float32), kin)
        blocks.append(block)
    return np.concatenate(blocks, axis=0).astype(jnp.bfloat16)


def dot(a, b):
    return lax.dot_general(a, b, (((1,), (0,)), ((), ())), preferred_element_type=jnp.float32)


def dot_nt(a, b):
    return lax.dot_general(a, b, (((1,), (1,)), ((), ())), preferred_element_type=jnp.float32)


def in_hbm(array):
    return pltpu.with_memory_space_constraint(array, pltpu.HBM)


def pick(index, values):
    out = jnp.full(index.shape, values[0], jnp.int32)
    for k in range(1, len(values)):
        out = jnp.where(index == k, values[k], out)
    return out


def fetch(pairs, sems):
    copies = [pltpu.make_async_copy(source, target, sems.at[n]) for n, (source, target) in enumerate(pairs)]
    for copy in copies:
        copy.start()
    return copies


def class_select(target, offs, fn_count, edge, classes, least=0):
    shape = target.shape
    item, lane = iota(shape, 1), iota(shape, 2)
    member = item % fn_count
    depth = jnp.minimum(item // fn_count + least, 2)
    inner = jnp.bitwise_and(target - pick(member, offs), classes - 1)
    source = member * edge + depth * classes + inner
    rows = fn_count * edge
    wide = [
        jnp.where(source == lane + k * LANES, 1.0, 0.0).astype(jnp.bfloat16)
        for k in range(-(-rows // LANES))
    ]
    return jnp.concatenate(wide, axis=2).reshape(shape[0] * shape[1], -1)[:, :rows]


def coefficient_rows(band, pattern, offs, fn_count):
    width, blocks = band.shape[1], pattern.shape[1]
    spread = jnp.where(
        iota((blocks, width), 1) // fn_count == iota((blocks, width), 0), 1.0, 0.0
    ).astype(jnp.bfloat16)
    small = band.astype(jnp.float32) * dot(pattern.astype(jnp.float32).astype(jnp.bfloat16), spread)
    small = jnp.concatenate([small, small], axis=0)
    small = jnp.concatenate([small, jnp.zeros((SUBLANES, LANES - width), jnp.float32)], axis=1)
    at, lane = iota((SUBLANES, LANES), 0), iota((SUBLANES, LANES), 1)
    off = pick(at % fn_count, offs)
    small = jnp.where(lane == width, (off // 256).astype(jnp.float32), small)
    return jnp.where(lane == width + 1, (off % 256).astype(jnp.float32), small)


def pack_kernel(dims, offs_hbm, *refs):
    fn_count, edge, plane_len, classes, shares, groups, sub_count, carried = dims
    sources, outs, kept = refs[:carried], refs[carried : carried + groups], refs[carried + groups : -2]
    offs_ref, sems = refs[-2:]
    copies = fetch(((offs_hbm, offs_ref), *zip(sources, kept)), sems)
    rows = fn_count * edge
    tiles = plane_len // LANES // shares
    near = classes // groups
    rank = lax.axis_index("brick") * sub_count + lax.axis_index("sub")
    mine = jnp.bitwise_and(rank, shares - 1)
    copies[0].wait()
    offs = [offs_ref[k] for k in range(fn_count)]
    target = jnp.bitwise_xor(iota((classes, SUBLANES, LANES), 0), rank // shares)
    select = class_select(target, offs, fn_count, edge, classes)
    copies[1].wait()
    psi = kept[0][...].reshape(rows, plane_len)
    for share in range(shares):
        there = jnp.bitwise_xor(mine, share)
        ordered = dot(select, psi[:, share * tiles * LANES : (share + 1) * tiles * LANES])
        ordered = ordered.reshape(groups, near, SUBLANES, tiles * LANES)
        for k in range(groups):
            for t in range(tiles):
                outs[k][:, there, t] = ordered[k, :, :, t * LANES : (t + 1) * LANES].astype(jnp.bfloat16)
    for copy in copies[2:]:
        copy.wait()


def apply_kernel(
    dims,
    offs_hbm,
    psi_ref,
    pot_ref,
    cross_ref,
    kin_ref,
    kern_ref,
    mult_ref,
    patt_ref,
    out_ref,
    offs_ref,
    sems,
):
    fn_count, edge, plane_len, classes, shares, chunk, reach = dims
    copies = fetch(((offs_hbm, offs_ref),), sems)
    rows = fn_count * edge
    tiles = plane_len // LANES // shares
    pairs = (tiles + 1) // 2
    chunks = plane_len // chunk
    psi = psi_ref[...].reshape(rows, plane_len)
    pot = pot_ref[...].reshape(rows, plane_len)
    copies[0].wait()
    offs = [offs_ref[k] for k in range(fn_count)]
    shape = (classes, 2 * SUBLANES, LANES)
    select = class_select(iota(shape, 0), offs, fn_count, edge, classes)
    shape = (classes, SUBLANES, LANES)
    deep = class_select(iota(shape, 0), offs, fn_count, edge, classes, 2)
    lead = jnp.concatenate([kin_ref[...], deep], axis=0)
    patt = patt_ref[...]
    small = [coefficient_rows(ref[...], patt, offs, fn_count)[None] for ref in (mult_ref, kern_ref)]
    upper = iota(shape, 1) < fn_count
    held = {}
    for j in range(chunks):
        lo, hi = max(0, j - reach), min(chunks, j + reach + 1)
        here = slice(j * chunk, (j + 1) * chunk)
        acc = dot(
            psi[:, lo * chunk : hi * chunk],
            cross_ref[(lo - j + reach) * chunk : (hi - j + reach) * chunk, :],
        )
        led = dot(lead, psi[:, here])
        acc = acc + led[:rows]
        acc = acc + pot[:, here].astype(jnp.float32) * psi[:, here].astype(jnp.float32)
        ordered = dot(select, acc.astype(jnp.bfloat16)).reshape(classes, 2, SUBLANES, chunk)
        deeps = (ordered[:, 1], led[rows:].reshape(classes, SUBLANES, chunk))
        for n in range(chunk // LANES):
            share, t = divmod(j * (chunk // LANES) + n, tiles)
            at = slice(n * LANES, (n + 1) * LANES)
            out_ref[:, share, t] = ordered[:, 0, :, at].astype(jnp.bfloat16)
            for kind in range(2):
                value = deeps[kind][:, :, at]
                if t % 2 == 0 and t + 1 < tiles:
                    held[kind, share] = value
                    continue
                pair = (held[kind, share], value) if t % 2 else (value, small[kind])
                out_ref[:, share, tiles + kind * pairs + t // 2] = jnp.where(upper, *pair).astype(jnp.bfloat16)


def turn_kernel(*refs):
    groups = len(refs) - refs[0].shape[0]
    arrived, outs = refs[:groups], refs[groups:]
    for near, out in enumerate(outs):
        for far in range(groups):
            out[far] = arrived[far][near]


def grid_kernel(dims, *refs):
    fn_count, edge, classes, shares, width, band_reach, sub_count = dims
    psi_refs, (h_ref, out_ref, psi_all) = refs[:-3], refs[-3:]
    devices = h_ref.shape[0]
    tiles = psi_refs[0].shape[1]
    pairs = (tiles + 1) // 2
    full = devices * SUBLANES
    rank = lax.axis_index("brick") * sub_count + lax.axis_index("sub")
    my_class = rank // shares
    classes_bits = classes.bit_length() - 1
    near = len(psi_refs)
    for n, ref in enumerate(psi_refs):
        for far in range(ref.shape[0]):
            psi_all[jnp.bitwise_xor(rank, far * near + n)] = ref[far]

    upper = iota((devices, SUBLANES, LANES), 1) < fn_count
    both = []
    for v in range(pairs):
        ours = h_ref[:, tiles + pairs + v].astype(jnp.float32)
        theirs = h_ref[:, tiles + v].astype(jnp.float32)
        both.append(jnp.where(upper, ours, pltpu.roll(theirs, fn_count, axis=1)))
        both.append(jnp.where(upper, pltpu.roll(ours, fn_count, axis=1), theirs))
    halves = both.pop()
    stacked = [
        jnp.concatenate([psi_all[:, t].reshape(full, LANES) for t in range(tiles)], axis=1),
        jnp.concatenate([x.reshape(full, LANES).astype(jnp.bfloat16) for x in both], axis=1),
        jnp.concatenate([h_ref[:, t].reshape(full, LANES) for t in range(tiles)], axis=1),
    ]

    flat = halves.reshape(full, LANES).astype(jnp.bfloat16)
    where_hi, where_lo = width, width + 1
    lane_a, lane_b = iota((LANES, full), 0), iota((full, LANES), 1)
    weigh_a = jnp.where(lane_a == where_hi, 256.0, jnp.where(lane_a == where_lo, 1.0, 0.0))
    weigh_b = jnp.where(lane_b == where_hi, 256.0, jnp.where(lane_b == where_lo, 1.0, 0.0))
    off_row = dot(flat, weigh_a.astype(jnp.bfloat16)).astype(jnp.int32)
    off_col = dot_nt(weigh_b.astype(jnp.bfloat16), flat).astype(jnp.int32)

    planes = devices * Q // classes

    def first_plane(off):
        inner = jnp.bitwise_and(my_class - off, classes - 1)
        return jnp.right_shift(off + inner - my_class, classes_bits)

    gap = first_plane(off_row) - first_plane(off_col)
    half_row = jnp.bitwise_and(iota((full, full), 0) // fn_count, 1)
    half_col = jnp.bitwise_and(iota((full, full), 1) // fn_count, 1)

    def mask(row_depth, col_depth):
        return jnp.bitwise_and(gap + row_depth - col_depth, planes - 1) == 0

    col_depth = (half_col, 2, half_col)
    low = [mask(half_row, d) for d in col_depth]
    top = [mask(2, d) for d in col_depth]

    turned = pltpu.roll(halves, fn_count, axis=1)
    expand = jnp.where(
        (iota((LANES, full), 0) == iota((LANES, full), 1) // SUBLANES * fn_count + iota((LANES, full), 1) % fn_count)
        & (iota((LANES, full), 0) < width),
        1.0,
        0.0,
    ).astype(jnp.bfloat16)

    def dense(rows):
        wide = dot(rows.reshape(full, LANES).astype(jnp.bfloat16), expand)
        turned_rows = []
        for owner in range(devices):
            shift = (owner - band_reach) * SUBLANES % full
            block = wide[owner * SUBLANES : (owner + 1) * SUBLANES]
            turned_rows.append(pltpu.roll(block, shift, axis=1) if shift else block)
        return jnp.concatenate(turned_rows, axis=0)

    plus = dense(jnp.where(upper, halves, turned))
    minus = -dense(jnp.where(upper, turned, halves))
    coef = (minus, jnp.where(half_col == 0, minus, plus), plus)
    mixed = jnp.concatenate(
        [
            jnp.concatenate([jnp.where(k, c, 0.0).astype(jnp.bfloat16) for k, c in zip(ks, coef)], axis=1)
            for ks in (low, top)
        ],
        axis=0,
    )

    grad = dot(mixed, jnp.concatenate(stacked, axis=0))
    for t in range(tiles):
        out_ref[:, t] = (
            grad[:full, t * LANES : (t + 1) * LANES].reshape(devices, SUBLANES, LANES).astype(jnp.bfloat16)
        )
    second = grad[full:].reshape(devices, SUBLANES, tiles * LANES)
    for v in range((tiles + 1) // 2):
        even = second[:, :, 2 * v * LANES : (2 * v + 1) * LANES]
        if 2 * v + 1 < tiles:
            even = jnp.where(upper, even, second[:, :, (2 * v + 1) * LANES : (2 * v + 2) * LANES])
        out_ref[:, tiles + v] = even.astype(jnp.bfloat16)

    sums = []
    for part in range(3):
        low_gram = jnp.where(low[part], dot_nt(stacked[0], stacked[part]), 0.0)
        top_gram = dot_nt(stacked[1], stacked[part])
        top_gram = jnp.where(top[part] & (half_row == 0), top_gram, 0.0)
        total = (low_gram + top_gram).reshape(devices, SUBLANES, full)
        sums.append(total + pltpu.roll(total, fn_count, axis=1))
    first = sums[0] + pltpu.roll(sums[0], full - fn_count, axis=2)
    third = sums[2] + pltpu.roll(sums[2], fn_count, axis=2)
    lanes_half = jnp.bitwise_and(iota((devices, SUBLANES, full), 2) // fn_count, 1)
    bands = sums[1] + jnp.where(lanes_half == 0, first, third)
    bands = jnp.where(upper, bands[:, :, :LANES], bands[:, :, LANES:])
    bands = bands * (1.0 / float(edge**3))
    out_ref[:, tiles + (tiles + 1) // 2] = bands.astype(jnp.bfloat16)


def receive_kernel(dims, offs_hbm, in_ref, grad_ref, margin_ref, energy_ref, offs_ref, sem):
    fn_count, edge, plane_len, classes, shares, band_reach, sub_count = dims
    tiles = plane_len // LANES // shares
    rows = fn_count * edge
    devices = classes * shares
    width = margin_ref.shape[1]
    copy = pltpu.make_async_copy(offs_hbm, offs_ref, sem)
    copy.start()
    copy.wait()
    rank = lax.axis_index("brick") * sub_count + lax.axis_index("sub")
    offs = [offs_ref[k] for k in range(fn_count)]
    inner = classes * SUBLANES

    shape = (fn_count, edge, inner)
    member, plane = iota(shape, 0), iota(shape, 1)
    slot = iota(shape, 2)
    cls, sub = slot // SUBLANES, slot % SUBLANES
    half, owner_fn = sub // fn_count, sub % fn_count
    at = jnp.bitwise_and(cls - pick(owner_fn, offs), classes - 1)
    same = owner_fn == member
    low = jnp.where(same & (plane == at + half * classes), 1.0, 0.0)
    top = same & (plane == at + 2 * classes)
    for parity in range(2):
        tops = jnp.where(top & (half == parity), 1.0, 0.0)
        place = jnp.concatenate([low.astype(jnp.bfloat16), tops.astype(jnp.bfloat16)], axis=2)
        place = place.reshape(rows, 2 * inner)
        columns, spots = [], []
        for share in range(shares):
            for t in range(parity, tiles, 2):
                columns.append(
                    jnp.concatenate(
                        [
                            in_ref[:, share, t].reshape(inner, LANES),
                            in_ref[:, share, tiles + t // 2].reshape(inner, LANES),
                        ],
                        axis=0,
                    )
                )
                spots.append((share * tiles + t) * LANES)
        placed = dot(place, jnp.concatenate(columns, axis=1)).astype(jnp.bfloat16)
        for n, spot in enumerate(spots):
            grad_ref[:, :, spot : spot + LANES] = placed[:, n * LANES : (n + 1) * LANES].reshape(
                fn_count, edge, LANES
            )

    total = jnp.sum(
        in_ref[:, :, tiles + (tiles + 1) // 2].reshape(devices, SUBLANES, LANES).astype(jnp.float32), axis=0
    )
    lane, col = iota((LANES, LANES), 0), iota((LANES, LANES), 1)
    partner = lax.rem(rank + col // fn_count - band_reach + devices, devices)
    for kind, ref in ((0, margin_ref), (1, energy_ref)):
        wanted = partner * SUBLANES + kind * fn_count + col % fn_count
        picked = [
            lax.dot_general(
                total,
                jnp.where(wanted == lane + part * LANES, 1.0, 0.0),
                (((1,), (0,)), ((), ())),
                preferred_element_type=jnp.float32,
                precision=lax.Precision.HIGHEST,
            )
            for part in range(2)
        ]
        ref[...] = (picked[0][:fn_count] + picked[1][fn_count:])[:, :width]


def transposed_shards(classes, shares, psi, potential, offsets, kernel, multipliers, pattern):
    fn_count, edge, plane_len = psi.shape
    sub_count = lax.axis_size("sub")
    devices = sub_count * lax.axis_size("brick")
    width = kernel.shape[1]
    tiles = plane_len // LANES // shares
    band_reach = 2 * K
    chunk = edge * SUBLANES
    reach = -(-filter_reach // SUBLANES)
    params = pltpu.CompilerParams(vmem_limit_bytes=20 * 2**20)
    vmem = pl.BlockSpec(memory_space=pltpu.VMEM)

    hbm = pl.BlockSpec(memory_space=pltpu.HBM)
    groups = 4
    near = devices // groups
    kinetic = np.kron(np.eye(fn_count, dtype=np.float32), kinetic_numpy(edge)).astype(jnp.bfloat16)
    cross = cross_stack(edge, SUBLANES, reach)
    units = tiles + (tiles + 1) // 2 * 2
    offsets = in_hbm(offsets)

    def block(*lead):
        return jax.ShapeDtypeStruct((*lead, SUBLANES, LANES), jnp.bfloat16)

    def cost(flops, moved):
        return pl.CostEstimate(flops=flops, bytes_accessed=moved, transcendentals=0)

    def exchange(array, bits):
        return lax.ppermute(array, axes, [(i, i ^ bits) for i in range(devices)])

    axes = ("brick", "sub")
    size = psi.size
    kinetic, cross = jnp.asarray(kinetic), jnp.asarray(cross)
    carried = (psi, potential, cross, kinetic, kernel, multipliers, pattern)
    results = pl.pallas_call(
        functools.partial(
            pack_kernel, (fn_count, edge, plane_len, classes, shares, groups, sub_count, len(carried))
        ),
        out_shape=[block(near // shares, shares, tiles)] * groups
        + [jax.ShapeDtypeStruct(x.shape, x.dtype) for x in carried],
        in_specs=[hbm] * (1 + len(carried)),
        out_specs=[vmem] * (groups + len(carried)),
        scratch_shapes=[
            pltpu.SMEM(offsets.shape, offsets.dtype),
            pltpu.SemaphoreType.DMA((1 + len(carried),)),
        ],
        compiler_params=params,
        cost_estimate=cost(512 * size, 4 * size),
        name="pack",
    )(offsets, *(in_hbm(x) for x in carried))
    packed, kept = results[:groups], results[groups:]
    packed = [x.reshape(near, tiles, SUBLANES, LANES) for x in packed]
    arrived = [None] * groups
    arrived[0] = packed[0]
    for far in (3, 2, 1):
        arrived[far] = exchange(packed[far], far * near)

    applied = pl.pallas_call(
        functools.partial(apply_kernel, (fn_count, edge, plane_len, classes, shares, chunk, reach)),
        out_shape=block(classes, shares, units),
        in_specs=[hbm] + [vmem] * len(kept),
        out_specs=vmem,
        scratch_shapes=[pltpu.SMEM(offsets.shape, offsets.dtype), pltpu.SemaphoreType.DMA((1,))],
        compiler_params=params,
        cost_estimate=cost(4608 * size, 8 * size),
        name="apply",
    )(offsets, *kept)
    held = lax.all_to_all(applied.reshape(devices, units, SUBLANES, LANES), axes, 0, 0, tiled=True)

    turned = pl.pallas_call(
        turn_kernel,
        out_shape=[block(groups, tiles)] * near,
        in_specs=[vmem] * groups,
        out_specs=[vmem] * near,
        compiler_params=params,
        cost_estimate=cost(0, 4 * size),
        name="turn",
    )(*arrived)
    gathered = [x if n == 0 else exchange(x, n) for n, x in enumerate(turned)]

    back_units = tiles + (tiles + 1) // 2 + 1
    made = pl.pallas_call(
        functools.partial(grid_kernel, (fn_count, edge, classes, shares, width, band_reach, sub_count)),
        out_shape=jax.ShapeDtypeStruct((devices, back_units, SUBLANES, LANES), jnp.bfloat16),
        in_specs=[vmem] * (near + 1),
        out_specs=vmem,
        scratch_shapes=[pltpu.VMEM((devices, tiles, SUBLANES, LANES), jnp.bfloat16)],
        compiler_params=params,
        name="grid",
    )(*gathered, held)
    back = lax.all_to_all(made, axes, 0, 0, tiled=True)
    back = back.reshape(classes, shares, back_units, SUBLANES, LANES)
    return pl.pallas_call(
        functools.partial(receive_kernel, (fn_count, edge, plane_len, classes, shares, band_reach, sub_count)),
        out_shape=(
            jax.ShapeDtypeStruct(psi.shape, jnp.bfloat16),
            jax.ShapeDtypeStruct((fn_count, width), jnp.float32),
            jax.ShapeDtypeStruct((fn_count, width), jnp.float32),
        ),
        in_specs=[pl.BlockSpec(memory_space=pltpu.HBM), vmem],
        out_specs=(vmem, vmem, vmem),
        scratch_shapes=[pltpu.SMEM(offsets.shape, offsets.dtype), pltpu.SemaphoreType.DMA],
        compiler_params=params,
        name="receive",
    )(offsets, back)


def any_shards(psi, potential, offsets, kernel, multipliers, pattern):
    devices = lax.axis_size("brick") * lax.axis_size("sub")
    plan = plan_of(devices, *psi.shape, kernel.shape[1])
    if plan is None:
        return shards(psi, potential, offsets, kernel, multipliers, pattern)
    return transposed_shards(*plan, psi, potential, offsets, kernel, multipliers, pattern)


def solution(mesh):
    in_specs = (
        P(("brick", "sub"), None, None),
        P(("brick", "sub"), None, None),
        P(("brick", "sub")),
        P(("brick", "sub"), None),
        P(("brick", "sub"), None),
        P(("brick", "sub"), None),
    )
    out_specs = (
        P(("brick", "sub"), None, None),
        P(("brick", "sub"), None),
        P(("brick", "sub"), None),
    )
    return jax.shard_map(any_shards, mesh=mesh, in_specs=in_specs, out_specs=out_specs, check_vma=False)
```

```python
import functools
import math

import jax
import jax.numpy as jnp
import numpy as np
from jax import lax
from jax.experimental import pallas as pl
from jax.experimental.pallas import tpu as pltpu
from jax.sharding import PartitionSpec as P

Q = 8
K = 6


filter_reach = 14


def shifted(block, axis, distance):
    devices = range(lax.axis_size(axis))
    route = [((i - distance) % len(devices), i) for i in devices]
    return lax.ppermute(block, axis, route)


def kinetic_matrix(edge_len):
    positions = jnp.arange(edge_len, dtype=jnp.int32)
    offset_gap = positions[:, None] - positions[None, :]
    distance = jnp.abs(offset_gap).astype(jnp.float32)
    parity_sign = 1.0 - 2.0 * (jnp.abs(offset_gap) % 2).astype(jnp.float32)
    off_diag = parity_sign / jnp.maximum(distance, 1.0) ** 2
    entries = jnp.where(offset_gap == 0, math.pi**2 / 6.0, off_diag)
    entries = jnp.where(jnp.abs(offset_gap) <= filter_reach, entries, 0.0)
    return entries.astype(jnp.bfloat16)


def cross_matrix(kinetic, edge_len):
    kin_float = kinetic.astype(jnp.float32)
    identity = jnp.eye(edge_len, dtype=jnp.float32)
    return (jnp.kron(kin_float, identity) + jnp.kron(identity, kin_float)).astype(jnp.bfloat16)


def apply_hamiltonian(psi, potential):
    fn_count, edge_len, plane_len = psi.shape
    kinetic = kinetic_matrix(edge_len)
    first_pass = jnp.einsum("wx,fxq->fwq", kinetic, psi, preferred_element_type=jnp.float32)
    cross = cross_matrix(kinetic, edge_len)
    second_pass = jnp.dot(
        psi.reshape(fn_count * edge_len, plane_len), cross, preferred_element_type=jnp.float32
    )
    summed = first_pass + second_pass.reshape(fn_count, edge_len, plane_len)
    result = summed + potential.astype(jnp.float32) * psi.astype(jnp.float32)
    return result.astype(jnp.bfloat16)


def embed(functions, region_start, window_len):

    def place(function, start_at):
        zeros_block = jnp.zeros((window_len, function.shape[1]), function.dtype)
        return lax.dynamic_update_slice_in_dim(zeros_block, function, start_at, 0)

    return jax.vmap(place)(functions, region_start)


def extract(window, region_start, edge_len):

    def take(planes, start_at):
        return lax.dynamic_slice_in_dim(planes, start_at, edge_len, 0)

    return jax.vmap(take)(window, region_start)


def dense_kernel(band_rows, group_count, band_reach, fn_count):
    dense_rows = []
    for slot_group in range(group_count):
        padded = jnp.pad(
            band_rows[slot_group], ((0, 0), (group_count * fn_count, group_count * fn_count))
        )
        first_col = (group_count + band_reach - slot_group) * fn_count
        dense_rows.append(padded[:, first_col : first_col + group_count * fn_count])
    return jnp.concatenate(dense_rows, axis=0)


def band_from_dense(dense, group_count, band_reach, fn_count):
    padded = jnp.pad(dense, ((0, 0), (band_reach * fn_count, band_reach * fn_count)))
    band_width = (2 * band_reach + 1) * fn_count
    pieces = []
    for slot_group in range(group_count):
        first_col = slot_group * fn_count
        pieces.append(padded[first_col : first_col + fn_count, first_col : first_col + band_width])
    return jnp.stack(pieces)


def grid_work(phi, hphi, kernel_rows, multi_rows, group_count, band_reach, fn_count, edge_len):
    volume_scale = 1.0 / float(edge_len**3)
    contract = (((1,), (1,)), ((), ()))
    margin = lax.dot_general(phi, phi, contract, preferred_element_type=jnp.float32) * volume_scale
    energy = lax.dot_general(phi, hphi, contract, preferred_element_type=jnp.float32) * volume_scale
    mixed = jnp.concatenate(
        [
            dense_kernel(kernel_rows, group_count, band_reach, fn_count),
            -dense_kernel(multi_rows, group_count, band_reach, fn_count),
        ],
        axis=1,
    )
    stacked = jnp.concatenate([hphi, phi], axis=0)
    grad = jnp.dot(mixed, stacked, preferred_element_type=jnp.float32).astype(jnp.bfloat16)
    margin_rows = band_from_dense(margin, group_count, band_reach, fn_count).astype(jnp.bfloat16)
    energy_rows = band_from_dense(energy, group_count, band_reach, fn_count).astype(jnp.bfloat16)
    return (grad, margin_rows, energy_rows)


def shards(psi, potential, offsets, kernel, multipliers, pattern):
    fn_count, edge_len, plane_len = psi.shape
    sub_count = lax.axis_size("sub")
    brick_count = lax.axis_size("brick")
    total_planes = Q * sub_count * brick_count
    band_reach = 2 * K
    band_width = kernel.shape[1]
    hpsi = apply_hamiltonian(psi, potential)
    spread = jnp.repeat(pattern, fn_count, axis=1).astype(jnp.bfloat16)
    kernel_eff = kernel * spread
    multi_eff = multipliers * spread
    margin_sum = jnp.zeros((fn_count, band_width), jnp.float32)
    energy_sum = jnp.zeros((fn_count, band_width), jnp.float32)
    my_rank = lax.axis_index("brick") * sub_count + lax.axis_index("sub")
    group_count = 2 * K + 1
    window_len = group_count * Q
    region_start = jnp.mod(offsets - (my_rank - K) * Q, total_planes)
    window_psi = embed(psi, region_start, window_len)
    window_hpsi = embed(hpsi, region_start, window_len)
    arrived = [None] * group_count
    for offset in range(-K, K + 1):
        first_plane = (offset + K) * Q
        payload = (
            window_psi[:, first_plane : first_plane + Q],
            window_hpsi[:, first_plane : first_plane + Q],
            kernel_eff,
            multi_eff,
        )
        if offset != 0:
            payload = shifted(
                (payload[0], payload[1], payload[2], payload[3]), ("brick", "sub"), offset
            )
        arrived[K - offset] = payload
    phi = jnp.concatenate([arrival[0] for arrival in arrived], axis=0).reshape(
        group_count * fn_count, Q * plane_len
    )
    hphi = jnp.concatenate([arrival[1] for arrival in arrived], axis=0).reshape(
        group_count * fn_count, Q * plane_len
    )
    kernel_rows = jnp.stack([arrival[2] for arrival in arrived])
    multi_rows = jnp.stack([arrival[3] for arrival in arrived])
    grad, margin_rows, energy_rows = grid_work(
        phi, hphi, kernel_rows, multi_rows, group_count, band_reach, fn_count, edge_len
    )
    grad = grad.reshape(group_count, fn_count, Q, plane_len)
    window = [None] * group_count
    for offset in range(-K, K + 1):
        slot_group = K - offset
        payload = (grad[slot_group], margin_rows[slot_group], energy_rows[slot_group])
        if offset != 0:
            payload = shifted((payload[0], payload[1], payload[2]), ("brick", "sub"), -offset)
        window[offset + K] = payload[0]
        margin_sum = margin_sum + payload[1].astype(jnp.float32)
        energy_sum = energy_sum + payload[2].astype(jnp.float32)
    gradient = extract(jnp.concatenate(window, axis=1), region_start, edge_len)
    return (gradient, margin_sum, energy_sum)


EARLY_PAIRS = 1
SUBLANES = 8
LANES = 128


def iota(shape, dim):
    return lax.broadcasted_iota(jnp.int32, shape, dim)


def plan_of(devices, fn_count, edge_len, plane_len, band_width):
    tiles = plane_len // LANES
    for shares in range(1, tiles + 1):
        if devices % shares or tiles % shares:
            continue
        classes = devices // shares
        per_class = edge_len // classes
        fits = (
            plane_len % (2 * LANES) == 0
            and edge_len % classes == 0
            and tiles // shares > 2 * EARLY_PAIRS
            and (devices * Q) % classes == 0
            and classes & (classes - 1) == 0
            and fn_count * 2 == SUBLANES
            and per_class == 3
            and edge_len % SUBLANES == 0
            and band_width + 2 <= LANES
            and devices * SUBLANES == 2 * LANES
            and band_width == (4 * K + 1) * fn_count
        )
        if fits:
            return classes, shares
    return None


def kinetic_numpy(edge_len):
    positions = np.arange(edge_len)
    gap = np.abs(positions[:, None] - positions[None, :])
    sign = 1.0 - 2.0 * (gap % 2)
    entries = sign / np.maximum(gap, 1).astype(np.float32) ** 2
    entries = np.where(gap == 0, np.float32(math.pi**2 / 6.0), entries)
    entries = np.where(gap <= filter_reach, entries, 0.0)
    return entries.astype(np.float32)


def cross_blocks(edge_len, chunk):
    line = kinetic_numpy(edge_len).astype(jnp.bfloat16).astype(np.float32)[0]
    period = math.lcm(edge_len, chunk)
    reach = -(-filter_reach * edge_len // chunk)
    stacks = []
    for first in range(0, period, chunk):
        row = np.arange(first - reach * chunk, first + (reach + 1) * chunk)[:, None]
        col = np.arange(first, first + chunk)[None, :]
        gap_y = np.abs(row // edge_len - col // edge_len)
        gap_z = np.abs(row % edge_len - col % edge_len)
        weight = np.where(np.arange(edge_len) <= filter_reach, line, 0.0)
        block = np.where(gap_z == 0, weight[np.minimum(gap_y, edge_len - 1)], 0.0)
        block = block + np.where(gap_y == 0, weight[gap_z], 0.0)
        stacks.append(block)
    return np.stack(stacks).astype(jnp.bfloat16), reach


def dot(a, b):
    return lax.dot_general(a, b, (((1,), (0,)), ((), ())), preferred_element_type=jnp.float32)


def dot_nt(a, b):
    return lax.dot_general(a, b, (((1,), (1,)), ((), ())), preferred_element_type=jnp.float32)


def in_hbm(array):
    return pltpu.with_memory_space_constraint(array, pltpu.HBM)


def pick(index, values):
    out = jnp.full(index.shape, values[0], jnp.int32)
    for k in range(1, len(values)):
        out = jnp.where(index == k, values[k], out)
    return out


def fetch(pairs, sems):
    copies = [pltpu.make_async_copy(source, target, sems.at[n]) for n, (source, target) in enumerate(pairs)]
    for copy in copies:
        copy.start()
    return copies


def class_select(target, off_rows, fn_count, edge, classes, least=0):
    shape = target.shape
    item, lane = iota(shape, 1), iota(shape, 2)
    member = item % fn_count
    depth = jnp.minimum(item // fn_count + least, 2)
    off_rows = jnp.concatenate([off_rows] * (shape[1] // SUBLANES), axis=0)[None]
    inner = jnp.bitwise_and(target - off_rows, classes - 1)
    source = member * edge + depth * classes + inner
    rows = fn_count * edge
    wide = [
        jnp.where(source == lane + k * LANES, 1.0, 0.0).astype(jnp.bfloat16)
        for k in range(-(-rows // LANES))
    ]
    return jnp.concatenate(wide, axis=2).reshape(shape[0] * shape[1], -1)[:, :rows]


def coefficient_rows(band, pattern, off_rows, fn_count):
    width, blocks = band.shape[1], pattern.shape[1]
    spread = jnp.where(
        iota((blocks, width), 1) // fn_count == iota((blocks, width), 0), 1.0, 0.0
    ).astype(jnp.bfloat16)
    small = band.astype(jnp.float32) * dot(pattern.astype(jnp.float32).astype(jnp.bfloat16), spread)
    small = jnp.concatenate([small, small], axis=0)
    small = jnp.concatenate([small, jnp.zeros((SUBLANES, LANES - width), jnp.float32)], axis=1)
    lane = iota((SUBLANES, LANES), 1)
    small = jnp.where(lane == width, jnp.right_shift(off_rows, 8).astype(jnp.float32), small)
    return jnp.where(lane == width + 1, jnp.bitwise_and(off_rows, 255).astype(jnp.float32), small)


def pair_units(deep, count, upper, last):
    made = []
    for t in range(0, count, 2):
        even = deep[..., t * LANES : (t + 1) * LANES]
        odd = deep[..., (t + 1) * LANES : (t + 2) * LANES] if t + 1 < count else last
        made.append(jnp.where(upper, even, odd).astype(jnp.bfloat16))
    return made


def pack_kernel(dims, offs_hbm, *refs):
    fn_count, edge, plane_len, classes, shares, groups, sub_count, carried = dims
    sources, outs, kept = refs[:carried], refs[carried : carried + groups], refs[carried + groups : -4]
    off_rows_ref, off_lanes_ref, offs_ref, sems = refs[-4:]
    copies = fetch(((offs_hbm, offs_ref), *zip(sources, kept)), sems)
    rows = fn_count * edge
    tiles = plane_len // LANES // shares
    near = classes // groups
    rank = lax.axis_index("brick") * sub_count + lax.axis_index("sub")
    mine = jnp.bitwise_and(rank, shares - 1)
    copies[0].wait()
    offs = [offs_ref[k] for k in range(fn_count)]
    off_rows = pick(iota((SUBLANES, LANES), 0) % fn_count, offs)
    off_rows_ref[...] = off_rows
    off_lanes_ref[...] = pick(iota((SUBLANES, LANES), 1) % fn_count, offs)
    target = jnp.bitwise_xor(iota((classes, SUBLANES, LANES), 0), rank // shares)
    select = class_select(target, off_rows, fn_count, edge, classes)
    deep = class_select(target, off_rows, fn_count, edge, classes, 2)
    upper = iota((near, SUBLANES, LANES), 1) < fn_count
    copies[1].wait()
    psi = kept[0][...].reshape(rows, plane_len)
    for share in range(shares):
        there = jnp.bitwise_xor(mine, share)
        ordered = dot(select, psi[:, share * tiles * LANES : (share + 1) * tiles * LANES])
        ordered = ordered.reshape(groups, near, SUBLANES, tiles * LANES)
        for k in range(groups):
            for t in range(tiles):
                outs[k][:, there, t] = ordered[k, :, :, t * LANES : (t + 1) * LANES].astype(jnp.bfloat16)
        start = share * tiles * LANES
        second = dot(deep, psi[:, start : start + 2 * EARLY_PAIRS * LANES])
        second = second.reshape(groups, near, SUBLANES, 2 * EARLY_PAIRS * LANES)
        for k in range(groups):
            for v, piece in enumerate(pair_units(second[k], 2 * EARLY_PAIRS, upper, None)):
                outs[k][:, there, tiles + v] = piece
    for copy in copies[2:]:
        copy.wait()


def apply_kernel(
    dims,
    off_rows_ref,
    psi_ref,
    pot_ref,
    kin_ref,
    kern_ref,
    mult_ref,
    patt_ref,
    cross_hbm,
    out_ref,
    result_ref,
    cross_ref,
    sems,
):
    fn_count, edge, plane_len, classes, shares, chunk, reach = dims
    copies = fetch([(cross_hbm.at[k], cross_ref.at[k]) for k in range(cross_ref.shape[0])], sems)
    rows = fn_count * edge
    tiles = plane_len // LANES // shares
    chunks = plane_len // chunk
    psi = psi_ref[...].reshape(rows, plane_len)
    pot = pot_ref[...].reshape(rows, plane_len)
    off_rows = off_rows_ref[...]
    shape = (classes, 2 * SUBLANES, LANES)
    select = class_select(iota(shape, 0), off_rows, fn_count, edge, classes)
    shape = (classes, SUBLANES, LANES)
    deep = class_select(iota(shape, 0), off_rows, fn_count, edge, classes, 2)
    patt = patt_ref[...]
    small = [coefficient_rows(ref[...], patt, off_rows, fn_count)[None] for ref in (mult_ref, kern_ref)]
    upper = iota(shape, 1) < fn_count
    led = dot(kin_ref[...], psi)
    for j in range(chunks):
        if j < len(copies):
            copies[j].wait()
        lo, hi = max(0, j - reach), min(chunks, j + reach + 1)
        here = slice(j * chunk, (j + 1) * chunk)
        acc = dot(
            psi[:, lo * chunk : hi * chunk],
            cross_ref[j % cross_ref.shape[0], (lo - j + reach) * chunk : (hi - j + reach) * chunk],
        )
        acc = acc + led[:, here]
        acc = acc + pot[:, here].astype(jnp.float32) * psi[:, here].astype(jnp.float32)
        result_ref[:, here] = acc.astype(jnp.bfloat16)
    ordered = dot(select, result_ref[...]).reshape(classes, 2, SUBLANES, plane_len)
    late = 2 * EARLY_PAIRS
    for share in range(shares):
        first, last = share * tiles * LANES, (share + 1) * tiles * LANES
        for t in range(tiles):
            at = slice(first + t * LANES, first + (t + 1) * LANES)
            out_ref[:, share, t] = ordered[:, 0, :, at].astype(jnp.bfloat16)
        rest = dot(deep, psi[:, first + late * LANES : last]).reshape(classes, SUBLANES, -1)
        made = pair_units(ordered[:, 1, :, first:last], tiles, upper, small[0])
        made += pair_units(rest, tiles - late, upper, small[1])
        for v, piece in enumerate(made):
            out_ref[:, share, tiles + v] = piece


def turn_kernel(*refs):
    groups = len(refs) - refs[0].shape[0]
    arrived, outs = refs[:groups], refs[groups:]
    for near, out in enumerate(outs):
        for far in range(groups):
            out[far] = arrived[far][near]


def grid_kernel(dims, *refs):
    fn_count, edge, classes, shares, width, band_reach, sub_count = dims
    psi_refs, (h_ref, out_ref, psi_all) = refs[:-3], refs[-3:]
    devices = h_ref.shape[0]
    tiles = psi_refs[0].shape[1] - EARLY_PAIRS
    pairs = (tiles + 1) // 2
    full = devices * SUBLANES
    rank = lax.axis_index("brick") * sub_count + lax.axis_index("sub")
    my_class = rank // shares
    classes_bits = classes.bit_length() - 1
    near = len(psi_refs)
    for n, ref in enumerate(psi_refs):
        for far in range(ref.shape[0]):
            psi_all[jnp.bitwise_xor(rank, far * near + n)] = ref[far]

    upper = iota((devices, SUBLANES, LANES), 1) < fn_count
    both = []
    for v in range(pairs):
        early = v < EARLY_PAIRS
        ours = psi_all[:, tiles + v] if early else h_ref[:, tiles + pairs + v - EARLY_PAIRS]
        ours = ours.astype(jnp.float32)
        theirs = h_ref[:, tiles + v].astype(jnp.float32)
        both.append(jnp.where(upper, ours, pltpu.roll(theirs, fn_count, axis=1)))
        both.append(jnp.where(upper, pltpu.roll(ours, fn_count, axis=1), theirs))
    halves = both.pop()
    stacked = [
        jnp.concatenate([psi_all[:, t].reshape(full, LANES) for t in range(tiles)], axis=1),
        jnp.concatenate([x.reshape(full, LANES).astype(jnp.bfloat16) for x in both], axis=1),
        jnp.concatenate([h_ref[:, t].reshape(full, LANES) for t in range(tiles)], axis=1),
    ]

    flat = halves.reshape(full, LANES).astype(jnp.bfloat16)
    where_hi, where_lo = width, width + 1
    lane_a, lane_b = iota((LANES, full), 0), iota((full, LANES), 1)
    weigh_a = jnp.where(lane_a == where_hi, 256.0, jnp.where(lane_a == where_lo, 1.0, 0.0))
    weigh_b = jnp.where(lane_b == where_hi, 256.0, jnp.where(lane_b == where_lo, 1.0, 0.0))
    off_row = dot(flat, weigh_a.astype(jnp.bfloat16)).astype(jnp.int32)
    off_col = dot_nt(weigh_b.astype(jnp.bfloat16), flat).astype(jnp.int32)

    planes = devices * Q // classes

    def first_plane(off):
        inner = jnp.bitwise_and(my_class - off, classes - 1)
        return jnp.right_shift(off + inner - my_class, classes_bits)

    gap = first_plane(off_row) - first_plane(off_col)
    half_row = jnp.bitwise_and(iota((full, full), 0) // fn_count, 1)
    half_col = jnp.bitwise_and(iota((full, full), 1) // fn_count, 1)

    def mask(row_depth, col_depth):
        return jnp.bitwise_and(gap + row_depth - col_depth, planes - 1) == 0

    col_depth = (half_col, 2, half_col)
    low = [mask(half_row, d) for d in col_depth]
    top = [mask(2, d) for d in col_depth]

    turned = pltpu.roll(halves, fn_count, axis=1)
    expand = jnp.where(
        (iota((LANES, full), 0) == iota((LANES, full), 1) // SUBLANES * fn_count + iota((LANES, full), 1) % fn_count)
        & (iota((LANES, full), 0) < width),
        1.0,
        0.0,
    ).astype(jnp.bfloat16)

    def dense(rows):
        wide = dot(rows.reshape(full, LANES).astype(jnp.bfloat16), expand)
        turned_rows = []
        for owner in range(devices):
            shift = (owner - band_reach) * SUBLANES % full
            block = wide[owner * SUBLANES : (owner + 1) * SUBLANES]
            turned_rows.append(pltpu.roll(block, shift, axis=1) if shift else block)
        return jnp.concatenate(turned_rows, axis=0)

    plus = dense(jnp.where(upper, halves, turned))
    minus = -dense(jnp.where(upper, turned, halves))
    coef = (minus, jnp.where(half_col == 0, minus, plus), plus)
    mixed = jnp.concatenate(
        [
            jnp.concatenate([jnp.where(k, c, 0.0).astype(jnp.bfloat16) for k, c in zip(ks, coef)], axis=1)
            for ks in (low, top)
        ],
        axis=0,
    )

    grad = dot(mixed, jnp.concatenate(stacked, axis=0))
    for t in range(tiles):
        out_ref[:, t] = (
            grad[:full, t * LANES : (t + 1) * LANES].reshape(devices, SUBLANES, LANES).astype(jnp.bfloat16)
        )
    second = grad[full:].reshape(devices, SUBLANES, tiles * LANES)
    for v in range((tiles + 1) // 2):
        even = second[:, :, 2 * v * LANES : (2 * v + 1) * LANES]
        if 2 * v + 1 < tiles:
            even = jnp.where(upper, even, second[:, :, (2 * v + 1) * LANES : (2 * v + 2) * LANES])
        out_ref[:, tiles + v] = even.astype(jnp.bfloat16)

    sums = []
    for part in range(3):
        low_gram = jnp.where(low[part], dot_nt(stacked[0], stacked[part]), 0.0)
        top_gram = dot_nt(stacked[1], stacked[part])
        top_gram = jnp.where(top[part] & (half_row == 0), top_gram, 0.0)
        total = (low_gram + top_gram).reshape(devices, SUBLANES, full)
        sums.append(total + pltpu.roll(total, fn_count, axis=1))
    first = sums[0] + pltpu.roll(sums[0], full - fn_count, axis=2)
    third = sums[2] + pltpu.roll(sums[2], fn_count, axis=2)
    lanes_half = jnp.bitwise_and(iota((devices, SUBLANES, full), 2) // fn_count, 1)
    bands = sums[1] + jnp.where(lanes_half == 0, first, third)
    bands = jnp.where(upper, bands[:, :, :LANES], bands[:, :, LANES:])
    bands = bands * (1.0 / float(edge**3))
    out_ref[:, tiles + (tiles + 1) // 2] = bands.astype(jnp.bfloat16)


def receive_kernel(dims, off_lanes_ref, in_ref, grad_hbm, margin_ref, energy_ref, grad_ref, sems):
    fn_count, edge, plane_len, classes, shares, band_reach, sub_count = dims
    tiles = plane_len // LANES // shares
    rows = fn_count * edge
    devices = classes * shares
    width = margin_ref.shape[1]
    rank = lax.axis_index("brick") * sub_count + lax.axis_index("sub")
    inner = classes * SUBLANES

    shape = (fn_count, edge, inner)
    member, plane = iota(shape, 0), iota(shape, 1)
    slot = iota(shape, 2)
    cls, sub = slot // SUBLANES, slot % SUBLANES
    half, owner_fn = sub // fn_count, sub % fn_count
    off_lanes = jnp.concatenate([off_lanes_ref[...]] * (inner // LANES), axis=1)[:1, None]
    at = jnp.bitwise_and(cls - off_lanes, classes - 1)
    same = owner_fn == member
    low = jnp.where(same & (plane == at + half * classes), 1.0, 0.0).astype(jnp.bfloat16)
    top = same & (plane == at + 2 * classes)
    place = []
    for parity in range(2):
        tops = jnp.where(top & (half == parity), 1.0, 0.0).astype(jnp.bfloat16)
        place.append(jnp.concatenate([low, tops], axis=2).reshape(rows, 2 * inner))
    copies = []
    for share in range(shares):
        for parity in range(2):
            columns = [
                jnp.concatenate(
                    [
                        in_ref[:, share, t].reshape(inner, LANES),
                        in_ref[:, share, tiles + t // 2].reshape(inner, LANES),
                    ],
                    axis=0,
                )
                for t in range(parity, tiles, 2)
            ]
            placed = dot(place[parity], jnp.concatenate(columns, axis=1)).astype(jnp.bfloat16)
            for n, t in enumerate(range(parity, tiles, 2)):
                spot = (share * tiles + t) * LANES
                grad_ref[:, :, spot : spot + LANES] = placed[:, n * LANES : (n + 1) * LANES].reshape(
                    fn_count, edge, LANES
                )
        part = pl.ds(share * tiles * LANES, tiles * LANES)
        copies.append(
            pltpu.make_async_copy(grad_ref.at[:, :, part], grad_hbm.at[:, :, part], sems.at[share])
        )
        copies[-1].start()

    total = jnp.sum(
        in_ref[:, :, tiles + (tiles + 1) // 2].reshape(devices, SUBLANES, LANES).astype(jnp.float32), axis=0
    )
    terms = []
    for _ in range(3):
        terms.append(total.astype(jnp.bfloat16))
        total = total - terms[-1].astype(jnp.float32)
    terms = jnp.concatenate(terms + terms[-1:], axis=0)
    lane, col = iota((LANES, LANES), 0), iota((LANES, LANES), 1)
    partner = lax.rem(rank + col // fn_count - band_reach + devices, devices)
    for kind, ref in ((0, margin_ref), (1, energy_ref)):
        wanted = partner * SUBLANES + kind * fn_count + col % fn_count
        row = jnp.zeros((fn_count, LANES), jnp.float32)
        for part in range(2):
            picked = dot(terms, jnp.where(wanted == lane + part * LANES, 1.0, 0.0).astype(jnp.bfloat16))
            for n in range(3):
                first = n * SUBLANES + part * fn_count
                row = row + picked[first : first + fn_count]
        ref[...] = row[:, :width]
    for copy in copies:
        copy.wait()


def transposed_shards(classes, shares, psi, potential, offsets, kernel, multipliers, pattern):
    fn_count, edge, plane_len = psi.shape
    sub_count = lax.axis_size("sub")
    devices = sub_count * lax.axis_size("brick")
    width = kernel.shape[1]
    tiles = plane_len // LANES // shares
    band_reach = 2 * K
    chunk = 2 * LANES
    params = pltpu.CompilerParams(vmem_limit_bytes=20 * 2**20)
    vmem = pl.BlockSpec(memory_space=pltpu.VMEM)

    hbm = pl.BlockSpec(memory_space=pltpu.HBM)
    groups = 4
    near = devices // groups
    kinetic = np.kron(np.eye(fn_count, dtype=np.float32), kinetic_numpy(edge)).astype(jnp.bfloat16)
    cross, reach = cross_blocks(edge, chunk)
    early = tiles + EARLY_PAIRS
    units = tiles + (tiles + 1) // 2 * 2 - EARLY_PAIRS
    offsets = in_hbm(offsets)

    def block(*lead):
        return jax.ShapeDtypeStruct((*lead, SUBLANES, LANES), jnp.bfloat16)

    def cost(flops, moved):
        return pl.CostEstimate(flops=flops, bytes_accessed=moved, transcendentals=0)

    def exchange(array, bits):
        return lax.ppermute(array, axes, [(i, i ^ bits) for i in range(devices)])

    axes = ("brick", "sub")
    size = psi.size
    kinetic, cross = jnp.asarray(kinetic), jnp.asarray(cross)
    carried = (psi, potential, kinetic, kernel, multipliers, pattern)
    results = pl.pallas_call(
        functools.partial(
            pack_kernel, (fn_count, edge, plane_len, classes, shares, groups, sub_count, len(carried))
        ),
        out_shape=[block(near // shares, shares, early)] * groups
        + [jax.ShapeDtypeStruct(x.shape, x.dtype) for x in carried]
        + [jax.ShapeDtypeStruct((SUBLANES, LANES), jnp.int32)] * 2,
        in_specs=[hbm] * (1 + len(carried)),
        out_specs=[vmem] * (groups + len(carried) + 2),
        scratch_shapes=[
            pltpu.SMEM(offsets.shape, offsets.dtype),
            pltpu.SemaphoreType.DMA((1 + len(carried),)),
        ],
        compiler_params=params,
        cost_estimate=cost(512 * size, 4 * size),
        name="pack",
    )(offsets, *(in_hbm(x) for x in carried))
    packed, kept = results[:groups], results[groups:-2]
    off_rows, off_lanes = results[-2:]
    packed = [x.reshape(near, early, SUBLANES, LANES) for x in packed]
    arrived = [None] * groups
    arrived[0] = packed[0]
    for far in (3, 2, 1):
        arrived[far] = exchange(packed[far], far * near)

    applied = pl.pallas_call(
        functools.partial(apply_kernel, (fn_count, edge, plane_len, classes, shares, chunk, reach)),
        out_shape=block(classes, shares, units),
        in_specs=[vmem] * (1 + len(kept)) + [hbm],
        out_specs=vmem,
        scratch_shapes=[
            pltpu.VMEM((fn_count * edge, plane_len), jnp.bfloat16),
            pltpu.VMEM(cross.shape, jnp.bfloat16),
            pltpu.SemaphoreType.DMA((cross.shape[0],)),
        ],
        compiler_params=params,
        cost_estimate=cost(4608 * size, 8 * size),
        name="apply",
    )(off_rows, *kept, in_hbm(cross))
    held = lax.all_to_all(applied.reshape(devices, units, SUBLANES, LANES), axes, 0, 0, tiled=True)

    turned = pl.pallas_call(
        turn_kernel,
        out_shape=[block(groups, early)] * near,
        in_specs=[vmem] * groups,
        out_specs=[vmem] * near,
        compiler_params=params,
        cost_estimate=cost(0, 4 * size),
        name="turn",
    )(*arrived)
    gathered = [x if n == 0 else exchange(x, n) for n, x in enumerate(turned)]

    back_units = tiles + (tiles + 1) // 2 + 1
    made = pl.pallas_call(
        functools.partial(grid_kernel, (fn_count, edge, classes, shares, width, band_reach, sub_count)),
        out_shape=jax.ShapeDtypeStruct((devices, back_units, SUBLANES, LANES), jnp.bfloat16),
        in_specs=[vmem] * (near + 1),
        out_specs=vmem,
        scratch_shapes=[pltpu.VMEM((devices, early, SUBLANES, LANES), jnp.bfloat16)],
        compiler_params=params,
        name="grid",
    )(*gathered, held)
    back = lax.all_to_all(made, axes, 0, 0, tiled=True)
    back = back.reshape(classes, shares, back_units, SUBLANES, LANES)
    return pl.pallas_call(
        functools.partial(receive_kernel, (fn_count, edge, plane_len, classes, shares, band_reach, sub_count)),
        out_shape=(
            jax.ShapeDtypeStruct(psi.shape, jnp.bfloat16),
            jax.ShapeDtypeStruct((fn_count, width), jnp.float32),
            jax.ShapeDtypeStruct((fn_count, width), jnp.float32),
        ),
        in_specs=[vmem, vmem],
        out_specs=(hbm, vmem, vmem),
        scratch_shapes=[pltpu.VMEM(psi.shape, jnp.bfloat16), pltpu.SemaphoreType.DMA((shares,))],
        compiler_params=params,
        name="receive",
    )(off_lanes, back)


def any_shards(psi, potential, offsets, kernel, multipliers, pattern):
    devices = lax.axis_size("brick") * lax.axis_size("sub")
    plan = plan_of(devices, *psi.shape, kernel.shape[1])
    if plan is None:
        return shards(psi, potential, offsets, kernel, multipliers, pattern)
    return transposed_shards(*plan, psi, potential, offsets, kernel, multipliers, pattern)


def solution(mesh):
    in_specs = (
        P(("brick", "sub"), None, None),
        P(("brick", "sub"), None, None),
        P(("brick", "sub")),
        P(("brick", "sub"), None),
        P(("brick", "sub"), None),
        P(("brick", "sub"), None),
    )
    out_specs = (
        P(("brick", "sub"), None, None),
        P(("brick", "sub"), None),
        P(("brick", "sub"), None),
    )
    return jax.shard_map(any_shards, mesh=mesh, in_specs=in_specs, out_specs=out_specs, check_vma=False)
```

```python
import functools
import math

import jax
import jax.numpy as jnp
import numpy as np
from jax import lax
from jax.experimental import pallas as pl
from jax.experimental.pallas import tpu as pltpu
from jax.sharding import PartitionSpec as P

Q = 8
K = 6


filter_reach = 14


def shifted(block, axis, distance):
    devices = range(lax.axis_size(axis))
    route = [((i - distance) % len(devices), i) for i in devices]
    return lax.ppermute(block, axis, route)


def kinetic_matrix(edge_len):
    positions = jnp.arange(edge_len, dtype=jnp.int32)
    offset_gap = positions[:, None] - positions[None, :]
    distance = jnp.abs(offset_gap).astype(jnp.float32)
    parity_sign = 1.0 - 2.0 * (jnp.abs(offset_gap) % 2).astype(jnp.float32)
    off_diag = parity_sign / jnp.maximum(distance, 1.0) ** 2
    entries = jnp.where(offset_gap == 0, math.pi**2 / 6.0, off_diag)
    entries = jnp.where(jnp.abs(offset_gap) <= filter_reach, entries, 0.0)
    return entries.astype(jnp.bfloat16)


def cross_matrix(kinetic, edge_len):
    kin_float = kinetic.astype(jnp.float32)
    identity = jnp.eye(edge_len, dtype=jnp.float32)
    return (jnp.kron(kin_float, identity) + jnp.kron(identity, kin_float)).astype(jnp.bfloat16)


def apply_hamiltonian(psi, potential):
    fn_count, edge_len, plane_len = psi.shape
    kinetic = kinetic_matrix(edge_len)
    first_pass = jnp.einsum("wx,fxq->fwq", kinetic, psi, preferred_element_type=jnp.float32)
    cross = cross_matrix(kinetic, edge_len)
    second_pass = jnp.dot(
        psi.reshape(fn_count * edge_len, plane_len), cross, preferred_element_type=jnp.float32
    )
    summed = first_pass + second_pass.reshape(fn_count, edge_len, plane_len)
    result = summed + potential.astype(jnp.float32) * psi.astype(jnp.float32)
    return result.astype(jnp.bfloat16)


def embed(functions, region_start, window_len):

    def place(function, start_at):
        zeros_block = jnp.zeros((window_len, function.shape[1]), function.dtype)
        return lax.dynamic_update_slice_in_dim(zeros_block, function, start_at, 0)

    return jax.vmap(place)(functions, region_start)


def extract(window, region_start, edge_len):

    def take(planes, start_at):
        return lax.dynamic_slice_in_dim(planes, start_at, edge_len, 0)

    return jax.vmap(take)(window, region_start)


def dense_kernel(band_rows, group_count, band_reach, fn_count):
    dense_rows = []
    for slot_group in range(group_count):
        padded = jnp.pad(
            band_rows[slot_group], ((0, 0), (group_count * fn_count, group_count * fn_count))
        )
        first_col = (group_count + band_reach - slot_group) * fn_count
        dense_rows.append(padded[:, first_col : first_col + group_count * fn_count])
    return jnp.concatenate(dense_rows, axis=0)


def band_from_dense(dense, group_count, band_reach, fn_count):
    padded = jnp.pad(dense, ((0, 0), (band_reach * fn_count, band_reach * fn_count)))
    band_width = (2 * band_reach + 1) * fn_count
    pieces = []
    for slot_group in range(group_count):
        first_col = slot_group * fn_count
        pieces.append(padded[first_col : first_col + fn_count, first_col : first_col + band_width])
    return jnp.stack(pieces)


def grid_work(phi, hphi, kernel_rows, multi_rows, group_count, band_reach, fn_count, edge_len):
    volume_scale = 1.0 / float(edge_len**3)
    contract = (((1,), (1,)), ((), ()))
    margin = lax.dot_general(phi, phi, contract, preferred_element_type=jnp.float32) * volume_scale
    energy = lax.dot_general(phi, hphi, contract, preferred_element_type=jnp.float32) * volume_scale
    mixed = jnp.concatenate(
        [
            dense_kernel(kernel_rows, group_count, band_reach, fn_count),
            -dense_kernel(multi_rows, group_count, band_reach, fn_count),
        ],
        axis=1,
    )
    stacked = jnp.concatenate([hphi, phi], axis=0)
    grad = jnp.dot(mixed, stacked, preferred_element_type=jnp.float32).astype(jnp.bfloat16)
    margin_rows = band_from_dense(margin, group_count, band_reach, fn_count).astype(jnp.bfloat16)
    energy_rows = band_from_dense(energy, group_count, band_reach, fn_count).astype(jnp.bfloat16)
    return (grad, margin_rows, energy_rows)


def shards(psi, potential, offsets, kernel, multipliers, pattern):
    fn_count, edge_len, plane_len = psi.shape
    sub_count = lax.axis_size("sub")
    brick_count = lax.axis_size("brick")
    total_planes = Q * sub_count * brick_count
    band_reach = 2 * K
    band_width = kernel.shape[1]
    hpsi = apply_hamiltonian(psi, potential)
    spread = jnp.repeat(pattern, fn_count, axis=1).astype(jnp.bfloat16)
    kernel_eff = kernel * spread
    multi_eff = multipliers * spread
    margin_sum = jnp.zeros((fn_count, band_width), jnp.float32)
    energy_sum = jnp.zeros((fn_count, band_width), jnp.float32)
    my_rank = lax.axis_index("brick") * sub_count + lax.axis_index("sub")
    group_count = 2 * K + 1
    window_len = group_count * Q
    region_start = jnp.mod(offsets - (my_rank - K) * Q, total_planes)
    window_psi = embed(psi, region_start, window_len)
    window_hpsi = embed(hpsi, region_start, window_len)
    arrived = [None] * group_count
    for offset in range(-K, K + 1):
        first_plane = (offset + K) * Q
        payload = (
            window_psi[:, first_plane : first_plane + Q],
            window_hpsi[:, first_plane : first_plane + Q],
            kernel_eff,
            multi_eff,
        )
        if offset != 0:
            payload = shifted(
                (payload[0], payload[1], payload[2], payload[3]), ("brick", "sub"), offset
            )
        arrived[K - offset] = payload
    phi = jnp.concatenate([arrival[0] for arrival in arrived], axis=0).reshape(
        group_count * fn_count, Q * plane_len
    )
    hphi = jnp.concatenate([arrival[1] for arrival in arrived], axis=0).reshape(
        group_count * fn_count, Q * plane_len
    )
    kernel_rows = jnp.stack([arrival[2] for arrival in arrived])
    multi_rows = jnp.stack([arrival[3] for arrival in arrived])
    grad, margin_rows, energy_rows = grid_work(
        phi, hphi, kernel_rows, multi_rows, group_count, band_reach, fn_count, edge_len
    )
    grad = grad.reshape(group_count, fn_count, Q, plane_len)
    window = [None] * group_count
    for offset in range(-K, K + 1):
        slot_group = K - offset
        payload = (grad[slot_group], margin_rows[slot_group], energy_rows[slot_group])
        if offset != 0:
            payload = shifted((payload[0], payload[1], payload[2]), ("brick", "sub"), -offset)
        window[offset + K] = payload[0]
        margin_sum = margin_sum + payload[1].astype(jnp.float32)
        energy_sum = energy_sum + payload[2].astype(jnp.float32)
    gradient = extract(jnp.concatenate(window, axis=1), region_start, edge_len)
    return (gradient, margin_sum, energy_sum)


EARLY_PAIRS = 2
EARLY_TILES = 7
SUBLANES = 8
LANES = 128


def iota(shape, dim):
    return lax.broadcasted_iota(jnp.int32, shape, dim)


def plan_of(devices, fn_count, edge_len, plane_len, band_width):
    tiles = plane_len // LANES
    for shares in range(1, tiles + 1):
        if devices % shares or tiles % shares:
            continue
        classes = devices // shares
        per_class = edge_len // classes
        fits = (
            plane_len % (2 * LANES) == 0
            and edge_len % classes == 0
            and tiles // shares > 2 * EARLY_PAIRS
            and (devices * Q) % classes == 0
            and classes & (classes - 1) == 0
            and fn_count * 2 == SUBLANES
            and per_class == 3
            and edge_len % SUBLANES == 0
            and band_width + 2 <= LANES
            and devices * SUBLANES == 2 * LANES
            and band_width == (4 * K + 1) * fn_count
        )
        if fits:
            return classes, shares
    return None


def kinetic_numpy(edge_len):
    positions = np.arange(edge_len)
    gap = np.abs(positions[:, None] - positions[None, :])
    sign = 1.0 - 2.0 * (gap % 2)
    entries = sign / np.maximum(gap, 1).astype(np.float32) ** 2
    entries = np.where(gap == 0, np.float32(math.pi**2 / 6.0), entries)
    entries = np.where(gap <= filter_reach, entries, 0.0)
    return entries.astype(np.float32)


def cross_blocks(edge_len, chunk):
    line = kinetic_numpy(edge_len).astype(jnp.bfloat16).astype(np.float32)[0]
    period = math.lcm(edge_len, chunk)
    reach = -(-filter_reach * edge_len // chunk)
    stacks = []
    for first in range(0, period, chunk):
        row = np.arange(first - reach * chunk, first + (reach + 1) * chunk)[:, None]
        col = np.arange(first, first + chunk)[None, :]
        gap_y = np.abs(row // edge_len - col // edge_len)
        gap_z = np.abs(row % edge_len - col % edge_len)
        weight = np.where(np.arange(edge_len) <= filter_reach, line, 0.0)
        block = np.where(gap_z == 0, weight[np.minimum(gap_y, edge_len - 1)], 0.0)
        block = block + np.where(gap_y == 0, weight[gap_z], 0.0)
        stacks.append(block)
    return np.stack(stacks).astype(jnp.bfloat16), reach


def dot(a, b):
    return lax.dot_general(a, b, (((1,), (0,)), ((), ())), preferred_element_type=jnp.float32)


def dot_nt(a, b):
    return lax.dot_general(a, b, (((1,), (1,)), ((), ())), preferred_element_type=jnp.float32)


def in_hbm(array):
    return pltpu.with_memory_space_constraint(array, pltpu.HBM)


def pick(index, values):
    out = jnp.full(index.shape, values[0], jnp.int32)
    for k in range(1, len(values)):
        out = jnp.where(index == k, values[k], out)
    return out


def fetch(pairs, sems):
    copies = [pltpu.make_async_copy(source, target, sems.at[n]) for n, (source, target) in enumerate(pairs)]
    for copy in copies:
        copy.start()
    return copies


def class_select(target, off_rows, fn_count, edge, classes, least=0):
    shape = target.shape
    item, lane = iota(shape, 1), iota(shape, 2)
    member = item % fn_count
    depth = jnp.minimum(item // fn_count + least, 2)
    off_rows = jnp.concatenate([off_rows] * (shape[1] // SUBLANES), axis=0)[None]
    inner = jnp.bitwise_and(target - off_rows, classes - 1)
    source = member * edge + depth * classes + inner
    rows = fn_count * edge
    wide = [
        jnp.where(source == lane + k * LANES, 1.0, 0.0).astype(jnp.bfloat16)
        for k in range(-(-rows // LANES))
    ]
    return jnp.concatenate(wide, axis=2).reshape(shape[0] * shape[1], -1)[:, :rows]


def coefficient_rows(band, pattern, off_rows, fn_count):
    width, blocks = band.shape[1], pattern.shape[1]
    spread = jnp.where(
        iota((blocks, width), 1) // fn_count == iota((blocks, width), 0), 1.0, 0.0
    ).astype(jnp.bfloat16)
    small = band.astype(jnp.float32) * dot(pattern.astype(jnp.float32).astype(jnp.bfloat16), spread)
    small = jnp.concatenate([small, small], axis=0)
    small = jnp.concatenate([small, jnp.zeros((SUBLANES, LANES - width), jnp.float32)], axis=1)
    lane = iota((SUBLANES, LANES), 1)
    small = jnp.where(lane == width, jnp.right_shift(off_rows, 8).astype(jnp.float32), small)
    return jnp.where(lane == width + 1, jnp.bitwise_and(off_rows, 255).astype(jnp.float32), small)


def pair_units(deep, count, upper, last):
    made = []
    for t in range(0, count, 2):
        even = deep[..., t * LANES : (t + 1) * LANES]
        odd = deep[..., (t + 1) * LANES : (t + 2) * LANES] if t + 1 < count else last
        made.append(jnp.where(upper, even, odd).astype(jnp.bfloat16))
    return made


def pack_kernel(dims, offs_hbm, *refs):
    fn_count, edge, plane_len, classes, shares, groups, sub_count, carried = dims
    sources, outs, kept = refs[:carried], refs[carried : carried + groups], refs[carried + groups : -4]
    off_rows_ref, off_lanes_ref, offs_ref, sems = refs[-4:]
    copies = fetch(((offs_hbm, offs_ref), *zip(sources, kept)), sems)
    rows = fn_count * edge
    tiles = plane_len // LANES // shares
    near = classes // groups
    rank = lax.axis_index("brick") * sub_count + lax.axis_index("sub")
    mine = jnp.bitwise_and(rank, shares - 1)
    copies[0].wait()
    offs = [offs_ref[k] for k in range(fn_count)]
    off_rows = pick(iota((SUBLANES, LANES), 0) % fn_count, offs)
    off_rows_ref[...] = off_rows
    off_lanes_ref[...] = pick(iota((SUBLANES, LANES), 1) % fn_count, offs)
    target = jnp.bitwise_xor(iota((classes, SUBLANES, LANES), 0), rank // shares)
    select = class_select(target, off_rows, fn_count, edge, classes)
    deep = class_select(target, off_rows, fn_count, edge, classes, 2)
    upper = iota((near, SUBLANES, LANES), 1) < fn_count
    copies[1].wait()
    psi = kept[0][...].reshape(rows, plane_len)
    for share in range(shares):
        there = jnp.bitwise_xor(mine, share)
        ordered = dot(select, psi[:, share * tiles * LANES : (share + 1) * tiles * LANES])
        ordered = ordered.reshape(groups, near, SUBLANES, tiles * LANES)
        for k in range(groups):
            for t in range(tiles):
                outs[k][:, there, t] = ordered[k, :, :, t * LANES : (t + 1) * LANES].astype(jnp.bfloat16)
        start = share * tiles * LANES
        second = dot(deep, psi[:, start : start + 2 * EARLY_PAIRS * LANES])
        second = second.reshape(groups, near, SUBLANES, 2 * EARLY_PAIRS * LANES)
        for k in range(groups):
            for v, piece in enumerate(pair_units(second[k], 2 * EARLY_PAIRS, upper, None)):
                outs[k][:, there, tiles + v] = piece
    for copy in copies[2:]:
        copy.wait()


def apply_kernel(
    dims,
    off_rows_ref,
    psi_ref,
    pot_ref,
    kin_ref,
    kern_ref,
    mult_ref,
    patt_ref,
    cross_hbm,
    out_ref,
    result_ref,
    cross_ref,
    sems,
):
    fn_count, edge, plane_len, classes, shares, chunk, reach = dims
    copies = fetch([(cross_hbm.at[k], cross_ref.at[k]) for k in range(cross_ref.shape[0])], sems)
    rows = fn_count * edge
    tiles = plane_len // LANES // shares
    chunks = plane_len // chunk
    psi = psi_ref[...].reshape(rows, plane_len)
    pot = pot_ref[...].reshape(rows, plane_len)
    off_rows = off_rows_ref[...]
    shape = (classes, 2 * SUBLANES, LANES)
    select = class_select(iota(shape, 0), off_rows, fn_count, edge, classes)
    shape = (classes, SUBLANES, LANES)
    deep = class_select(iota(shape, 0), off_rows, fn_count, edge, classes, 2)
    patt = patt_ref[...]
    small = [coefficient_rows(ref[...], patt, off_rows, fn_count)[None] for ref in (mult_ref, kern_ref)]
    upper = iota(shape, 1) < fn_count
    led = dot(kin_ref[...], psi)
    for j in range(chunks):
        if j < len(copies):
            copies[j].wait()
        lo, hi = max(0, j - reach), min(chunks, j + reach + 1)
        here = slice(j * chunk, (j + 1) * chunk)
        acc = dot(
            psi[:, lo * chunk : hi * chunk],
            cross_ref[j % cross_ref.shape[0], (lo - j + reach) * chunk : (hi - j + reach) * chunk],
        )
        acc = acc + led[:, here]
        acc = acc + pot[:, here].astype(jnp.float32) * psi[:, here].astype(jnp.float32)
        result_ref[:, here] = acc.astype(jnp.bfloat16)
    ordered = dot(select, result_ref[...]).reshape(classes, 2, SUBLANES, plane_len)
    late = 2 * EARLY_PAIRS
    for share in range(shares):
        first, last = share * tiles * LANES, (share + 1) * tiles * LANES
        for t in range(tiles):
            at = slice(first + t * LANES, first + (t + 1) * LANES)
            out_ref[:, share, t] = ordered[:, 0, :, at].astype(jnp.bfloat16)
        rest = dot(deep, psi[:, first + late * LANES : last]).reshape(classes, SUBLANES, -1)
        made = pair_units(ordered[:, 1, :, first:last], tiles, upper, small[0])
        made += pair_units(rest, tiles - late, upper, small[1])
        for v, piece in enumerate(made):
            out_ref[:, share, tiles + v] = piece


def turn_kernel(*refs):
    groups = len(refs) - refs[0].shape[0]
    arrived, outs = refs[:groups], refs[groups:]
    for near, out in enumerate(outs):
        for far in range(groups):
            out[far] = arrived[far][near]


def grid_rows(psi_all, h_ref, tiles, fn_count, wanted):
    devices = h_ref.shape[0]
    full = devices * SUBLANES
    pairs = (tiles + 1) // 2
    upper = iota((devices, SUBLANES, LANES), 1) < fn_count
    both = {}
    for v in range(pairs):
        if 2 * v not in wanted and 2 * v + 1 not in wanted:
            continue
        ours = psi_all[:, tiles + v] if v < EARLY_PAIRS else h_ref[:, tiles + pairs + v - EARLY_PAIRS]
        ours, theirs = ours.astype(jnp.float32), h_ref[:, tiles + v].astype(jnp.float32)
        both[2 * v] = jnp.where(upper, ours, pltpu.roll(theirs, fn_count, axis=1))
        both[2 * v + 1] = jnp.where(upper, pltpu.roll(ours, fn_count, axis=1), theirs)
    inside = [t for t in wanted if t < tiles]
    stacked = [
        jnp.concatenate([psi_all[:, t].reshape(full, LANES) for t in inside], axis=1),
        jnp.concatenate([both[t].reshape(full, LANES).astype(jnp.bfloat16) for t in inside], axis=1),
        jnp.concatenate([h_ref[:, t].reshape(full, LANES) for t in inside], axis=1),
    ]
    return stacked, both


def same_plane(gap, planes, row_depth, fn_count):
    half_col = jnp.bitwise_and(iota(gap.shape, 1) // fn_count, 1)
    return [
        jnp.bitwise_and(gap + row_depth - depth, planes - 1) == 0 for depth in (half_col, 2, half_col)
    ]


def masked(masks, plus, minus, fn_count):
    half_col = jnp.bitwise_and(iota(plus.shape, 1) // fn_count, 1)
    coef = (minus, jnp.where(half_col == 0, minus, plus), plus)
    return jnp.concatenate(
        [jnp.where(k, c, 0.0).astype(jnp.bfloat16) for k, c in zip(masks, coef)], axis=1
    )


def first_kernel(dims, *refs):
    fn_count, _, classes, shares, width, band_reach, sub_count, groups = dims
    near = len(refs) - groups - 7
    psi_refs, h_ref, outs = refs[:near], refs[near], refs[near + 1 : near + 1 + groups]
    psi_all, low_ref, plus_ref, minus_ref, gap_ref, grad_ref = refs[near + 1 + groups :]
    tiles = psi_refs[0].shape[1] - EARLY_PAIRS
    devices = h_ref.shape[0]
    full = devices * SUBLANES
    rank = lax.axis_index("brick") * sub_count + lax.axis_index("sub")
    my_class = rank // shares
    classes_bits = classes.bit_length() - 1
    for n, ref in enumerate(psi_refs):
        for far in range(groups):
            psi_all[jnp.bitwise_xor(rank, far * near + n)] = ref[far]

    stacked, both = grid_rows(psi_all, h_ref, tiles, fn_count, (*range(EARLY_TILES), tiles))
    halves = both[tiles]
    flat = halves.reshape(full, LANES).astype(jnp.bfloat16)
    lane_a, lane_b = iota((LANES, full), 0), iota((full, LANES), 1)
    weigh_a = jnp.where(lane_a == width, 256.0, jnp.where(lane_a == width + 1, 1.0, 0.0))
    weigh_b = jnp.where(lane_b == width, 256.0, jnp.where(lane_b == width + 1, 1.0, 0.0))
    off_row = dot(flat, weigh_a.astype(jnp.bfloat16)).astype(jnp.int32)
    off_col = dot_nt(weigh_b.astype(jnp.bfloat16), flat).astype(jnp.int32)

    def first_plane(off):
        inner = jnp.bitwise_and(my_class - off, classes - 1)
        return jnp.right_shift(off + inner - my_class, classes_bits)

    gap = first_plane(off_row) - first_plane(off_col)
    gap_ref[...] = gap

    turned = pltpu.roll(halves, fn_count, axis=1)
    upper = iota(halves.shape, 1) < fn_count
    column = iota((LANES, full), 1)
    column = column // SUBLANES * fn_count + column % fn_count
    expand = jnp.where((lane_a == column) & (lane_a < width), 1.0, 0.0).astype(jnp.bfloat16)

    def dense(rows):
        wide = dot(rows.reshape(full, LANES).astype(jnp.bfloat16), expand)
        turned_rows = []
        for owner in range(devices):
            shift = (owner - band_reach) * SUBLANES % full
            block = wide[owner * SUBLANES : (owner + 1) * SUBLANES]
            turned_rows.append(pltpu.roll(block, shift, axis=1) if shift else block)
        return jnp.concatenate(turned_rows, axis=0)

    plus = dense(jnp.where(upper, halves, turned))
    minus = -dense(jnp.where(upper, turned, halves))
    plus_ref[...] = plus
    minus_ref[...] = minus
    half_row = jnp.bitwise_and(iota((full, full), 0) // fn_count, 1)
    low = masked(same_plane(gap, devices * Q // classes, half_row, fn_count), plus, minus, fn_count)
    low_ref[...] = low
    grad = dot(low, jnp.concatenate(stacked, axis=0))
    for t in range(EARLY_TILES):
        piece = grad[:, t * LANES : (t + 1) * LANES].reshape(devices, SUBLANES, LANES)
        grad_ref[:, t] = piece.astype(jnp.bfloat16)
    for far in range(groups):
        for n in range(near):
            outs[far][n] = grad_ref[jnp.bitwise_xor(rank, far * near + n)]


def second_kernel(dims, psi_all, h_ref, low_ref, plus_ref, minus_ref, gap_ref, out_ref):
    fn_count, edge, classes = dims
    tiles = psi_all.shape[1] - EARLY_PAIRS
    devices = h_ref.shape[0]
    full = devices * SUBLANES
    planes = devices * Q // classes
    pairs = (tiles + 1) // 2
    stacked, _ = grid_rows(psi_all, h_ref, tiles, fn_count, range(tiles))
    gap = gap_ref[...]
    half_row = jnp.bitwise_and(iota((full, full), 0) // fn_count, 1)
    low = same_plane(gap, planes, half_row, fn_count)
    top = same_plane(gap, planes, 2, fn_count)
    rows = jnp.concatenate(stacked, axis=0)
    rest = dot(low_ref[...], rows[:, EARLY_TILES * LANES :])
    for t in range(tiles - EARLY_TILES):
        piece = rest[:, t * LANES : (t + 1) * LANES].reshape(devices, SUBLANES, LANES)
        out_ref[:, t] = piece.astype(jnp.bfloat16)
    upper = iota((devices, SUBLANES, LANES), 1) < fn_count
    second = dot(masked(top, plus_ref[...], minus_ref[...], fn_count), rows)
    second = second.reshape(devices, SUBLANES, tiles * LANES)
    for v, piece in enumerate(pair_units(second, tiles, upper, 0.0)):
        out_ref[:, tiles - EARLY_TILES + v] = piece

    sums = []
    for part in range(3):
        low_gram = jnp.where(low[part], dot_nt(stacked[0], stacked[part]), 0.0)
        top_gram = dot_nt(stacked[1], stacked[part])
        top_gram = jnp.where(top[part] & (half_row == 0), top_gram, 0.0)
        total = (low_gram + top_gram).reshape(devices, SUBLANES, full)
        sums.append(total + pltpu.roll(total, fn_count, axis=1))
    first = sums[0] + pltpu.roll(sums[0], full - fn_count, axis=2)
    third = sums[2] + pltpu.roll(sums[2], fn_count, axis=2)
    lanes_half = jnp.bitwise_and(iota((devices, SUBLANES, full), 2) // fn_count, 1)
    bands = sums[1] + jnp.where(lanes_half == 0, first, third)
    bands = jnp.where(upper, bands[:, :, :LANES], bands[:, :, LANES:])
    bands = bands * (1.0 / float(edge**3))
    out_ref[:, tiles - EARLY_TILES + pairs] = bands.astype(jnp.bfloat16)


def receive_kernel(dims, off_lanes_ref, in_ref, *refs):
    fn_count, edge, plane_len, classes, shares, band_reach, sub_count, near = dims
    early_refs, (grad_hbm, margin_ref, energy_ref, grad_ref, early_ref, sems) = refs[:near], refs[near:]
    tiles = plane_len // LANES // shares
    rows = fn_count * edge
    devices = classes * shares
    width = margin_ref.shape[1]
    rank = lax.axis_index("brick") * sub_count + lax.axis_index("sub")
    inner = classes * SUBLANES
    for n, ref in enumerate(early_refs):
        for far in range(ref.shape[0]):
            source = jnp.bitwise_xor(rank, far * near + n)
            early_ref[source // shares, jnp.bitwise_and(source, shares - 1)] = ref[far]
    pair_at = tiles - EARLY_TILES

    shape = (fn_count, edge, inner)
    member, plane = iota(shape, 0), iota(shape, 1)
    slot = iota(shape, 2)
    cls, sub = slot // SUBLANES, slot % SUBLANES
    half, owner_fn = sub // fn_count, sub % fn_count
    off_lanes = jnp.concatenate([off_lanes_ref[...]] * (inner // LANES), axis=1)[:1, None]
    at = jnp.bitwise_and(cls - off_lanes, classes - 1)
    same = owner_fn == member
    low = jnp.where(same & (plane == at + half * classes), 1.0, 0.0).astype(jnp.bfloat16)
    top = same & (plane == at + 2 * classes)
    place = []
    for parity in range(2):
        tops = jnp.where(top & (half == parity), 1.0, 0.0).astype(jnp.bfloat16)
        place.append(jnp.concatenate([low, tops], axis=2).reshape(rows, 2 * inner))
    copies = []
    for share in range(shares):
        for parity in range(2):
            columns = [
                jnp.concatenate(
                    [
                        (
                            early_ref[:, share, t] if t < EARLY_TILES else in_ref[:, share, t - EARLY_TILES]
                        ).reshape(inner, LANES),
                        in_ref[:, share, pair_at + t // 2].reshape(inner, LANES),
                    ],
                    axis=0,
                )
                for t in range(parity, tiles, 2)
            ]
            placed = dot(place[parity], jnp.concatenate(columns, axis=1)).astype(jnp.bfloat16)
            for n, t in enumerate(range(parity, tiles, 2)):
                spot = (share * tiles + t) * LANES
                grad_ref[:, :, spot : spot + LANES] = placed[:, n * LANES : (n + 1) * LANES].reshape(
                    fn_count, edge, LANES
                )
        part = pl.ds(share * tiles * LANES, tiles * LANES)
        copies.append(
            pltpu.make_async_copy(grad_ref.at[:, :, part], grad_hbm.at[:, :, part], sems.at[share])
        )
        copies[-1].start()

    total = jnp.sum(
        in_ref[:, :, pair_at + (tiles + 1) // 2].reshape(devices, SUBLANES, LANES).astype(jnp.float32), axis=0
    )
    terms = []
    for _ in range(3):
        terms.append(total.astype(jnp.bfloat16))
        total = total - terms[-1].astype(jnp.float32)
    terms = jnp.concatenate(terms + terms[-1:], axis=0)
    lane, col = iota((LANES, LANES), 0), iota((LANES, LANES), 1)
    partner = lax.rem(rank + col // fn_count - band_reach + devices, devices)
    for kind, ref in ((0, margin_ref), (1, energy_ref)):
        wanted = partner * SUBLANES + kind * fn_count + col % fn_count
        row = jnp.zeros((fn_count, LANES), jnp.float32)
        for part in range(2):
            picked = dot(terms, jnp.where(wanted == lane + part * LANES, 1.0, 0.0).astype(jnp.bfloat16))
            for n in range(3):
                first = n * SUBLANES + part * fn_count
                row = row + picked[first : first + fn_count]
        ref[...] = row[:, :width]
    for copy in copies:
        copy.wait()


def transposed_shards(classes, shares, psi, potential, offsets, kernel, multipliers, pattern):
    fn_count, edge, plane_len = psi.shape
    sub_count = lax.axis_size("sub")
    devices = sub_count * lax.axis_size("brick")
    width = kernel.shape[1]
    tiles = plane_len // LANES // shares
    band_reach = 2 * K
    chunk = 2 * LANES
    params = pltpu.CompilerParams(vmem_limit_bytes=20 * 2**20)
    vmem = pl.BlockSpec(memory_space=pltpu.VMEM)

    hbm = pl.BlockSpec(memory_space=pltpu.HBM)
    groups = 4
    near = devices // groups
    kinetic = np.kron(np.eye(fn_count, dtype=np.float32), kinetic_numpy(edge)).astype(jnp.bfloat16)
    cross, reach = cross_blocks(edge, chunk)
    early = tiles + EARLY_PAIRS
    units = tiles + (tiles + 1) // 2 * 2 - EARLY_PAIRS
    offsets = in_hbm(offsets)

    def block(*lead):
        return jax.ShapeDtypeStruct((*lead, SUBLANES, LANES), jnp.bfloat16)

    def cost(flops, moved):
        return pl.CostEstimate(flops=flops, bytes_accessed=moved, transcendentals=0)

    def exchange(array, bits):
        return lax.ppermute(array, axes, [(i, i ^ bits) for i in range(devices)])

    axes = ("brick", "sub")
    size = psi.size
    kinetic, cross = jnp.asarray(kinetic), jnp.asarray(cross)
    carried = (psi, potential, kinetic, kernel, multipliers, pattern)
    results = pl.pallas_call(
        functools.partial(
            pack_kernel, (fn_count, edge, plane_len, classes, shares, groups, sub_count, len(carried))
        ),
        out_shape=[block(near // shares, shares, early)] * groups
        + [jax.ShapeDtypeStruct(x.shape, x.dtype) for x in carried]
        + [jax.ShapeDtypeStruct((SUBLANES, LANES), jnp.int32)] * 2,
        in_specs=[hbm] * (1 + len(carried)),
        out_specs=[vmem] * (groups + len(carried) + 2),
        scratch_shapes=[
            pltpu.SMEM(offsets.shape, offsets.dtype),
            pltpu.SemaphoreType.DMA((1 + len(carried),)),
        ],
        compiler_params=params,
        cost_estimate=cost(512 * size, 4 * size),
        name="pack",
    )(offsets, *(in_hbm(x) for x in carried))
    packed, kept = results[:groups], results[groups:-2]
    off_rows, off_lanes = results[-2:]
    packed = [x.reshape(near, early, SUBLANES, LANES) for x in packed]
    arrived = [None] * groups
    arrived[0] = packed[0]
    for far in (3, 2, 1):
        arrived[far] = exchange(packed[far], far * near)

    applied = pl.pallas_call(
        functools.partial(apply_kernel, (fn_count, edge, plane_len, classes, shares, chunk, reach)),
        out_shape=block(classes, shares, units),
        in_specs=[vmem] * (1 + len(kept)) + [hbm],
        out_specs=vmem,
        scratch_shapes=[
            pltpu.VMEM((fn_count * edge, plane_len), jnp.bfloat16),
            pltpu.VMEM(cross.shape, jnp.bfloat16),
            pltpu.SemaphoreType.DMA((cross.shape[0],)),
        ],
        compiler_params=params,
        cost_estimate=cost(4608 * size, 8 * size),
        name="apply",
    )(off_rows, *kept, in_hbm(cross))
    held = lax.all_to_all(applied.reshape(devices, units, SUBLANES, LANES), axes, 0, 0, tiled=True)

    turned = pl.pallas_call(
        turn_kernel,
        out_shape=[block(groups, early)] * near,
        in_specs=[vmem] * groups,
        out_specs=[vmem] * near,
        compiler_params=params,
        cost_estimate=cost(0, 4 * size),
        name="turn",
    )(*arrived)
    gathered = [x if n == 0 else exchange(x, n) for n, x in enumerate(turned)]

    full = devices * SUBLANES
    results = pl.pallas_call(
        functools.partial(
            first_kernel, (fn_count, edge, classes, shares, width, band_reach, sub_count, groups)
        ),
        out_shape=[block(near, EARLY_TILES)] * groups
        + [
            block(devices, early),
            jax.ShapeDtypeStruct((full, 3 * full), jnp.bfloat16),
            jax.ShapeDtypeStruct((full, full), jnp.float32),
            jax.ShapeDtypeStruct((full, full), jnp.float32),
            jax.ShapeDtypeStruct((full, full), jnp.int32),
        ],
        in_specs=[vmem] * (near + 1),
        out_specs=[vmem] * (groups + 5),
        scratch_shapes=[pltpu.VMEM((devices, EARLY_TILES, SUBLANES, LANES), jnp.bfloat16)],
        compiler_params=params,
        cost_estimate=cost(1024 * size, 4 * size),
        name="first",
    )(*gathered, held)
    leaving, tables = results[:groups], results[groups:]
    returned = [leaving[0]] + [None] * (groups - 1)
    for far in (3, 2, 1):
        returned[far] = exchange(leaving[far], far * near)

    back_units = tiles - EARLY_TILES + (tiles + 1) // 2 + 1
    made = pl.pallas_call(
        functools.partial(second_kernel, (fn_count, edge, classes)),
        out_shape=block(devices, back_units),
        in_specs=[vmem] * 6,
        out_specs=vmem,
        compiler_params=params,
        cost_estimate=cost(2048 * size, 4 * size),
        name="second",
    )(tables[0], held, *tables[1:])
    back = lax.all_to_all(made, axes, 0, 0, tiled=True)
    back = back.reshape(classes, shares, back_units, SUBLANES, LANES)
    spread = pl.pallas_call(
        turn_kernel,
        out_shape=[block(groups, EARLY_TILES)] * near,
        in_specs=[vmem] * groups,
        out_specs=[vmem] * near,
        compiler_params=params,
        cost_estimate=cost(0, 4 * size),
        name="spread",
    )(*returned)
    homed = [x if n == 0 else exchange(x, n) for n, x in enumerate(spread)]
    return pl.pallas_call(
        functools.partial(
            receive_kernel, (fn_count, edge, plane_len, classes, shares, band_reach, sub_count, near)
        ),
        out_shape=(
            jax.ShapeDtypeStruct(psi.shape, jnp.bfloat16),
            jax.ShapeDtypeStruct((fn_count, width), jnp.float32),
            jax.ShapeDtypeStruct((fn_count, width), jnp.float32),
        ),
        in_specs=[vmem] * (2 + near),
        out_specs=(hbm, vmem, vmem),
        scratch_shapes=[
            pltpu.VMEM(psi.shape, jnp.bfloat16),
            pltpu.VMEM((classes, shares, EARLY_TILES, SUBLANES, LANES), jnp.bfloat16),
            pltpu.SemaphoreType.DMA((shares,)),
        ],
        compiler_params=params,
        name="receive",
    )(off_lanes, back, *homed)


def any_shards(psi, potential, offsets, kernel, multipliers, pattern):
    devices = lax.axis_size("brick") * lax.axis_size("sub")
    plan = plan_of(devices, *psi.shape, kernel.shape[1])
    if plan is None:
        return shards(psi, potential, offsets, kernel, multipliers, pattern)
    return transposed_shards(*plan, psi, potential, offsets, kernel, multipliers, pattern)


def solution(mesh):
    in_specs = (
        P(("brick", "sub"), None, None),
        P(("brick", "sub"), None, None),
        P(("brick", "sub")),
        P(("brick", "sub"), None),
        P(("brick", "sub"), None),
        P(("brick", "sub"), None),
    )
    out_specs = (
        P(("brick", "sub"), None, None),
        P(("brick", "sub"), None),
        P(("brick", "sub"), None),
    )
    return jax.shard_map(any_shards, mesh=mesh, in_specs=in_specs, out_specs=out_specs, check_vma=False)
```

```python
import functools
import math

import jax
import jax.numpy as jnp
import numpy as np
from jax import lax
from jax.experimental import pallas as pl
from jax.experimental.pallas import tpu as pltpu
from jax.sharding import PartitionSpec as P

Q = 8
K = 6


filter_reach = 14


def shifted(block, axis, distance):
    devices = range(lax.axis_size(axis))
    route = [((i - distance) % len(devices), i) for i in devices]
    return lax.ppermute(block, axis, route)


def kinetic_matrix(edge_len):
    positions = jnp.arange(edge_len, dtype=jnp.int32)
    offset_gap = positions[:, None] - positions[None, :]
    distance = jnp.abs(offset_gap).astype(jnp.float32)
    parity_sign = 1.0 - 2.0 * (jnp.abs(offset_gap) % 2).astype(jnp.float32)
    off_diag = parity_sign / jnp.maximum(distance, 1.0) ** 2
    entries = jnp.where(offset_gap == 0, math.pi**2 / 6.0, off_diag)
    entries = jnp.where(jnp.abs(offset_gap) <= filter_reach, entries, 0.0)
    return entries.astype(jnp.bfloat16)


def cross_matrix(kinetic, edge_len):
    kin_float = kinetic.astype(jnp.float32)
    identity = jnp.eye(edge_len, dtype=jnp.float32)
    return (jnp.kron(kin_float, identity) + jnp.kron(identity, kin_float)).astype(jnp.bfloat16)


def apply_hamiltonian(psi, potential):
    fn_count, edge_len, plane_len = psi.shape
    kinetic = kinetic_matrix(edge_len)
    first_pass = jnp.einsum("wx,fxq->fwq", kinetic, psi, preferred_element_type=jnp.float32)
    cross = cross_matrix(kinetic, edge_len)
    second_pass = jnp.dot(
        psi.reshape(fn_count * edge_len, plane_len), cross, preferred_element_type=jnp.float32
    )
    summed = first_pass + second_pass.reshape(fn_count, edge_len, plane_len)
    result = summed + potential.astype(jnp.float32) * psi.astype(jnp.float32)
    return result.astype(jnp.bfloat16)


def embed(functions, region_start, window_len):

    def place(function, start_at):
        zeros_block = jnp.zeros((window_len, function.shape[1]), function.dtype)
        return lax.dynamic_update_slice_in_dim(zeros_block, function, start_at, 0)

    return jax.vmap(place)(functions, region_start)


def extract(window, region_start, edge_len):

    def take(planes, start_at):
        return lax.dynamic_slice_in_dim(planes, start_at, edge_len, 0)

    return jax.vmap(take)(window, region_start)


def dense_kernel(band_rows, group_count, band_reach, fn_count):
    dense_rows = []
    for slot_group in range(group_count):
        padded = jnp.pad(
            band_rows[slot_group], ((0, 0), (group_count * fn_count, group_count * fn_count))
        )
        first_col = (group_count + band_reach - slot_group) * fn_count
        dense_rows.append(padded[:, first_col : first_col + group_count * fn_count])
    return jnp.concatenate(dense_rows, axis=0)


def band_from_dense(dense, group_count, band_reach, fn_count):
    padded = jnp.pad(dense, ((0, 0), (band_reach * fn_count, band_reach * fn_count)))
    band_width = (2 * band_reach + 1) * fn_count
    pieces = []
    for slot_group in range(group_count):
        first_col = slot_group * fn_count
        pieces.append(padded[first_col : first_col + fn_count, first_col : first_col + band_width])
    return jnp.stack(pieces)


def grid_work(phi, hphi, kernel_rows, multi_rows, group_count, band_reach, fn_count, edge_len):
    volume_scale = 1.0 / float(edge_len**3)
    contract = (((1,), (1,)), ((), ()))
    margin = lax.dot_general(phi, phi, contract, preferred_element_type=jnp.float32) * volume_scale
    energy = lax.dot_general(phi, hphi, contract, preferred_element_type=jnp.float32) * volume_scale
    mixed = jnp.concatenate(
        [
            dense_kernel(kernel_rows, group_count, band_reach, fn_count),
            -dense_kernel(multi_rows, group_count, band_reach, fn_count),
        ],
        axis=1,
    )
    stacked = jnp.concatenate([hphi, phi], axis=0)
    grad = jnp.dot(mixed, stacked, preferred_element_type=jnp.float32).astype(jnp.bfloat16)
    margin_rows = band_from_dense(margin, group_count, band_reach, fn_count).astype(jnp.bfloat16)
    energy_rows = band_from_dense(energy, group_count, band_reach, fn_count).astype(jnp.bfloat16)
    return (grad, margin_rows, energy_rows)


def shards(psi, potential, offsets, kernel, multipliers, pattern):
    fn_count, edge_len, plane_len = psi.shape
    sub_count = lax.axis_size("sub")
    brick_count = lax.axis_size("brick")
    total_planes = Q * sub_count * brick_count
    band_reach = 2 * K
    band_width = kernel.shape[1]
    hpsi = apply_hamiltonian(psi, potential)
    spread = jnp.repeat(pattern, fn_count, axis=1).astype(jnp.bfloat16)
    kernel_eff = kernel * spread
    multi_eff = multipliers * spread
    margin_sum = jnp.zeros((fn_count, band_width), jnp.float32)
    energy_sum = jnp.zeros((fn_count, band_width), jnp.float32)
    my_rank = lax.axis_index("brick") * sub_count + lax.axis_index("sub")
    group_count = 2 * K + 1
    window_len = group_count * Q
    region_start = jnp.mod(offsets - (my_rank - K) * Q, total_planes)
    window_psi = embed(psi, region_start, window_len)
    window_hpsi = embed(hpsi, region_start, window_len)
    arrived = [None] * group_count
    for offset in range(-K, K + 1):
        first_plane = (offset + K) * Q
        payload = (
            window_psi[:, first_plane : first_plane + Q],
            window_hpsi[:, first_plane : first_plane + Q],
            kernel_eff,
            multi_eff,
        )
        if offset != 0:
            payload = shifted(
                (payload[0], payload[1], payload[2], payload[3]), ("brick", "sub"), offset
            )
        arrived[K - offset] = payload
    phi = jnp.concatenate([arrival[0] for arrival in arrived], axis=0).reshape(
        group_count * fn_count, Q * plane_len
    )
    hphi = jnp.concatenate([arrival[1] for arrival in arrived], axis=0).reshape(
        group_count * fn_count, Q * plane_len
    )
    kernel_rows = jnp.stack([arrival[2] for arrival in arrived])
    multi_rows = jnp.stack([arrival[3] for arrival in arrived])
    grad, margin_rows, energy_rows = grid_work(
        phi, hphi, kernel_rows, multi_rows, group_count, band_reach, fn_count, edge_len
    )
    grad = grad.reshape(group_count, fn_count, Q, plane_len)
    window = [None] * group_count
    for offset in range(-K, K + 1):
        slot_group = K - offset
        payload = (grad[slot_group], margin_rows[slot_group], energy_rows[slot_group])
        if offset != 0:
            payload = shifted((payload[0], payload[1], payload[2]), ("brick", "sub"), -offset)
        window[offset + K] = payload[0]
        margin_sum = margin_sum + payload[1].astype(jnp.float32)
        energy_sum = energy_sum + payload[2].astype(jnp.float32)
    gradient = extract(jnp.concatenate(window, axis=1), region_start, edge_len)
    return (gradient, margin_sum, energy_sum)


EARLY_PAIRS = 2
EARLY_TILES = 7
SUBLANES = 8
LANES = 128


def iota(shape, dim):
    return lax.broadcasted_iota(jnp.int32, shape, dim)


def plan_of(devices, fn_count, edge_len, plane_len, band_width):
    tiles = plane_len // LANES
    for shares in range(1, tiles + 1):
        if devices % shares or tiles % shares:
            continue
        classes = devices // shares
        per_class = edge_len // classes
        fits = (
            plane_len % (2 * LANES) == 0
            and edge_len % classes == 0
            and tiles // shares > 2 * EARLY_PAIRS
            and (devices * Q) % classes == 0
            and classes & (classes - 1) == 0
            and fn_count * 2 == SUBLANES
            and per_class == 3
            and edge_len % SUBLANES == 0
            and band_width + 2 <= LANES
            and devices * SUBLANES == 2 * LANES
            and band_width == (4 * K + 1) * fn_count
        )
        if fits:
            return classes, shares
    return None


def kinetic_numpy(edge_len):
    positions = np.arange(edge_len)
    gap = np.abs(positions[:, None] - positions[None, :])
    sign = 1.0 - 2.0 * (gap % 2)
    entries = sign / np.maximum(gap, 1).astype(np.float32) ** 2
    entries = np.where(gap == 0, np.float32(math.pi**2 / 6.0), entries)
    entries = np.where(gap <= filter_reach, entries, 0.0)
    return entries.astype(np.float32)


def cross_blocks(edge_len, chunk):
    line = kinetic_numpy(edge_len).astype(jnp.bfloat16).astype(np.float32)[0]
    period = math.lcm(edge_len, chunk)
    reach = -(-filter_reach * edge_len // chunk)
    stacks = []
    for first in range(0, period, chunk):
        row = np.arange(first - reach * chunk, first + (reach + 1) * chunk)[:, None]
        col = np.arange(first, first + chunk)[None, :]
        gap_y = np.abs(row // edge_len - col // edge_len)
        gap_z = np.abs(row % edge_len - col % edge_len)
        weight = np.where(np.arange(edge_len) <= filter_reach, line, 0.0)
        block = np.where(gap_z == 0, weight[np.minimum(gap_y, edge_len - 1)], 0.0)
        block = block + np.where(gap_y == 0, weight[gap_z], 0.0)
        stacks.append(block)
    return np.stack(stacks).astype(jnp.bfloat16), reach


def dot(a, b):
    return lax.dot_general(a, b, (((1,), (0,)), ((), ())), preferred_element_type=jnp.float32)


def dot_nt(a, b):
    return lax.dot_general(a, b, (((1,), (1,)), ((), ())), preferred_element_type=jnp.float32)


def in_hbm(array):
    return pltpu.with_memory_space_constraint(array, pltpu.HBM)


def pick(index, values):
    out = jnp.full(index.shape, values[0], jnp.int32)
    for k in range(1, len(values)):
        out = jnp.where(index == k, values[k], out)
    return out


def fetch(pairs, sems):
    copies = [pltpu.make_async_copy(source, target, sems.at[n]) for n, (source, target) in enumerate(pairs)]
    for copy in copies:
        copy.start()
    return copies


def class_select(target, off_rows, fn_count, edge, classes, least=0):
    shape = target.shape
    item, lane = iota(shape, 1), iota(shape, 2)
    member = item % fn_count
    depth = jnp.minimum(item // fn_count + least, 2)
    off_rows = jnp.concatenate([off_rows] * (shape[1] // SUBLANES), axis=0)[None]
    inner = jnp.bitwise_and(target - off_rows, classes - 1)
    source = member * edge + depth * classes + inner
    rows = fn_count * edge
    wide = [
        jnp.where(source == lane + k * LANES, 1.0, 0.0).astype(jnp.bfloat16)
        for k in range(-(-rows // LANES))
    ]
    return jnp.concatenate(wide, axis=2).reshape(shape[0] * shape[1], -1)[:, :rows]


def coefficient_rows(band, pattern, off_rows, fn_count):
    width, blocks = band.shape[1], pattern.shape[1]
    spread = jnp.where(
        iota((blocks, width), 1) // fn_count == iota((blocks, width), 0), 1.0, 0.0
    ).astype(jnp.bfloat16)
    small = band.astype(jnp.float32) * dot(pattern.astype(jnp.float32).astype(jnp.bfloat16), spread)
    small = jnp.concatenate([small, small], axis=0)
    small = jnp.concatenate([small, jnp.zeros((SUBLANES, LANES - width), jnp.float32)], axis=1)
    lane = iota((SUBLANES, LANES), 1)
    small = jnp.where(lane == width, jnp.right_shift(off_rows, 8).astype(jnp.float32), small)
    return jnp.where(lane == width + 1, jnp.bitwise_and(off_rows, 255).astype(jnp.float32), small)


def pair_units(deep, count, upper, last):
    made = []
    for t in range(0, count, 2):
        even = deep[..., t * LANES : (t + 1) * LANES]
        odd = deep[..., (t + 1) * LANES : (t + 2) * LANES] if t + 1 < count else last
        made.append(jnp.where(upper, even, odd).astype(jnp.bfloat16))
    return made


def pack_kernel(dims, offs_hbm, *refs):
    fn_count, edge, plane_len, classes, shares, groups, sub_count, carried = dims
    sources, outs, kept = refs[:carried], refs[carried : carried + groups], refs[carried + groups : -4]
    off_rows_ref, off_lanes_ref, offs_ref, sems = refs[-4:]
    copies = fetch(((offs_hbm, offs_ref), *zip(sources, kept)), sems)
    rows = fn_count * edge
    tiles = plane_len // LANES // shares
    near = classes // groups
    rank = lax.axis_index("brick") * sub_count + lax.axis_index("sub")
    mine = jnp.bitwise_and(rank, shares - 1)
    copies[0].wait()
    offs = [offs_ref[k] for k in range(fn_count)]
    off_rows = pick(iota((SUBLANES, LANES), 0) % fn_count, offs)
    off_rows_ref[...] = off_rows
    off_lanes_ref[...] = pick(iota((SUBLANES, LANES), 1) % fn_count, offs)
    target = jnp.bitwise_xor(iota((classes, SUBLANES, LANES), 0), rank // shares)
    select = class_select(target, off_rows, fn_count, edge, classes)
    deep = class_select(target, off_rows, fn_count, edge, classes, 2)
    upper = iota((near, SUBLANES, LANES), 1) < fn_count
    copies[1].wait()
    psi = kept[0][...].reshape(rows, plane_len)
    for share in range(shares):
        there = jnp.bitwise_xor(mine, share)
        ordered = dot(select, psi[:, share * tiles * LANES : (share + 1) * tiles * LANES])
        ordered = ordered.reshape(groups, near, SUBLANES, tiles * LANES)
        for k in range(groups):
            for t in range(tiles):
                outs[k][:, there, t] = ordered[k, :, :, t * LANES : (t + 1) * LANES].astype(jnp.bfloat16)
        start = share * tiles * LANES
        second = dot(deep, psi[:, start : start + 2 * EARLY_PAIRS * LANES])
        second = second.reshape(groups, near, SUBLANES, 2 * EARLY_PAIRS * LANES)
        for k in range(groups):
            for v, piece in enumerate(pair_units(second[k], 2 * EARLY_PAIRS, upper, None)):
                outs[k][:, there, tiles + v] = piece
    for copy in copies[2:]:
        copy.wait()


def apply_kernel(
    dims,
    off_rows_ref,
    psi_ref,
    cross_ref,
    kin_ref,
    kern_ref,
    mult_ref,
    patt_ref,
    pot_hbm,
    last_hbm,
    out_hbm,
    out_ref,
    result_ref,
    pot_ref,
    last_ref,
    sems,
    out_sems,
):
    fn_count, edge, plane_len, classes, shares, chunk, reach = dims
    copies = fetch(((pot_hbm, pot_ref), (last_hbm, last_ref)), sems)
    stacks = [cross_ref.at[k] for k in range(cross_ref.shape[0])] + [last_ref.at[0]]
    rows = fn_count * edge
    tiles = plane_len // LANES // shares
    chunks = plane_len // chunk
    psi = psi_ref[...].reshape(rows, plane_len)
    off_rows = off_rows_ref[...]
    shape = (classes, 2 * SUBLANES, LANES)
    select = class_select(iota(shape, 0), off_rows, fn_count, edge, classes)
    shape = (classes, SUBLANES, LANES)
    deep = class_select(iota(shape, 0), off_rows, fn_count, edge, classes, 2)
    patt = patt_ref[...]
    small = [coefficient_rows(ref[...], patt, off_rows, fn_count)[None] for ref in (mult_ref, kern_ref)]
    upper = iota(shape, 1) < fn_count
    led = dot(kin_ref[...], psi)
    late = 2 * EARLY_PAIRS
    rest = [
        dot(deep, psi[:, (share * tiles + late) * LANES : (share + 1) * tiles * LANES]).reshape(
            classes, SUBLANES, -1
        )
        for share in range(shares)
    ]
    copies[0].wait()
    pot = pot_ref[...].reshape(rows, plane_len)
    for j in range(chunks):
        if j == len(stacks) - 1:
            copies[1].wait()
        lo, hi = max(0, j - reach), min(chunks, j + reach + 1)
        here = slice(j * chunk, (j + 1) * chunk)
        acc = dot(
            psi[:, lo * chunk : hi * chunk],
            stacks[j % len(stacks)][(lo - j + reach) * chunk : (hi - j + reach) * chunk, :],
        )
        acc = acc + led[:, here]
        acc = acc + pot[:, here].astype(jnp.float32) * psi[:, here].astype(jnp.float32)
        result_ref[:, here] = acc.astype(jnp.bfloat16)
    leaving = []
    for share in range(shares):
        first, last = 0, tiles * LANES
        ordered = dot(select, result_ref[:, share * last : (share + 1) * last])
        ordered = ordered.reshape(classes, 2, SUBLANES, last)
        for t in range(tiles):
            at = slice(first + t * LANES, first + (t + 1) * LANES)
            out_ref[:, share, t] = ordered[:, 0, :, at].astype(jnp.bfloat16)
        made = pair_units(ordered[:, 1, :, first:last], tiles, upper, small[0])
        made += pair_units(rest[share], tiles - late, upper, small[1])
        for v, piece in enumerate(made):
            out_ref[:, share, tiles + v] = piece
        leaving.append(pltpu.make_async_copy(out_ref.at[:, share], out_hbm.at[:, share], out_sems.at[share]))
        leaving[-1].start()
    for copy in leaving:
        copy.wait()


def turn_kernel(*refs):
    groups = len(refs) - refs[0].shape[0]
    arrived, outs = refs[:groups], refs[groups:]
    for near, out in enumerate(outs):
        for far in range(groups):
            out[far] = arrived[far][near]


def grid_rows(psi_all, h_ref, tiles, fn_count, wanted):
    devices = h_ref.shape[0]
    full = devices * SUBLANES
    pairs = (tiles + 1) // 2
    upper = iota((devices, SUBLANES, LANES), 1) < fn_count
    both = {}
    for v in range(pairs):
        if 2 * v not in wanted and 2 * v + 1 not in wanted:
            continue
        ours = psi_all[:, tiles + v] if v < EARLY_PAIRS else h_ref[:, tiles + pairs + v - EARLY_PAIRS]
        ours, theirs = ours.astype(jnp.float32), h_ref[:, tiles + v].astype(jnp.float32)
        both[2 * v] = jnp.where(upper, ours, pltpu.roll(theirs, fn_count, axis=1))
        both[2 * v + 1] = jnp.where(upper, pltpu.roll(ours, fn_count, axis=1), theirs)
    inside = [t for t in wanted if t < tiles]
    stacked = [
        jnp.concatenate([psi_all[:, t].reshape(full, LANES) for t in inside], axis=1),
        jnp.concatenate([both[t].reshape(full, LANES).astype(jnp.bfloat16) for t in inside], axis=1),
        jnp.concatenate([h_ref[:, t].reshape(full, LANES) for t in inside], axis=1),
    ]
    return stacked, both


def same_plane(gap, planes, row_depth, fn_count):
    half_col = jnp.bitwise_and(iota(gap.shape, 1) // fn_count, 1)
    return [
        jnp.bitwise_and(gap + row_depth - depth, planes - 1) == 0 for depth in (half_col, 2, half_col)
    ]


def masked(masks, plus, minus, fn_count):
    half_col = jnp.bitwise_and(iota(plus.shape, 1) // fn_count, 1)
    coef = (minus, jnp.where(half_col == 0, minus, plus), plus)
    return jnp.concatenate(
        [jnp.where(k, c, 0.0).astype(jnp.bfloat16) for k, c in zip(masks, coef)], axis=1
    )


def first_kernel(dims, *refs):
    fn_count, _, classes, shares, width, band_reach, sub_count, groups = dims
    near = len(refs) - groups - 7
    psi_refs, h_ref, outs = refs[:near], refs[near], refs[near + 1 : near + 1 + groups]
    psi_all, low_ref, plus_ref, minus_ref, gap_ref, grad_ref = refs[near + 1 + groups :]
    tiles = psi_refs[0].shape[1] - EARLY_PAIRS
    devices = h_ref.shape[0]
    full = devices * SUBLANES
    rank = lax.axis_index("brick") * sub_count + lax.axis_index("sub")
    my_class = rank // shares
    classes_bits = classes.bit_length() - 1
    for n, ref in enumerate(psi_refs):
        for far in range(groups):
            psi_all[jnp.bitwise_xor(rank, far * near + n)] = ref[far]

    stacked, both = grid_rows(psi_all, h_ref, tiles, fn_count, (*range(EARLY_TILES), tiles))
    halves = both[tiles]
    flat = halves.reshape(full, LANES).astype(jnp.bfloat16)
    lane_a, lane_b = iota((LANES, full), 0), iota((full, LANES), 1)
    weigh_a = jnp.where(lane_a == width, 256.0, jnp.where(lane_a == width + 1, 1.0, 0.0))
    weigh_b = jnp.where(lane_b == width, 256.0, jnp.where(lane_b == width + 1, 1.0, 0.0))
    off_row = dot(flat, weigh_a.astype(jnp.bfloat16)).astype(jnp.int32)
    off_col = dot_nt(weigh_b.astype(jnp.bfloat16), flat).astype(jnp.int32)

    def first_plane(off):
        inner = jnp.bitwise_and(my_class - off, classes - 1)
        return jnp.right_shift(off + inner - my_class, classes_bits)

    gap = first_plane(off_row) - first_plane(off_col)
    gap_ref[...] = gap

    turned = pltpu.roll(halves, fn_count, axis=1)
    upper = iota(halves.shape, 1) < fn_count
    column = iota((LANES, full), 1)
    column = column // SUBLANES * fn_count + column % fn_count
    expand = jnp.where((lane_a == column) & (lane_a < width), 1.0, 0.0).astype(jnp.bfloat16)

    def dense(rows):
        wide = dot(rows.reshape(full, LANES).astype(jnp.bfloat16), expand)
        turned_rows = []
        for owner in range(devices):
            shift = (owner - band_reach) * SUBLANES % full
            block = wide[owner * SUBLANES : (owner + 1) * SUBLANES]
            turned_rows.append(pltpu.roll(block, shift, axis=1) if shift else block)
        return jnp.concatenate(turned_rows, axis=0)

    plus = dense(jnp.where(upper, halves, turned))
    minus = -dense(jnp.where(upper, turned, halves))
    plus_ref[...] = plus
    minus_ref[...] = minus
    half_row = jnp.bitwise_and(iota((full, full), 0) // fn_count, 1)
    low = masked(same_plane(gap, devices * Q // classes, half_row, fn_count), plus, minus, fn_count)
    low_ref[...] = low
    grad = dot(low, jnp.concatenate(stacked, axis=0))
    for t in range(EARLY_TILES):
        piece = grad[:, t * LANES : (t + 1) * LANES].reshape(devices, SUBLANES, LANES)
        grad_ref[:, t] = piece.astype(jnp.bfloat16)
    for far in range(groups):
        for n in range(near):
            outs[far][n] = grad_ref[jnp.bitwise_xor(rank, far * near + n)]


def second_kernel(dims, psi_all, h_ref, low_ref, plus_ref, minus_ref, gap_ref, out_ref):
    fn_count, edge, classes = dims
    tiles = psi_all.shape[1] - EARLY_PAIRS
    devices = h_ref.shape[0]
    full = devices * SUBLANES
    planes = devices * Q // classes
    pairs = (tiles + 1) // 2
    stacked, both = grid_rows(psi_all, h_ref, tiles, fn_count, range(tiles))
    upper = iota((devices // 2, SUBLANES, LANES), 1) < fn_count
    dense_rows = []
    for t in range(tiles):
        two = both[t].reshape(devices // 2, 2, SUBLANES, LANES)
        two = jnp.where(upper, two[:, 0], pltpu.roll(two[:, 1], fn_count, axis=1))
        dense_rows.append(two.reshape(full // 2, LANES).astype(jnp.bfloat16))
    psi_rows = jnp.concatenate([stacked[0], jnp.concatenate(dense_rows, axis=1)], axis=0)
    gap = gap_ref[...]
    half_row = jnp.bitwise_and(iota((full, full), 0) // fn_count, 1)
    low = same_plane(gap, planes, half_row, fn_count)
    top = same_plane(gap, planes, 2, fn_count)
    rows = jnp.concatenate(stacked, axis=0)
    rest = dot(low_ref[...], rows[:, EARLY_TILES * LANES :])
    for t in range(tiles - EARLY_TILES):
        piece = rest[:, t * LANES : (t + 1) * LANES].reshape(devices, SUBLANES, LANES)
        out_ref[:, t] = piece.astype(jnp.bfloat16)
    upper = iota((devices, SUBLANES, LANES), 1) < fn_count
    second = dot(masked(top, plus_ref[...], minus_ref[...], fn_count), rows)
    second = second.reshape(devices, SUBLANES, tiles * LANES)
    for v, piece in enumerate(pair_units(second, tiles, upper, 0.0)):
        out_ref[:, tiles - EARLY_TILES + v] = piece

    sums = []
    for part in range(3):
        gram = dot_nt(psi_rows, stacked[part])
        low_gram = jnp.where(low[part], gram[:full], 0.0).reshape(devices, SUBLANES, full)
        deep = gram[full:].reshape(devices // 2, SUBLANES, full)
        other = pltpu.roll(deep, fn_count, axis=1)
        upper = iota(deep.shape, 1) < fn_count
        deep = jnp.stack([jnp.where(upper, deep, other), jnp.where(upper, other, deep)], axis=1)
        deep = jnp.where(top[part], deep.reshape(full, full), 0.0).reshape(devices, SUBLANES, full)
        sums.append(low_gram + pltpu.roll(low_gram, fn_count, axis=1) + deep)
    first = sums[0] + pltpu.roll(sums[0], full - fn_count, axis=2)
    third = sums[2] + pltpu.roll(sums[2], fn_count, axis=2)
    lanes_half = jnp.bitwise_and(iota((devices, SUBLANES, full), 2) // fn_count, 1)
    bands = sums[1] + jnp.where(lanes_half == 0, first, third)
    upper = iota((devices, SUBLANES, LANES), 1) < fn_count
    bands = jnp.where(upper, bands[:, :, :LANES], bands[:, :, LANES:])
    bands = bands * (1.0 / float(edge**3))
    out_ref[:, tiles - EARLY_TILES + pairs] = bands.astype(jnp.bfloat16)


def receive_kernel(dims, off_lanes_ref, in_ref, *refs):
    fn_count, edge, plane_len, classes, shares, band_reach, sub_count, near = dims
    early_refs, (grad_hbm, margin_ref, energy_ref, grad_ref, early_ref, sems) = refs[:near], refs[near:]
    tiles = plane_len // LANES // shares
    rows = fn_count * edge
    devices = classes * shares
    width = margin_ref.shape[1]
    rank = lax.axis_index("brick") * sub_count + lax.axis_index("sub")
    inner = classes * SUBLANES
    for n, ref in enumerate(early_refs):
        for far in range(ref.shape[0]):
            source = jnp.bitwise_xor(rank, far * near + n)
            early_ref[source // shares, jnp.bitwise_and(source, shares - 1)] = ref[far]
    pair_at = tiles - EARLY_TILES

    shape = (fn_count, edge, inner)
    member, plane = iota(shape, 0), iota(shape, 1)
    slot = iota(shape, 2)
    cls, sub = slot // SUBLANES, slot % SUBLANES
    half, owner_fn = sub // fn_count, sub % fn_count
    off_lanes = jnp.concatenate([off_lanes_ref[...]] * (inner // LANES), axis=1)[:1, None]
    at = jnp.bitwise_and(cls - off_lanes, classes - 1)
    same = owner_fn == member
    low = jnp.where(same & (plane == at + half * classes), 1.0, 0.0).astype(jnp.bfloat16)
    top = same & (plane == at + 2 * classes)
    place = []
    for parity in range(2):
        tops = jnp.where(top & (half == parity), 1.0, 0.0).astype(jnp.bfloat16)
        place.append(jnp.concatenate([low, tops], axis=2).reshape(rows, 2 * inner))
    copies = []
    for share in range(shares):
        for parity in range(2):
            columns = [
                jnp.concatenate(
                    [
                        (
                            early_ref[:, share, t] if t < EARLY_TILES else in_ref[:, share, t - EARLY_TILES]
                        ).reshape(inner, LANES),
                        in_ref[:, share, pair_at + t // 2].reshape(inner, LANES),
                    ],
                    axis=0,
                )
                for t in range(parity, tiles, 2)
            ]
            placed = dot(place[parity], jnp.concatenate(columns, axis=1)).astype(jnp.bfloat16)
            for n, t in enumerate(range(parity, tiles, 2)):
                spot = (share * tiles + t) * LANES
                grad_ref[:, :, spot : spot + LANES] = placed[:, n * LANES : (n + 1) * LANES].reshape(
                    fn_count, edge, LANES
                )
        part = pl.ds(share * tiles * LANES, tiles * LANES)
        copies.append(
            pltpu.make_async_copy(grad_ref.at[:, :, part], grad_hbm.at[:, :, part], sems.at[share])
        )
        copies[-1].start()

    total = jnp.sum(
        in_ref[:, :, pair_at + (tiles + 1) // 2].reshape(devices, SUBLANES, LANES).astype(jnp.float32), axis=0
    )
    terms = []
    for _ in range(3):
        terms.append(total.astype(jnp.bfloat16))
        total = total - terms[-1].astype(jnp.float32)
    terms = jnp.concatenate(terms + terms[-1:], axis=0)
    lane, col = iota((LANES, LANES), 0), iota((LANES, LANES), 1)
    partner = lax.rem(rank + col // fn_count - band_reach + devices, devices)
    for kind, ref in ((0, margin_ref), (1, energy_ref)):
        wanted = partner * SUBLANES + kind * fn_count + col % fn_count
        row = jnp.zeros((fn_count, LANES), jnp.float32)
        for part in range(2):
            picked = dot(terms, jnp.where(wanted == lane + part * LANES, 1.0, 0.0).astype(jnp.bfloat16))
            for n in range(3):
                first = n * SUBLANES + part * fn_count
                row = row + picked[first : first + fn_count]
        ref[...] = row[:, :width]
    for copy in copies:
        copy.wait()


def transposed_shards(classes, shares, psi, potential, offsets, kernel, multipliers, pattern):
    fn_count, edge, plane_len = psi.shape
    sub_count = lax.axis_size("sub")
    devices = sub_count * lax.axis_size("brick")
    width = kernel.shape[1]
    tiles = plane_len // LANES // shares
    band_reach = 2 * K
    chunk = 2 * LANES
    params = pltpu.CompilerParams(vmem_limit_bytes=20 * 2**20)
    vmem = pl.BlockSpec(memory_space=pltpu.VMEM)

    hbm = pl.BlockSpec(memory_space=pltpu.HBM)
    groups = 4
    near = devices // groups
    kinetic = np.kron(np.eye(fn_count, dtype=np.float32), kinetic_numpy(edge)).astype(jnp.bfloat16)
    cross, reach = cross_blocks(edge, chunk)
    early = tiles + EARLY_PAIRS
    units = tiles + (tiles + 1) // 2 * 2 - EARLY_PAIRS
    offsets = in_hbm(offsets)

    def block(*lead):
        return jax.ShapeDtypeStruct((*lead, SUBLANES, LANES), jnp.bfloat16)

    def cost(flops, moved):
        return pl.CostEstimate(flops=flops, bytes_accessed=moved, transcendentals=0)

    def exchange(array, bits):
        return lax.ppermute(array, axes, [(i, i ^ bits) for i in range(devices)])

    axes = ("brick", "sub")
    size = psi.size
    carried = (psi, cross[:-1], kinetic, kernel, multipliers, pattern)
    results = pl.pallas_call(
        functools.partial(
            pack_kernel, (fn_count, edge, plane_len, classes, shares, groups, sub_count, len(carried))
        ),
        out_shape=[block(near // shares, shares, early)] * groups
        + [jax.ShapeDtypeStruct(x.shape, x.dtype) for x in carried]
        + [jax.ShapeDtypeStruct((SUBLANES, LANES), jnp.int32)] * 2,
        in_specs=[hbm] * (1 + len(carried)),
        out_specs=[vmem] * (groups + len(carried) + 2),
        scratch_shapes=[
            pltpu.SMEM(offsets.shape, offsets.dtype),
            pltpu.SemaphoreType.DMA((1 + len(carried),)),
        ],
        compiler_params=params,
        cost_estimate=cost(512 * size, 4 * size),
        name="pack",
    )(offsets, *(in_hbm(jnp.asarray(x)) for x in carried))
    packed, kept = results[:groups], results[groups:-2]
    off_rows, off_lanes = results[-2:]
    packed = [x.reshape(near, early, SUBLANES, LANES) for x in packed]
    arrived = [None] * groups
    arrived[0] = packed[0]
    for far in (3, 2, 1):
        arrived[far] = exchange(packed[far], far * near)

    applied = pl.pallas_call(
        functools.partial(apply_kernel, (fn_count, edge, plane_len, classes, shares, chunk, reach)),
        out_shape=block(classes, shares, units),
        in_specs=[vmem] * (1 + len(kept)) + [hbm] * 2,
        out_specs=hbm,
        scratch_shapes=[
            pltpu.VMEM((classes, shares, units, SUBLANES, LANES), jnp.bfloat16),
            pltpu.VMEM((fn_count * edge, plane_len), jnp.bfloat16),
            pltpu.VMEM(potential.shape, potential.dtype),
            pltpu.VMEM(cross[-1:].shape, jnp.bfloat16),
            pltpu.SemaphoreType.DMA((2,)),
            pltpu.SemaphoreType.DMA((shares,)),
        ],
        compiler_params=params,
        cost_estimate=cost(4608 * size, 8 * size),
        name="apply",
    )(off_rows, *kept, in_hbm(potential), in_hbm(jnp.asarray(cross[-1:])))
    held = lax.all_to_all(applied.reshape(devices, units, SUBLANES, LANES), axes, 0, 0, tiled=True)

    turned = pl.pallas_call(
        turn_kernel,
        out_shape=[block(groups, early)] * near,
        in_specs=[vmem] * groups,
        out_specs=[vmem] * near,
        compiler_params=params,
        cost_estimate=cost(0, 4 * size),
        name="turn",
    )(*arrived)
    gathered = [x if n == 0 else exchange(x, n) for n, x in enumerate(turned)]

    full = devices * SUBLANES
    results = pl.pallas_call(
        functools.partial(
            first_kernel, (fn_count, edge, classes, shares, width, band_reach, sub_count, groups)
        ),
        out_shape=[block(near, EARLY_TILES)] * groups
        + [
            block(devices, early),
            jax.ShapeDtypeStruct((full, 3 * full), jnp.bfloat16),
            jax.ShapeDtypeStruct((full, full), jnp.float32),
            jax.ShapeDtypeStruct((full, full), jnp.float32),
            jax.ShapeDtypeStruct((full, full), jnp.int32),
        ],
        in_specs=[vmem] * (near + 1),
        out_specs=[vmem] * (groups + 5),
        scratch_shapes=[pltpu.VMEM((devices, EARLY_TILES, SUBLANES, LANES), jnp.bfloat16)],
        compiler_params=params,
        cost_estimate=cost(1024 * size, 4 * size),
        name="first",
    )(*gathered, held)
    leaving, tables = results[:groups], results[groups:]
    returned = [leaving[0]] + [None] * (groups - 1)
    for far in (3, 2, 1):
        returned[far] = exchange(leaving[far], far * near)

    back_units = tiles - EARLY_TILES + (tiles + 1) // 2 + 1
    made = pl.pallas_call(
        functools.partial(second_kernel, (fn_count, edge, classes)),
        out_shape=block(devices, back_units),
        in_specs=[vmem] * 6,
        out_specs=vmem,
        compiler_params=params,
        cost_estimate=cost(2048 * size, 4 * size),
        name="second",
    )(tables[0], held, *tables[1:])
    back = lax.all_to_all(made, axes, 0, 0, tiled=True)
    back = back.reshape(classes, shares, back_units, SUBLANES, LANES)
    spread = pl.pallas_call(
        turn_kernel,
        out_shape=[block(groups, EARLY_TILES)] * near,
        in_specs=[vmem] * groups,
        out_specs=[vmem] * near,
        compiler_params=params,
        cost_estimate=cost(0, 4 * size),
        name="spread",
    )(*returned)
    homed = [x if n == 0 else exchange(x, n) for n, x in enumerate(spread)]
    return pl.pallas_call(
        functools.partial(
            receive_kernel, (fn_count, edge, plane_len, classes, shares, band_reach, sub_count, near)
        ),
        out_shape=(
            jax.ShapeDtypeStruct(psi.shape, jnp.bfloat16),
            jax.ShapeDtypeStruct((fn_count, width), jnp.float32),
            jax.ShapeDtypeStruct((fn_count, width), jnp.float32),
        ),
        in_specs=[vmem] * (2 + near),
        out_specs=(hbm, vmem, vmem),
        scratch_shapes=[
            pltpu.VMEM(psi.shape, jnp.bfloat16),
            pltpu.VMEM((classes, shares, EARLY_TILES, SUBLANES, LANES), jnp.bfloat16),
            pltpu.SemaphoreType.DMA((shares,)),
        ],
        compiler_params=params,
        name="receive",
    )(off_lanes, back, *homed)


def any_shards(psi, potential, offsets, kernel, multipliers, pattern):
    devices = lax.axis_size("brick") * lax.axis_size("sub")
    plan = plan_of(devices, *psi.shape, kernel.shape[1])
    if plan is None:
        return shards(psi, potential, offsets, kernel, multipliers, pattern)
    return transposed_shards(*plan, psi, potential, offsets, kernel, multipliers, pattern)


def solution(mesh):
    in_specs = (
        P(("brick", "sub"), None, None),
        P(("brick", "sub"), None, None),
        P(("brick", "sub")),
        P(("brick", "sub"), None),
        P(("brick", "sub"), None),
        P(("brick", "sub"), None),
    )
    out_specs = (
        P(("brick", "sub"), None, None),
        P(("brick", "sub"), None),
        P(("brick", "sub"), None),
    )
    return jax.shard_map(any_shards, mesh=mesh, in_specs=in_specs, out_specs=out_specs, check_vma=False)
```

```python
import functools
import math

import jax
import jax.numpy as jnp
import numpy as np
from jax import lax
from jax.experimental import pallas as pl
from jax.experimental.pallas import tpu as pltpu
from jax.sharding import PartitionSpec as P

Q = 8
K = 6


filter_reach = 14


def shifted(block, axis, distance):
    devices = range(lax.axis_size(axis))
    route = [((i - distance) % len(devices), i) for i in devices]
    return lax.ppermute(block, axis, route)


def kinetic_matrix(edge_len):
    positions = jnp.arange(edge_len, dtype=jnp.int32)
    offset_gap = positions[:, None] - positions[None, :]
    distance = jnp.abs(offset_gap).astype(jnp.float32)
    parity_sign = 1.0 - 2.0 * (jnp.abs(offset_gap) % 2).astype(jnp.float32)
    off_diag = parity_sign / jnp.maximum(distance, 1.0) ** 2
    entries = jnp.where(offset_gap == 0, math.pi**2 / 6.0, off_diag)
    entries = jnp.where(jnp.abs(offset_gap) <= filter_reach, entries, 0.0)
    return entries.astype(jnp.bfloat16)


def cross_matrix(kinetic, edge_len):
    kin_float = kinetic.astype(jnp.float32)
    identity = jnp.eye(edge_len, dtype=jnp.float32)
    return (jnp.kron(kin_float, identity) + jnp.kron(identity, kin_float)).astype(jnp.bfloat16)


def apply_hamiltonian(psi, potential):
    fn_count, edge_len, plane_len = psi.shape
    kinetic = kinetic_matrix(edge_len)
    first_pass = jnp.einsum("wx,fxq->fwq", kinetic, psi, preferred_element_type=jnp.float32)
    cross = cross_matrix(kinetic, edge_len)
    second_pass = jnp.dot(
        psi.reshape(fn_count * edge_len, plane_len), cross, preferred_element_type=jnp.float32
    )
    summed = first_pass + second_pass.reshape(fn_count, edge_len, plane_len)
    result = summed + potential.astype(jnp.float32) * psi.astype(jnp.float32)
    return result.astype(jnp.bfloat16)


def embed(functions, region_start, window_len):

    def place(function, start_at):
        zeros_block = jnp.zeros((window_len, function.shape[1]), function.dtype)
        return lax.dynamic_update_slice_in_dim(zeros_block, function, start_at, 0)

    return jax.vmap(place)(functions, region_start)


def extract(window, region_start, edge_len):

    def take(planes, start_at):
        return lax.dynamic_slice_in_dim(planes, start_at, edge_len, 0)

    return jax.vmap(take)(window, region_start)


def dense_kernel(band_rows, group_count, band_reach, fn_count):
    dense_rows = []
    for slot_group in range(group_count):
        padded = jnp.pad(
            band_rows[slot_group], ((0, 0), (group_count * fn_count, group_count * fn_count))
        )
        first_col = (group_count + band_reach - slot_group) * fn_count
        dense_rows.append(padded[:, first_col : first_col + group_count * fn_count])
    return jnp.concatenate(dense_rows, axis=0)


def band_from_dense(dense, group_count, band_reach, fn_count):
    padded = jnp.pad(dense, ((0, 0), (band_reach * fn_count, band_reach * fn_count)))
    band_width = (2 * band_reach + 1) * fn_count
    pieces = []
    for slot_group in range(group_count):
        first_col = slot_group * fn_count
        pieces.append(padded[first_col : first_col + fn_count, first_col : first_col + band_width])
    return jnp.stack(pieces)


def grid_work(phi, hphi, kernel_rows, multi_rows, group_count, band_reach, fn_count, edge_len):
    volume_scale = 1.0 / float(edge_len**3)
    contract = (((1,), (1,)), ((), ()))
    margin = lax.dot_general(phi, phi, contract, preferred_element_type=jnp.float32) * volume_scale
    energy = lax.dot_general(phi, hphi, contract, preferred_element_type=jnp.float32) * volume_scale
    mixed = jnp.concatenate(
        [
            dense_kernel(kernel_rows, group_count, band_reach, fn_count),
            -dense_kernel(multi_rows, group_count, band_reach, fn_count),
        ],
        axis=1,
    )
    stacked = jnp.concatenate([hphi, phi], axis=0)
    grad = jnp.dot(mixed, stacked, preferred_element_type=jnp.float32).astype(jnp.bfloat16)
    margin_rows = band_from_dense(margin, group_count, band_reach, fn_count).astype(jnp.bfloat16)
    energy_rows = band_from_dense(energy, group_count, band_reach, fn_count).astype(jnp.bfloat16)
    return (grad, margin_rows, energy_rows)


def shards(psi, potential, offsets, kernel, multipliers, pattern):
    fn_count, edge_len, plane_len = psi.shape
    sub_count = lax.axis_size("sub")
    brick_count = lax.axis_size("brick")
    total_planes = Q * sub_count * brick_count
    band_reach = 2 * K
    band_width = kernel.shape[1]
    hpsi = apply_hamiltonian(psi, potential)
    spread = jnp.repeat(pattern, fn_count, axis=1).astype(jnp.bfloat16)
    kernel_eff = kernel * spread
    multi_eff = multipliers * spread
    margin_sum = jnp.zeros((fn_count, band_width), jnp.float32)
    energy_sum = jnp.zeros((fn_count, band_width), jnp.float32)
    my_rank = lax.axis_index("brick") * sub_count + lax.axis_index("sub")
    group_count = 2 * K + 1
    window_len = group_count * Q
    region_start = jnp.mod(offsets - (my_rank - K) * Q, total_planes)
    window_psi = embed(psi, region_start, window_len)
    window_hpsi = embed(hpsi, region_start, window_len)
    arrived = [None] * group_count
    for offset in range(-K, K + 1):
        first_plane = (offset + K) * Q
        payload = (
            window_psi[:, first_plane : first_plane + Q],
            window_hpsi[:, first_plane : first_plane + Q],
            kernel_eff,
            multi_eff,
        )
        if offset != 0:
            payload = shifted(
                (payload[0], payload[1], payload[2], payload[3]), ("brick", "sub"), offset
            )
        arrived[K - offset] = payload
    phi = jnp.concatenate([arrival[0] for arrival in arrived], axis=0).reshape(
        group_count * fn_count, Q * plane_len
    )
    hphi = jnp.concatenate([arrival[1] for arrival in arrived], axis=0).reshape(
        group_count * fn_count, Q * plane_len
    )
    kernel_rows = jnp.stack([arrival[2] for arrival in arrived])
    multi_rows = jnp.stack([arrival[3] for arrival in arrived])
    grad, margin_rows, energy_rows = grid_work(
        phi, hphi, kernel_rows, multi_rows, group_count, band_reach, fn_count, edge_len
    )
    grad = grad.reshape(group_count, fn_count, Q, plane_len)
    window = [None] * group_count
    for offset in range(-K, K + 1):
        slot_group = K - offset
        payload = (grad[slot_group], margin_rows[slot_group], energy_rows[slot_group])
        if offset != 0:
            payload = shifted((payload[0], payload[1], payload[2]), ("brick", "sub"), -offset)
        window[offset + K] = payload[0]
        margin_sum = margin_sum + payload[1].astype(jnp.float32)
        energy_sum = energy_sum + payload[2].astype(jnp.float32)
    gradient = extract(jnp.concatenate(window, axis=1), region_start, edge_len)
    return (gradient, margin_sum, energy_sum)


EARLY_PAIRS = 2
EARLY_TILES = 8
SUBLANES = 8
LANES = 128


def iota(shape, dim):
    return lax.broadcasted_iota(jnp.int32, shape, dim)


def plan_of(devices, fn_count, edge_len, plane_len, band_width):
    tiles = plane_len // LANES
    for shares in range(1, tiles + 1):
        if devices % shares or tiles % shares:
            continue
        classes = devices // shares
        per_class = edge_len // classes
        fits = (
            plane_len % (2 * LANES) == 0
            and edge_len % classes == 0
            and tiles // shares > 2 * EARLY_PAIRS
            and (devices * Q) % classes == 0
            and classes & (classes - 1) == 0
            and fn_count * 2 == SUBLANES
            and per_class == 3
            and edge_len % SUBLANES == 0
            and band_width + 2 <= LANES
            and devices * SUBLANES == 2 * LANES
            and band_width == (4 * K + 1) * fn_count
        )
        if fits:
            return classes, shares
    return None


def kinetic_numpy(edge_len):
    positions = np.arange(edge_len)
    gap = np.abs(positions[:, None] - positions[None, :])
    sign = 1.0 - 2.0 * (gap % 2)
    entries = sign / np.maximum(gap, 1).astype(np.float32) ** 2
    entries = np.where(gap == 0, np.float32(math.pi**2 / 6.0), entries)
    entries = np.where(gap <= filter_reach, entries, 0.0)
    return entries.astype(np.float32)


def cross_blocks(edge_len, chunk):
    line = kinetic_numpy(edge_len).astype(jnp.bfloat16).astype(np.float32)[0]
    period = math.lcm(edge_len, chunk)
    reach = -(-filter_reach * edge_len // chunk)
    stacks = []
    for first in range(0, period, chunk):
        row = np.arange(first - reach * chunk, first + (reach + 1) * chunk)[:, None]
        col = np.arange(first, first + chunk)[None, :]
        gap_y = np.abs(row // edge_len - col // edge_len)
        gap_z = np.abs(row % edge_len - col % edge_len)
        weight = np.where(np.arange(edge_len) <= filter_reach, line, 0.0)
        block = np.where(gap_z == 0, weight[np.minimum(gap_y, edge_len - 1)], 0.0)
        block = block + np.where(gap_y == 0, weight[gap_z], 0.0)
        stacks.append(block)
    return np.stack(stacks).astype(jnp.bfloat16), reach


def dot(a, b):
    return lax.dot_general(a, b, (((1,), (0,)), ((), ())), preferred_element_type=jnp.float32)


def dot_nt(a, b):
    return lax.dot_general(a, b, (((1,), (1,)), ((), ())), preferred_element_type=jnp.float32)


def in_hbm(array):
    return pltpu.with_memory_space_constraint(array, pltpu.HBM)


def pick(index, values):
    out = jnp.full(index.shape, values[0], jnp.int32)
    for k in range(1, len(values)):
        out = jnp.where(index == k, values[k], out)
    return out


def fetch(pairs, sems):
    copies = [pltpu.make_async_copy(source, target, sems.at[n]) for n, (source, target) in enumerate(pairs)]
    for copy in copies:
        copy.start()
    return copies


def class_select(target, off_rows, fn_count, edge, classes, least=0):
    shape = target.shape
    item, lane = iota(shape, 1), iota(shape, 2)
    member = item % fn_count
    depth = jnp.minimum(item // fn_count + least, 2)
    off_rows = jnp.concatenate([off_rows] * (shape[1] // SUBLANES), axis=0)[None]
    inner = jnp.bitwise_and(target - off_rows, classes - 1)
    source = member * edge + depth * classes + inner
    rows = fn_count * edge
    wide = [
        jnp.where(source == lane + k * LANES, 1.0, 0.0).astype(jnp.bfloat16)
        for k in range(-(-rows // LANES))
    ]
    return jnp.concatenate(wide, axis=2).reshape(shape[0] * shape[1], -1)[:, :rows]


def coefficient_rows(band, pattern, off_rows, fn_count):
    width, blocks = band.shape[1], pattern.shape[1]
    spread = jnp.where(
        iota((blocks, width), 1) // fn_count == iota((blocks, width), 0), 1.0, 0.0
    ).astype(jnp.bfloat16)
    small = band.astype(jnp.float32) * dot(pattern.astype(jnp.float32).astype(jnp.bfloat16), spread)
    small = jnp.concatenate([small, small], axis=0)
    small = jnp.concatenate([small, jnp.zeros((SUBLANES, LANES - width), jnp.float32)], axis=1)
    lane = iota((SUBLANES, LANES), 1)
    small = jnp.where(lane == width, jnp.right_shift(off_rows, 8).astype(jnp.float32), small)
    return jnp.where(lane == width + 1, jnp.bitwise_and(off_rows, 255).astype(jnp.float32), small)


def pair_units(deep, count, upper, last):
    made = []
    for t in range(0, count, 2):
        even = deep[..., t * LANES : (t + 1) * LANES]
        odd = deep[..., (t + 1) * LANES : (t + 2) * LANES] if t + 1 < count else last
        made.append(jnp.where(upper, even, odd).astype(jnp.bfloat16))
    return made


def pack_kernel(dims, offs_hbm, *refs):
    fn_count, edge, plane_len, classes, shares, groups, sub_count, carried = dims
    sources, outs, kept = refs[:carried], refs[carried : carried + groups], refs[carried + groups : -4]
    off_rows_ref, off_lanes_ref, offs_ref, sems = refs[-4:]
    copies = fetch(((offs_hbm, offs_ref), *zip(sources, kept)), sems)
    rows = fn_count * edge
    tiles = plane_len // LANES // shares
    near = classes // groups
    rank = lax.axis_index("brick") * sub_count + lax.axis_index("sub")
    mine = jnp.bitwise_and(rank, shares - 1)
    copies[0].wait()
    offs = [offs_ref[k] for k in range(fn_count)]
    off_rows = pick(iota((SUBLANES, LANES), 0) % fn_count, offs)
    off_rows_ref[...] = off_rows
    off_lanes_ref[...] = pick(iota((SUBLANES, LANES), 1) % fn_count, offs)
    target = jnp.bitwise_xor(iota((classes, SUBLANES, LANES), 0), rank // shares)
    select = class_select(target, off_rows, fn_count, edge, classes)
    deep = class_select(target, off_rows, fn_count, edge, classes, 2)
    upper = iota((near, SUBLANES, LANES), 1) < fn_count
    copies[1].wait()
    psi = kept[0][...].reshape(rows, plane_len)
    for share in range(shares):
        there = jnp.bitwise_xor(mine, share)
        ordered = dot(select, psi[:, share * tiles * LANES : (share + 1) * tiles * LANES])
        ordered = ordered.reshape(groups, near, SUBLANES, tiles * LANES)
        for k in range(groups):
            for t in range(tiles):
                outs[k][:, there, t] = ordered[k, :, :, t * LANES : (t + 1) * LANES].astype(jnp.bfloat16)
        start = share * tiles * LANES
        second = dot(deep, psi[:, start : start + 2 * EARLY_PAIRS * LANES])
        second = second.reshape(groups, near, SUBLANES, 2 * EARLY_PAIRS * LANES)
        for k in range(groups):
            for v, piece in enumerate(pair_units(second[k], 2 * EARLY_PAIRS, upper, None)):
                outs[k][:, there, tiles + v] = piece
    for copy in copies[2:]:
        copy.wait()


def apply_kernel(
    dims,
    off_rows_ref,
    psi_ref,
    cross_ref,
    kin_ref,
    kern_ref,
    mult_ref,
    patt_ref,
    pot_hbm,
    last_hbm,
    out_hbm,
    out_ref,
    result_ref,
    pot_ref,
    last_ref,
    sems,
    out_sems,
):
    fn_count, edge, plane_len, classes, shares, chunk, reach = dims
    copies = fetch(((pot_hbm, pot_ref), (last_hbm, last_ref)), sems)
    stacks = [cross_ref.at[k] for k in range(cross_ref.shape[0])] + [last_ref.at[0]]
    rows = fn_count * edge
    tiles = plane_len // LANES // shares
    chunks = plane_len // chunk
    psi = psi_ref[...].reshape(rows, plane_len)
    off_rows = off_rows_ref[...]
    shape = (classes, 2 * SUBLANES, LANES)
    select = class_select(iota(shape, 0), off_rows, fn_count, edge, classes)
    shape = (classes, SUBLANES, LANES)
    deep = class_select(iota(shape, 0), off_rows, fn_count, edge, classes, 2)
    patt = patt_ref[...]
    small = [coefficient_rows(ref[...], patt, off_rows, fn_count)[None] for ref in (mult_ref, kern_ref)]
    upper = iota(shape, 1) < fn_count
    led = dot(kin_ref[...], psi)
    late = 2 * EARLY_PAIRS
    rest = [
        dot(deep, psi[:, (share * tiles + late) * LANES : (share + 1) * tiles * LANES]).reshape(
            classes, SUBLANES, -1
        )
        for share in range(shares)
    ]
    copies[0].wait()
    pot = pot_ref[...].reshape(rows, plane_len)
    for j in range(chunks):
        if j == len(stacks) - 1:
            copies[1].wait()
        lo, hi = max(0, j - reach), min(chunks, j + reach + 1)
        here = slice(j * chunk, (j + 1) * chunk)
        acc = dot(
            psi[:, lo * chunk : hi * chunk],
            stacks[j % len(stacks)][(lo - j + reach) * chunk : (hi - j + reach) * chunk, :],
        )
        acc = acc + led[:, here]
        acc = acc + pot[:, here].astype(jnp.float32) * psi[:, here].astype(jnp.float32)
        result_ref[:, here] = acc.astype(jnp.bfloat16)
    leaving = []
    for share in range(shares):
        first, last = 0, tiles * LANES
        ordered = dot(select, result_ref[:, share * last : (share + 1) * last])
        ordered = ordered.reshape(classes, 2, SUBLANES, last)
        for t in range(tiles):
            at = slice(first + t * LANES, first + (t + 1) * LANES)
            out_ref[:, share, t] = ordered[:, 0, :, at].astype(jnp.bfloat16)
        made = pair_units(ordered[:, 1, :, first:last], tiles, upper, small[0])
        made += pair_units(rest[share], tiles - late, upper, small[1])
        for v, piece in enumerate(made):
            out_ref[:, share, tiles + v] = piece
        leaving.append(pltpu.make_async_copy(out_ref.at[:, share], out_hbm.at[:, share], out_sems.at[share]))
        leaving[-1].start()
    for copy in leaving:
        copy.wait()


def turn_kernel(*refs):
    groups = len(refs) - refs[0].shape[0]
    arrived, outs = refs[:groups], refs[groups:]
    for near, out in enumerate(outs):
        for far in range(groups):
            out[far] = arrived[far][near]


def grid_rows(psi_all, h_ref, tiles, fn_count, wanted):
    devices = h_ref.shape[0]
    full = devices * SUBLANES
    pairs = (tiles + 1) // 2
    upper = iota((devices, SUBLANES, LANES), 1) < fn_count
    both = {}
    for v in range(pairs):
        if 2 * v not in wanted and 2 * v + 1 not in wanted:
            continue
        ours = psi_all[:, tiles + v] if v < EARLY_PAIRS else h_ref[:, tiles + pairs + v - EARLY_PAIRS]
        ours, theirs = ours.astype(jnp.float32), h_ref[:, tiles + v].astype(jnp.float32)
        both[2 * v] = jnp.where(upper, ours, pltpu.roll(theirs, fn_count, axis=1))
        both[2 * v + 1] = jnp.where(upper, pltpu.roll(ours, fn_count, axis=1), theirs)
    inside = [t for t in wanted if t < tiles]
    stacked = [
        jnp.concatenate([psi_all[:, t].reshape(full, LANES) for t in inside], axis=1),
        jnp.concatenate([both[t].reshape(full, LANES).astype(jnp.bfloat16) for t in inside], axis=1),
        jnp.concatenate([h_ref[:, t].reshape(full, LANES) for t in inside], axis=1),
    ]
    return stacked, both


def same_plane(gap, planes, row_depth, fn_count):
    half_col = jnp.bitwise_and(iota(gap.shape, 1) // fn_count, 1)
    return [
        jnp.bitwise_and(gap + row_depth - depth, planes - 1) == 0 for depth in (half_col, 2, half_col)
    ]


def masked(masks, plus, minus, fn_count):
    half_col = jnp.bitwise_and(iota(plus.shape, 1) // fn_count, 1)
    coef = (minus, jnp.where(half_col == 0, minus, plus), plus)
    return jnp.concatenate(
        [jnp.where(k, c, 0.0).astype(jnp.bfloat16) for k, c in zip(masks, coef)], axis=1
    )


def first_kernel(dims, *refs):
    fn_count, _, classes, shares, width, band_reach, sub_count, groups = dims
    near = len(refs) - groups - 7
    psi_refs, h_ref, outs = refs[:near], refs[near], refs[near + 1 : near + 1 + groups]
    psi_all, low_ref, plus_ref, minus_ref, gap_ref, grad_ref = refs[near + 1 + groups :]
    tiles = psi_refs[0].shape[1] - EARLY_PAIRS
    devices = h_ref.shape[0]
    full = devices * SUBLANES
    rank = lax.axis_index("brick") * sub_count + lax.axis_index("sub")
    my_class = rank // shares
    classes_bits = classes.bit_length() - 1
    for n, ref in enumerate(psi_refs):
        for far in range(groups):
            psi_all[jnp.bitwise_xor(rank, far * near + n)] = ref[far]

    stacked, both = grid_rows(psi_all, h_ref, tiles, fn_count, (*range(EARLY_TILES), tiles))
    halves = both[tiles]
    flat = halves.reshape(full, LANES).astype(jnp.bfloat16)
    lane_a, lane_b = iota((LANES, full), 0), iota((full, LANES), 1)
    weigh_a = jnp.where(lane_a == width, 256.0, jnp.where(lane_a == width + 1, 1.0, 0.0))
    weigh_b = jnp.where(lane_b == width, 256.0, jnp.where(lane_b == width + 1, 1.0, 0.0))
    off_row = dot(flat, weigh_a.astype(jnp.bfloat16)).astype(jnp.int32)
    off_col = dot_nt(weigh_b.astype(jnp.bfloat16), flat).astype(jnp.int32)

    def first_plane(off):
        inner = jnp.bitwise_and(my_class - off, classes - 1)
        return jnp.right_shift(off + inner - my_class, classes_bits)

    gap = first_plane(off_row) - first_plane(off_col)
    gap_ref[...] = gap

    turned = pltpu.roll(halves, fn_count, axis=1)
    upper = iota(halves.shape, 1) < fn_count
    column = iota((LANES, full), 1)
    column = column // SUBLANES * fn_count + column % fn_count
    expand = jnp.where((lane_a == column) & (lane_a < width), 1.0, 0.0).astype(jnp.bfloat16)

    def dense(rows):
        wide = dot(rows.reshape(full, LANES).astype(jnp.bfloat16), expand)
        turned_rows = []
        for owner in range(devices):
            shift = (owner - band_reach) * SUBLANES % full
            block = wide[owner * SUBLANES : (owner + 1) * SUBLANES]
            turned_rows.append(pltpu.roll(block, shift, axis=1) if shift else block)
        return jnp.concatenate(turned_rows, axis=0)

    plus = dense(jnp.where(upper, halves, turned))
    minus = -dense(jnp.where(upper, turned, halves))
    plus_ref[...] = plus
    minus_ref[...] = minus
    half_row = jnp.bitwise_and(iota((full, full), 0) // fn_count, 1)
    low = masked(same_plane(gap, devices * Q // classes, half_row, fn_count), plus, minus, fn_count)
    low_ref[...] = low
    grad = dot(low, jnp.concatenate(stacked, axis=0))
    for t in range(EARLY_TILES):
        piece = grad[:, t * LANES : (t + 1) * LANES].reshape(devices, SUBLANES, LANES)
        grad_ref[:, t] = piece.astype(jnp.bfloat16)
    for far in range(groups):
        for n in range(near):
            outs[far][n] = grad_ref[jnp.bitwise_xor(rank, far * near + n)]


def second_kernel(dims, psi_all, h_ref, low_ref, plus_ref, minus_ref, gap_ref, out_ref):
    fn_count, edge, classes = dims
    tiles = psi_all.shape[1] - EARLY_PAIRS
    devices = h_ref.shape[0]
    full = devices * SUBLANES
    planes = devices * Q // classes
    pairs = (tiles + 1) // 2
    stacked, both = grid_rows(psi_all, h_ref, tiles, fn_count, range(tiles))
    upper = iota((devices // 2, SUBLANES, LANES), 1) < fn_count
    dense_rows = []
    for t in range(tiles):
        two = both[t].reshape(devices // 2, 2, SUBLANES, LANES)
        two = jnp.where(upper, two[:, 0], pltpu.roll(two[:, 1], fn_count, axis=1))
        dense_rows.append(two.reshape(full // 2, LANES).astype(jnp.bfloat16))
    psi_rows = jnp.concatenate([stacked[0], jnp.concatenate(dense_rows, axis=1)], axis=0)
    gap = gap_ref[...]
    half_row = jnp.bitwise_and(iota((full, full), 0) // fn_count, 1)
    low = same_plane(gap, planes, half_row, fn_count)
    top = same_plane(gap, planes, 2, fn_count)
    rows = jnp.concatenate(stacked, axis=0)
    rest = dot(low_ref[...], rows[:, EARLY_TILES * LANES :])
    for t in range(tiles - EARLY_TILES):
        piece = rest[:, t * LANES : (t + 1) * LANES].reshape(devices, SUBLANES, LANES)
        out_ref[:, t] = piece.astype(jnp.bfloat16)
    upper = iota((devices, SUBLANES, LANES), 1) < fn_count
    second = dot(masked(top, plus_ref[...], minus_ref[...], fn_count), rows)
    second = second.reshape(devices, SUBLANES, tiles * LANES)
    for v, piece in enumerate(pair_units(second, tiles, upper, 0.0)):
        out_ref[:, tiles - EARLY_TILES + v] = piece

    sums = []
    for part in range(3):
        gram = dot_nt(psi_rows, stacked[part])
        low_gram = jnp.where(low[part], gram[:full], 0.0).reshape(devices, SUBLANES, full)
        deep = gram[full:].reshape(devices // 2, SUBLANES, full)
        other = pltpu.roll(deep, fn_count, axis=1)
        upper = iota(deep.shape, 1) < fn_count
        deep = jnp.stack([jnp.where(upper, deep, other), jnp.where(upper, other, deep)], axis=1)
        deep = jnp.where(top[part], deep.reshape(full, full), 0.0).reshape(devices, SUBLANES, full)
        sums.append(low_gram + pltpu.roll(low_gram, fn_count, axis=1) + deep)
    first = sums[0] + pltpu.roll(sums[0], full - fn_count, axis=2)
    third = sums[2] + pltpu.roll(sums[2], fn_count, axis=2)
    lanes_half = jnp.bitwise_and(iota((devices, SUBLANES, full), 2) // fn_count, 1)
    bands = sums[1] + jnp.where(lanes_half == 0, first, third)
    upper = iota((devices, SUBLANES, LANES), 1) < fn_count
    bands = jnp.where(upper, bands[:, :, :LANES], bands[:, :, LANES:])
    bands = bands * (1.0 / float(edge**3))
    out_ref[:, tiles - EARLY_TILES + pairs] = bands.astype(jnp.bfloat16)


def receive_kernel(dims, off_lanes_ref, in_ref, *refs):
    fn_count, edge, plane_len, classes, shares, band_reach, sub_count, near = dims
    early_refs, (grad_hbm, margin_ref, energy_ref, grad_ref, early_ref, sems) = refs[:near], refs[near:]
    tiles = plane_len // LANES // shares
    rows = fn_count * edge
    devices = classes * shares
    width = margin_ref.shape[1]
    rank = lax.axis_index("brick") * sub_count + lax.axis_index("sub")
    inner = classes * SUBLANES
    for n, ref in enumerate(early_refs):
        for far in range(ref.shape[0]):
            source = jnp.bitwise_xor(rank, far * near + n)
            early_ref[source // shares, jnp.bitwise_and(source, shares - 1)] = ref[far]
    pair_at = tiles - EARLY_TILES

    shape = (fn_count, edge, inner)
    member, plane = iota(shape, 0), iota(shape, 1)
    slot = iota(shape, 2)
    cls, sub = slot // SUBLANES, slot % SUBLANES
    half, owner_fn = sub // fn_count, sub % fn_count
    off_lanes = jnp.concatenate([off_lanes_ref[...]] * (inner // LANES), axis=1)[:1, None]
    at = jnp.bitwise_and(cls - off_lanes, classes - 1)
    same = owner_fn == member
    low = jnp.where(same & (plane == at + half * classes), 1.0, 0.0).astype(jnp.bfloat16)
    top = same & (plane == at + 2 * classes)
    place = []
    for parity in range(2):
        tops = jnp.where(top & (half == parity), 1.0, 0.0).astype(jnp.bfloat16)
        place.append(jnp.concatenate([low, tops], axis=2).reshape(rows, 2 * inner))
    copies = []
    for share in range(shares):
        for parity in range(2):
            columns = [
                jnp.concatenate(
                    [
                        (
                            early_ref[:, share, t] if t < EARLY_TILES else in_ref[:, share, t - EARLY_TILES]
                        ).reshape(inner, LANES),
                        in_ref[:, share, pair_at + t // 2].reshape(inner, LANES),
                    ],
                    axis=0,
                )
                for t in range(parity, tiles, 2)
            ]
            placed = dot(place[parity], jnp.concatenate(columns, axis=1)).astype(jnp.bfloat16)
            for n, t in enumerate(range(parity, tiles, 2)):
                spot = (share * tiles + t) * LANES
                grad_ref[:, :, spot : spot + LANES] = placed[:, n * LANES : (n + 1) * LANES].reshape(
                    fn_count, edge, LANES
                )
        part = pl.ds(share * tiles * LANES, tiles * LANES)
        copies.append(
            pltpu.make_async_copy(grad_ref.at[:, :, part], grad_hbm.at[:, :, part], sems.at[share])
        )
        copies[-1].start()

    total = jnp.sum(
        in_ref[:, :, pair_at + (tiles + 1) // 2].reshape(devices, SUBLANES, LANES).astype(jnp.float32), axis=0
    )
    terms = []
    for _ in range(3):
        terms.append(total.astype(jnp.bfloat16))
        total = total - terms[-1].astype(jnp.float32)
    terms = jnp.concatenate(terms + terms[-1:], axis=0)
    lane, col = iota((LANES, LANES), 0), iota((LANES, LANES), 1)
    partner = lax.rem(rank + col // fn_count - band_reach + devices, devices)
    for kind, ref in ((0, margin_ref), (1, energy_ref)):
        wanted = partner * SUBLANES + kind * fn_count + col % fn_count
        row = jnp.zeros((fn_count, LANES), jnp.float32)
        for part in range(2):
            picked = dot(terms, jnp.where(wanted == lane + part * LANES, 1.0, 0.0).astype(jnp.bfloat16))
            for n in range(3):
                first = n * SUBLANES + part * fn_count
                row = row + picked[first : first + fn_count]
        ref[...] = row[:, :width]
    for copy in copies:
        copy.wait()


def transposed_shards(classes, shares, psi, potential, offsets, kernel, multipliers, pattern):
    fn_count, edge, plane_len = psi.shape
    sub_count = lax.axis_size("sub")
    devices = sub_count * lax.axis_size("brick")
    width = kernel.shape[1]
    tiles = plane_len // LANES // shares
    band_reach = 2 * K
    chunk = 2 * LANES
    params = pltpu.CompilerParams(vmem_limit_bytes=20 * 2**20)
    vmem = pl.BlockSpec(memory_space=pltpu.VMEM)

    hbm = pl.BlockSpec(memory_space=pltpu.HBM)
    groups = 4
    near = devices // groups
    kinetic = np.kron(np.eye(fn_count, dtype=np.float32), kinetic_numpy(edge)).astype(jnp.bfloat16)
    cross, reach = cross_blocks(edge, chunk)
    early = tiles + EARLY_PAIRS
    units = tiles + (tiles + 1) // 2 * 2 - EARLY_PAIRS
    offsets = in_hbm(offsets)

    def block(*lead):
        return jax.ShapeDtypeStruct((*lead, SUBLANES, LANES), jnp.bfloat16)

    def cost(flops, moved):
        return pl.CostEstimate(flops=flops, bytes_accessed=moved, transcendentals=0)

    def exchange(array, bits):
        return lax.ppermute(array, axes, [(i, i ^ bits) for i in range(devices)])

    def within(blocks):
        moved = {}
        for n in range(len(blocks) - 1, 0, -1):
            moved[n] = exchange(blocks[n], n)
        return [blocks[0]] + [moved[n] for n in range(1, len(blocks))]

    axes = ("brick", "sub")
    size = psi.size
    carried = (psi, cross[:-1], kinetic, kernel, multipliers, pattern)
    results = pl.pallas_call(
        functools.partial(
            pack_kernel, (fn_count, edge, plane_len, classes, shares, groups, sub_count, len(carried))
        ),
        out_shape=[block(near // shares, shares, early)] * groups
        + [jax.ShapeDtypeStruct(x.shape, x.dtype) for x in carried]
        + [jax.ShapeDtypeStruct((SUBLANES, LANES), jnp.int32)] * 2,
        in_specs=[hbm] * (1 + len(carried)),
        out_specs=[vmem] * (groups + len(carried) + 2),
        scratch_shapes=[
            pltpu.SMEM(offsets.shape, offsets.dtype),
            pltpu.SemaphoreType.DMA((1 + len(carried),)),
        ],
        compiler_params=params,
        cost_estimate=cost(512 * size, 4 * size),
        name="pack",
    )(offsets, *(in_hbm(jnp.asarray(x)) for x in carried))
    packed, kept = results[:groups], results[groups:-2]
    off_rows, off_lanes = results[-2:]
    packed = [x.reshape(near, early, SUBLANES, LANES) for x in packed]
    arrived = [None] * groups
    arrived[0] = packed[0]
    for far in (3, 2, 1):
        arrived[far] = exchange(packed[far], far * near)

    applied = pl.pallas_call(
        functools.partial(apply_kernel, (fn_count, edge, plane_len, classes, shares, chunk, reach)),
        out_shape=block(classes, shares, units),
        in_specs=[vmem] * (1 + len(kept)) + [hbm] * 2,
        out_specs=hbm,
        scratch_shapes=[
            pltpu.VMEM((classes, shares, units, SUBLANES, LANES), jnp.bfloat16),
            pltpu.VMEM((fn_count * edge, plane_len), jnp.bfloat16),
            pltpu.VMEM(potential.shape, potential.dtype),
            pltpu.VMEM(cross[-1:].shape, jnp.bfloat16),
            pltpu.SemaphoreType.DMA((2,)),
            pltpu.SemaphoreType.DMA((shares,)),
        ],
        compiler_params=params,
        cost_estimate=cost(4608 * size, 8 * size),
        name="apply",
    )(off_rows, *kept, in_hbm(potential), in_hbm(jnp.asarray(cross[-1:])))
    held = lax.all_to_all(applied.reshape(devices, units, SUBLANES, LANES), axes, 0, 0, tiled=True)

    turned = pl.pallas_call(
        turn_kernel,
        out_shape=[block(groups, early)] * near,
        in_specs=[vmem] * groups,
        out_specs=[vmem] * near,
        compiler_params=params,
        cost_estimate=cost(0, 4 * size),
        name="turn",
    )(*arrived)
    gathered = within(turned)

    full = devices * SUBLANES
    results = pl.pallas_call(
        functools.partial(
            first_kernel, (fn_count, edge, classes, shares, width, band_reach, sub_count, groups)
        ),
        out_shape=[block(near, EARLY_TILES)] * groups
        + [
            block(devices, early),
            jax.ShapeDtypeStruct((full, 3 * full), jnp.bfloat16),
            jax.ShapeDtypeStruct((full, full), jnp.float32),
            jax.ShapeDtypeStruct((full, full), jnp.float32),
            jax.ShapeDtypeStruct((full, full), jnp.int32),
        ],
        in_specs=[vmem] * (near + 1),
        out_specs=[vmem] * (groups + 5),
        scratch_shapes=[pltpu.VMEM((devices, EARLY_TILES, SUBLANES, LANES), jnp.bfloat16)],
        compiler_params=params,
        cost_estimate=cost(1024 * size, 4 * size),
        name="first",
    )(*gathered, held)
    leaving, tables = results[:groups], results[groups:]
    returned = [leaving[0]] + [None] * (groups - 1)
    for far in (3, 2, 1):
        returned[far] = exchange(leaving[far], far * near)

    back_units = tiles - EARLY_TILES + (tiles + 1) // 2 + 1
    made = pl.pallas_call(
        functools.partial(second_kernel, (fn_count, edge, classes)),
        out_shape=block(devices, back_units),
        in_specs=[vmem] * 6,
        out_specs=vmem,
        compiler_params=params,
        cost_estimate=cost(2048 * size, 4 * size),
        name="second",
    )(tables[0], held, *tables[1:])
    back = lax.all_to_all(made, axes, 0, 0, tiled=True)
    back = back.reshape(classes, shares, back_units, SUBLANES, LANES)
    spread = pl.pallas_call(
        turn_kernel,
        out_shape=[block(groups, EARLY_TILES)] * near,
        in_specs=[vmem] * groups,
        out_specs=[vmem] * near,
        compiler_params=params,
        cost_estimate=cost(0, 4 * size),
        name="spread",
    )(*returned)
    homed = within(spread)
    return pl.pallas_call(
        functools.partial(
            receive_kernel, (fn_count, edge, plane_len, classes, shares, band_reach, sub_count, near)
        ),
        out_shape=(
            jax.ShapeDtypeStruct(psi.shape, jnp.bfloat16),
            jax.ShapeDtypeStruct((fn_count, width), jnp.float32),
            jax.ShapeDtypeStruct((fn_count, width), jnp.float32),
        ),
        in_specs=[vmem] * (2 + near),
        out_specs=(hbm, vmem, vmem),
        scratch_shapes=[
            pltpu.VMEM(psi.shape, jnp.bfloat16),
            pltpu.VMEM((classes, shares, EARLY_TILES, SUBLANES, LANES), jnp.bfloat16),
            pltpu.SemaphoreType.DMA((shares,)),
        ],
        compiler_params=params,
        name="receive",
    )(off_lanes, back, *homed)


def any_shards(psi, potential, offsets, kernel, multipliers, pattern):
    devices = lax.axis_size("brick") * lax.axis_size("sub")
    plan = plan_of(devices, *psi.shape, kernel.shape[1])
    if plan is None:
        return shards(psi, potential, offsets, kernel, multipliers, pattern)
    return transposed_shards(*plan, psi, potential, offsets, kernel, multipliers, pattern)


def solution(mesh):
    in_specs = (
        P(("brick", "sub"), None, None),
        P(("brick", "sub"), None, None),
        P(("brick", "sub")),
        P(("brick", "sub"), None),
        P(("brick", "sub"), None),
        P(("brick", "sub"), None),
    )
    out_specs = (
        P(("brick", "sub"), None, None),
        P(("brick", "sub"), None),
        P(("brick", "sub"), None),
    )
    return jax.shard_map(any_shards, mesh=mesh, in_specs=in_specs, out_specs=out_specs, check_vma=False)
```
